32 devices in a mesh: seq: 8 (over z, x), dp: 4 (over y, core).
Axes of the slice: x: 2, y: 2, z: 4, core: 2. Of those that a mesh axis runs over, the one named last changes fastest.
Arguments:
- tokens: bfloat16 [32, 512, 768], P('seq', 'dp')
- cotangent: bfloat16 [32, 512, 768], P('seq', 'dp'), may hold values from -6 to 6
- read_lengths: int32 [32], replicated, may hold values from 64 to 512, as said below
- row_reads: int32 [32], replicated, may hold values from 0 to 31, as said below
- qkv_master: float32 [768, 2304], P(('seq', 'dp')), may hold values from -0.25 to 0.25
- out_master: float32 [768, 768], P(('seq', 'dp')), may hold values from -1.25 to 1.25
- up_master: float32 [768, 3072], P(('seq', 'dp')), may hold values from -0.21875 to 0.21875
- down_master: float32 [3072, 768], P(None, ('seq', 'dp')), may hold values from -0.109375 to 0.109375
- vec_master: float32 [12, 768], P(None, ('seq', 'dp'))
- qkv_first: float32 [768, 2304], P(('seq', 'dp')), may hold values from -448 to 448
- out_first: float32 [768, 768], P(('seq', 'dp')), may hold values from -64 to 64
- up_first: float32 [768, 3072], P(('seq', 'dp')), may hold values from -256 to 256
- down_first: float32 [3072, 768], P(None, ('seq', 'dp')), may hold values from -256 to 256
- vec_first: float32 [12, 768], P(None, ('seq', 'dp')), may hold values from -448 to 448
- qkv_second: float32 [768, 2304], P(('seq', 'dp')), may hold values from 5242.88 to 20971.52
- out_second: float32 [768, 768], P(('seq', 'dp')), may hold values from 139.264 to 557.056
- up_second: float32 [768, 3072], P(('seq', 'dp')), may hold values from 2048 to 8192
- down_second: float32 [3072, 768], P(None, ('seq', 'dp')), may hold values from 2048 to 8192
- vec_second: float32 [12, 768], P(None, ('seq', 'dp')), may hold values from 5242.88 to 20971.52
Outputs:
- output: bfloat16 [32, 512, 768], P('seq', 'dp')
- input_grad: bfloat16 [32, 512, 768], P('seq', 'dp')
- qkv_updated: float32 [768, 2304], P(('seq', 'dp'))
- out_updated: float32 [768, 768], P(('seq', 'dp'))
- up_updated: float32 [768, 3072], P(('seq', 'dp'))
- down_updated: float32 [3072, 768], P(None, ('seq', 'dp'))
- vec_updated: float32 [12, 768], P(None, ('seq', 'dp'))
- qkv_first_new: float32 [768, 2304], P(('seq', 'dp'))
- out_first_new: float32 [768, 768], P(('seq', 'dp'))
- up_first_new: float32 [768, 3072], P(('seq', 'dp'))
- down_first_new: float32 [3072, 768], P(None, ('seq', 'dp'))
- vec_first_new: float32 [12, 768], P(None, ('seq', 'dp'))
- qkv_second_new: float32 [768, 2304], P(('seq', 'dp'))
- out_second_new: float32 [768, 768], P(('seq', 'dp'))
- up_second_new: float32 [768, 3072], P(('seq', 'dp'))
- down_second_new: float32 [3072, 768], P(None, ('seq', 'dp'))
- vec_second_new: float32 [12, 768], P(None, ('seq', 'dp'))
The draws below stay inside these ranges and needn't reach their ends.
Inputs may be any that keep to these rules, and one draw needn't show every extreme that they name: `read_lengths`: real slots of each read; the 4 rows of each index of seq include one read longer than 384 slots, and some read has 512 slots. Row r holds read row_reads[r]; every read is held by exactly one row.
All inputs are finite; a program needn't handle non-finite values.
Results may differ from the reference program's by a relative error of at most 0.014.
Values may be sent and summed in bfloat16 or wider, within the bound.
No kernel may reach another device: no remote copies, remote signals or barrier semaphores. Data moves between devices by JAX's collectives and lax.ppermute only.
A program may use at most 192 MiB of HBM per device.

```python
import math
import jax
import jax.numpy as jnp
from jax import lax

D = 768
HEADS = 12
HDIM = 64
FF = 3072
SLOTS = 512
ROWS_DEV = 4
STEP = 10
ROWS = 32
NVEC = 12
N_SEQ = 8


def row_plan(key):
    base = jax.random.fold_in(key, 11)
    key_len = jax.random.fold_in(base, 1)
    key_pick = jax.random.fold_in(base, 2)
    key_perm = jax.random.fold_in(base, 3)
    key_long = jax.random.fold_in(base, 4)
    key_top = jax.random.fold_in(base, 5)
    minimum = SLOTS // 8
    row_index = jnp.arange(ROWS, dtype=jnp.int32)
    seq_of_row = row_index // ROWS_DEV
    upper = SLOTS // 2 + SLOTS // 2 * (seq_of_row + 1) // N_SEQ
    row_len = jax.random.randint(key_len, (ROWS,), minimum, upper + 1, dtype=jnp.int32)
    long_len = jax.random.randint(key_long, (ROWS,), 3 * SLOTS // 4 + 1, SLOTS + 1, dtype=jnp.int32)
    full_pick = jax.random.randint(key_pick, (N_SEQ,), 0, ROWS_DEV, dtype=jnp.int32)
    is_long = row_index % ROWS_DEV == full_pick[seq_of_row]
    row_len = jnp.where(is_long, long_len, row_len).astype(jnp.int32)
    top_row = jax.random.randint(key_top, (), 0, N_SEQ, dtype=jnp.int32) * ROWS_DEV + full_pick[0]
    top_row = jnp.minimum(top_row, ROWS - 1)
    top_seq = top_row // ROWS_DEV
    top_row = top_seq * ROWS_DEV + full_pick[top_seq]
    row_len = jnp.where(row_index == top_row, SLOTS, row_len).astype(jnp.int32)
    row_order = jax.random.permutation(key_perm, ROWS).astype(jnp.int32)
    read_len = jnp.zeros((ROWS,), jnp.int32).at[row_order].set(row_len)
    return (read_len, row_order, row_len)


def draw_read_lengths(key, part):
    read_len, row_order, row_len = row_plan(key)
    return read_len


def draw_row_reads(key, part):
    read_len, row_order, row_len = row_plan(key)
    return row_order


def draw_tokens(key, part):
    read_len, row_order, row_len = row_plan(key)
    values = jax.random.normal(jax.random.fold_in(key, 5), (ROWS, SLOTS, D), jnp.float32)
    values = jnp.clip(values, -6.0, 6.0)
    live_slots = jnp.arange(SLOTS, dtype=jnp.int32)[None, :] < row_len[:, None]
    return jnp.where(live_slots[:, :, None], values, 0.0).astype(jnp.bfloat16)


def draw_vec_master(key, part):
    bias_noise = jax.random.normal(jax.random.fold_in(key, 3), (NVEC, D), jnp.float32) * 0.2
    spread = jax.random.uniform(jax.random.fold_in(key, 4), (NVEC, D), jnp.float32, 0.7, 1.3)
    row_index = jnp.arange(NVEC, dtype=jnp.int32)
    gain_rows = (row_index == 3) | (row_index == 6)
    return jnp.where(gain_rows[:, None], spread, bias_noise)


def with_spikes(array, key, source, target, blocks, factor):
    owner, partner = [(jnp.arange(array.shape[dim]) // (array.shape[dim] // blocks)).reshape([-1 if axis == dim else 1 for axis in range(array.ndim)]) for dim in (source, target)]
    chosen = jax.random.permutation(key, blocks)[partner]
    strong = (owner == chosen) | (owner == (partner + blocks // 2) % blocks)
    return jnp.where(strong, factor * array, array)


def steps_of(own_key, extent, shards, least, top_value):
    loudness, own = 1.0, jax.random.fold_in(own_key, 6)
    for axis_at, parts in shards:
        steps = jnp.exp(jax.random.uniform(jax.random.fold_in(own, axis_at), (parts,), jnp.float32, least / len(shards), top_value / len(shards)))
        loudness = loudness * jnp.repeat(steps, extent[axis_at] // parts).reshape([-1 if axis == axis_at else 1 for axis in range(len(extent))])
    return loudness


def gaussian(stream_key, dims, scale, most, cuts=(), held_as=jnp.bfloat16):
    values = jax.random.normal(stream_key, dims, jnp.float32) * scale
    if len(cuts) > 0:
        values = steps_of(stream_key, dims, cuts, -0.22, 0.18) * values
    return jnp.clip(values, min=-most, max=most).astype(held_as)


def bell_draw_with(key, dims, scale, reach, cuts, heavy, kind=jnp.bfloat16):
    entries = scale * jax.random.normal(key, dims, jnp.float32)
    if cuts:
        entries = entries * steps_of(key, dims, cuts, -0.22, 0.18)
    return jnp.clip(with_spikes(entries, jax.random.fold_in(key, 3), *heavy), -reach, reach).astype(kind)


def setup_inputs(seed: int = 0) -> dict:
    streams_of = jax.random.split(jax.random.key(seed), 20)
    tokens = draw_tokens(jax.random.fold_in(streams_of[19], 71), 0)
    cotangent = bell_draw_with(streams_of[1], (ROWS, SLOTS, D), 1.0, 6.0, ((0, 8), (1, 4)), (0, 2, 8, 2.0))
    read_lengths = draw_read_lengths(jax.random.fold_in(streams_of[19], 71), 0)
    row_reads = draw_row_reads(jax.random.fold_in(streams_of[19], 71), 0)
    qkv_master = gaussian(streams_of[4], (D, 3 * D), (D * 3 // 4) ** -0.5, 0.25, ((0, 32),), jnp.float32)
    out_master = gaussian(streams_of[5], (D, D), (D // 32) ** -0.5, 1.25, ((0, 32),), jnp.float32)
    up_master = gaussian(streams_of[6], (D, FF), D ** -0.5, 0.21875, ((0, 32),), jnp.float32)
    down_master = gaussian(streams_of[7], (FF, D), FF ** -0.5, 0.109375, ((1, 32),), jnp.float32)
    vec_master = draw_vec_master(jax.random.fold_in(streams_of[19], 71), 0)
    qkv_first = gaussian(streams_of[9], (D, 3 * D), (0.8 * (ROWS * SLOTS * 0.5) ** 0.5), 448.0, ((0, 32),), jnp.float32)
    out_first = gaussian(streams_of[10], (D, D), (0.13 * (ROWS * SLOTS * 0.5) ** 0.5), 64.0, ((0, 32),), jnp.float32)
    up_first = gaussian(streams_of[11], (D, FF), (0.5 * (ROWS * SLOTS * 0.5) ** 0.5), 256.0, ((0, 32),), jnp.float32)
    down_first = gaussian(streams_of[12], (FF, D), (0.5 * (ROWS * SLOTS * 0.5) ** 0.5), 256.0, ((1, 32),), jnp.float32)
    vec_first = gaussian(streams_of[13], (NVEC, D), (0.8 * (ROWS * SLOTS * 0.5) ** 0.5), 448.0, ((1, 32),), jnp.float32)
    qkv_second = jnp.clip(jnp.exp(math.log(20971.52) - 1.3862944 * jax.random.uniform(streams_of[14], (D, 3 * D), jnp.float32) ** steps_of(streams_of[14], (D, 3 * D), ((0, 32),), -0.2, 0.2)), 5242.88, 20971.52)
    out_second = jnp.clip(jnp.exp(math.log(557.056) - 1.3862944 * jax.random.uniform(streams_of[15], (D, D), jnp.float32) ** steps_of(streams_of[15], (D, D), ((0, 32),), -0.2, 0.2)), 139.264, 557.056)
    up_second = jnp.clip(jnp.exp(math.log(8192.0) - 1.3862944 * jax.random.uniform(streams_of[16], (D, FF), jnp.float32) ** steps_of(streams_of[16], (D, FF), ((0, 32),), -0.2, 0.2)), 2048.0, 8192.0)
    down_second = jnp.clip(jnp.exp(math.log(8192.0) - 1.3862944 * jax.random.uniform(streams_of[17], (FF, D), jnp.float32) ** steps_of(streams_of[17], (FF, D), ((1, 32),), -0.2, 0.2)), 2048.0, 8192.0)
    vec_second = jnp.clip(jnp.exp(math.log(20971.52) - 1.3862944 * jax.random.uniform(streams_of[18], (NVEC, D), jnp.float32) ** steps_of(streams_of[18], (NVEC, D), ((1, 32),), -0.2, 0.2)), 5242.88, 20971.52)
    return dict(tokens=tokens, cotangent=cotangent, read_lengths=read_lengths, row_reads=row_reads, qkv_master=qkv_master, out_master=out_master, up_master=up_master, down_master=down_master, vec_master=vec_master, qkv_first=qkv_first, out_first=out_first, up_first=up_first, down_first=down_first, vec_first=vec_first, qkv_second=qkv_second, out_second=out_second, up_second=up_second, down_second=down_second, vec_second=vec_second)


@jax.custom_vjp
def low(v):
    return lax.optimization_barrier(v.astype(jnp.bfloat16)).astype(jnp.float32)

@jax.custom_vjp
def low_back(v):
    return v

def low_keep(v):
    return (low(v), None)

def low_pass(kept, grad):
    return (grad,)

def back_keep(v):
    return (v, None)

def back_low(kept, grad):
    return (low(grad),)
low.defvjp(low_keep, low_pass)
low_back.defvjp(back_keep, back_low)
highest = lax.Precision.HIGHEST
norm_eps = 1e-12
beta_one = 0.5
beta_two = 0.5
adam_eps = 1e-08
masked_score = -1e+30
step_rates = (0.06, 0.3, 0.05, 0.025, 0.5)
step_decays = (0.01, 0.01, 0.01, 0.01, 0.0)

def layer_norm(values, scale_gain, norm_shift):
    centered = values - lax.optimization_barrier(jnp.mean(values, axis=-1, keepdims=True))
    variance = lax.optimization_barrier(jnp.mean(centered * centered, axis=-1, keepdims=True))
    return centered * lax.rsqrt(variance + norm_eps) * scale_gain + norm_shift

def attend_row(packed):
    qkv_row, live_row = packed
    head_parts = qkv_row.reshape(SLOTS, 3, HEADS, HDIM)
    scores = jnp.einsum('ihd,jhd->hij', head_parts[:, 0], head_parts[:, 1], precision=highest) * HDIM ** (-0.5)
    scores = low_back(scores)
    scores = jnp.where(live_row[None, None, :], scores, masked_score)
    probabilities = low(jax.nn.softmax(scores, axis=-1))
    mixed_heads = jnp.einsum('hij,jhd->ihd', probabilities, head_parts[:, 2], precision=highest)
    return low_back(low(mixed_heads)).reshape(SLOTS, HEADS * HDIM)

def forward(live_slots, inputs, qkv_master, out_master, up_master, down_master, vec_master):
    qkv_weight = low(qkv_master)
    out_weight = low(out_master)
    up_weight = low(up_master)
    down_weight = low(down_master)
    vectors = low(vec_master)
    zero_bias = jnp.zeros((D,), vectors.dtype)
    proj_bias = jnp.concatenate([vectors[0], zero_bias, vectors[1]])
    projected = jnp.einsum('rsd,de->rse', inputs, qkv_weight, precision=highest) + proj_bias
    projected = low_back(low(projected))
    attended = lax.map(jax.checkpoint(attend_row), (projected, live_slots))
    attn_proj = low_back(jnp.einsum('rsf,fo->rso', attended, out_weight, precision=highest)) + vectors[2]
    first_norm = layer_norm(inputs + attn_proj, vectors[3], vectors[4])
    hidden = low_back(jnp.einsum('rsd,df->rsf', low(first_norm), up_weight, precision=highest)) + vectors[8:].reshape(FF)
    active = low(jax.nn.gelu(hidden, approximate=False))
    branch = low_back(jnp.einsum('rsf,fo->rso', active, down_weight, precision=highest)) + vectors[5]
    result = layer_norm(first_norm + branch, vectors[6], vectors[7])
    return result * live_slots[:, :, None].astype(result.dtype)

def adam_step(master, first_moment, second_moment, gradient, step_rate, decay_rate):
    first_new = beta_one * first_moment + (1.0 - beta_one) * gradient
    second_new = beta_two * second_moment + (1.0 - beta_two) * gradient * gradient
    ratio = first_new / (1.0 - beta_one ** STEP) / (jnp.sqrt(second_new / (1.0 - beta_two ** STEP)) + adam_eps)
    return (master - step_rate * (ratio + decay_rate * master), first_new, second_new)

def reference(tokens, cotangent, read_lengths, row_reads, qkv_master, out_master, up_master, down_master, vec_master, qkv_first, out_first, up_first, down_first, vec_first, qkv_second, out_second, up_second, down_second, vec_second):
    lengths = read_lengths[row_reads]
    live_slots = jnp.arange(SLOTS, dtype=jnp.int32)[None, :] < lengths[:, None]
    group_rows = math.gcd(ROWS, 8)
    block_count = ROWS // group_rows
    masters = (qkv_master, out_master, up_master, down_master, vec_master)
    blocks = (tokens.astype(jnp.float32).reshape(block_count, group_rows, SLOTS, D), cotangent.astype(jnp.float32).reshape(block_count, group_rows, SLOTS, D), live_slots.reshape(block_count, group_rows, SLOTS))

    def run_block(totals, pieces):
        inputs, grad_result, live_block = pieces

        def layer_apply(values, qkv_weight, out_weight, up_weight, down_weight, vec_weight):
            return forward(live_block, values, qkv_weight, out_weight, up_weight, down_weight, vec_weight)
        result, backward_fn = jax.vjp(layer_apply, inputs, qkv_master, out_master, up_master, down_master, vec_master)
        gradients = backward_fn(grad_result)
        new_totals = tuple((old + new for old, new in zip(totals, gradients[1:])))
        return (new_totals, (result.astype(jnp.bfloat16), gradients[0].astype(jnp.bfloat16)))
    start_totals = tuple((jnp.zeros_like(item) for item in masters))
    totals, outputs = lax.scan(run_block, start_totals, blocks)
    output = outputs[0].reshape(ROWS, SLOTS, D)
    input_grad = outputs[1].reshape(ROWS, SLOTS, D)
    firsts = (qkv_first, out_first, up_first, down_first, vec_first)
    seconds = (qkv_second, out_second, up_second, down_second, vec_second)
    updates = [adam_step(masters[index], firsts[index], seconds[index], totals[index], step_rates[index], step_decays[index]) for index in range(5)]
    return (output, input_grad, updates[0][0], updates[1][0], updates[2][0], updates[3][0], updates[4][0], updates[0][1], updates[1][1], updates[2][1], updates[3][1], updates[4][1], updates[0][2], updates[1][2], updates[2][2], updates[3][2], updates[4][2])
```

```python
import functools

import jax
import jax.numpy as jnp
from jax import lax
from jax.experimental import pallas as pl
from jax.experimental.pallas import tpu as pltpu
from jax.sharding import PartitionSpec as P

HEADS = 12
STEP = 10
AXES = ("seq", "dp")

norm_eps = 1e-12
beta_one = 0.5
beta_two = 0.5
adam_eps = 1e-08
masked_score = -1e30
step_rates = (0.06, 0.3, 0.05, 0.025, 0.5)
step_decays = (0.01, 0.01, 0.01, 0.01, 0.0)

f32 = jnp.float32
bf16 = jnp.bfloat16
VEC_PAD = 128

ERF_T = 0.3275911
ERF_C = (0.254829592, -0.284496736, 1.421413741, -1.453152027, 1.061405429)

NT = (((1,), (1,)), ((), ()))
TN = (((0,), (0,)), ((), ()))


def dot(a, b, dims=(((1,), (0,)), ((), ()))):
    return lax.dot_general(a, b, dims, preferred_element_type=f32)


def params(mib=48):
    return pltpu.CompilerParams(vmem_limit_bytes=mib << 20)


def cost(flops, nbytes, trans=0):
    return pl.CostEstimate(
        flops=int(flops), bytes_accessed=int(nbytes), transcendentals=int(trans)
    )


def full(shape):
    return pl.BlockSpec(shape, lambda *_: (0,) * len(shape))


def swap(value, mask, count):
    return lax.ppermute(value, AXES, [(i, i ^ mask) for i in range(count)])


def line_digits(count):
    digits, base, rest = [], 8, count // 8
    while rest > 1:
        radix = 4 if rest % 4 == 0 else 2
        digits.append((radix, base))
        base *= radix
        rest //= radix
    return digits


def gather_pieces(own, count):
    line = own[None]
    for radix, base in line_digits(count):
        line = jnp.concatenate(
            [line] + [swap(line, base * m, count) for m in range(1, radix)], axis=0
        )
    piece_x = swap(line, 4, count)
    piece_y = swap(line, 2, count)
    half = own.shape[1] // 256 * 128
    cross = jnp.concatenate(
        [swap(piece_y[:, :, :half], 4, count), swap(piece_x[:, :, half:], 2, count)], axis=2
    )
    pieces = [line, piece_y, piece_x, cross]
    return pieces + [swap(piece, 1, count) for piece in pieces]


def assemble_kernel(index_ref, *refs):
    pieces, out_ref, sem = refs[:8], refs[8], refs[9]
    index = index_ref[0]
    for which, piece in enumerate(pieces):
        for z in range(piece.shape[0]):
            offset = 8 * z + 2 * (which % 4) + which // 4
            pltpu.make_async_copy(piece.at[z], out_ref.at[index ^ offset], sem).start()
    pltpu.make_async_copy(out_ref, out_ref, sem).wait()


def assemble(index, pieces):
    lines, rows, cols = pieces[0].shape
    out = pl.pallas_call(
        assemble_kernel,
        out_shape=jax.ShapeDtypeStruct((8 * lines, rows, cols), bf16),
        grid_spec=pltpu.PrefetchScalarGridSpec(
            num_scalar_prefetch=1,
            grid=(1,),
            in_specs=[pl.BlockSpec(memory_space=pl.ANY)] * 8,
            out_specs=pl.BlockSpec(memory_space=pl.ANY),
            scratch_shapes=[pltpu.SemaphoreType.DMA],
        ),
        compiler_params=params(8),
        cost_estimate=cost(0, 4 * 8 * lines * rows * cols),
        name="assemble",
    )(index, *pieces)
    return out.reshape(8 * lines * rows, cols)


def scatter_sum(own, other, count):
    def add(*terms):
        total = terms[0].astype(f32)
        for term in terms[1:]:
            total = total + term.astype(f32)
        return total.astype(bf16)

    received = swap(other, 1, count)
    half = own.shape[3] // 256 * 128
    cross = [add(own[3, :, :, :half], received[3, :, :, :half]), add(own[3, :, :, half:], received[3, :, :, half:])]
    via_x = swap(cross[0], 4, count)
    via_y = swap(cross[1], 2, count)
    piece_y = jnp.concatenate(
        [
            add(own[1, :, :, :half], received[1, :, :, :half], via_x),
            add(own[1, :, :, half:], received[1, :, :, half:]),
        ],
        axis=2,
    )
    piece_x = jnp.concatenate(
        [
            add(own[2, :, :, :half], received[2, :, :, :half]),
            add(own[2, :, :, half:], received[2, :, :, half:], via_y),
        ],
        axis=2,
    )
    from_y = swap(piece_y, 2, count)
    from_x = swap(piece_x, 4, count)
    line = add(own[0], received[0], from_x, from_y)
    terms = [line]
    for radix, base in reversed(line_digits(count)):
        if len(terms) > 1:
            line = add(*terms)
        span = line.shape[0] // radix
        parts = [line[m * span : (m + 1) * span] for m in range(radix)]
        terms = [parts[0]] + [swap(parts[m], base * m, count) for m in range(1, radix)]
    return terms


def project_kernel(x_ref, w_ref, b_ref, o_ref):
    o_ref[...] = (dot(x_ref[...], w_ref[...]) + b_ref[...]).astype(bf16)


def project(x, weight, bias):
    slots, feat = x.shape
    cols = bias.shape[1]
    tile = feat
    return pl.pallas_call(
        project_kernel,
        out_shape=jax.ShapeDtypeStruct((slots, cols), bf16),
        grid=(cols // tile,),
        in_specs=[
            full((slots, feat)),
            pl.BlockSpec((feat, tile), lambda i: (0, i)),
            pl.BlockSpec((1, tile), lambda i: (0, i)),
        ],
        out_specs=pl.BlockSpec((slots, tile), lambda i: (0, i)),
        compiler_params=params(),
        cost_estimate=cost(2 * slots * feat * cols, 2 * (slots * cols + feat * cols)),
        name="project",
    )(x, weight, bias)


def slot_live(scalar_ref, shape, axis):
    at = lax.broadcasted_iota(jnp.int32, shape, axis)
    quarter = scalar_ref[2]
    part = at // quarter
    position = (part ^ scalar_ref[1]) * quarter + (at - part * quarter)
    return position < scalar_ref[0]


def lane_parts(value):
    high = value.astype(bf16).astype(f32)
    middle = (value - high).astype(bf16).astype(f32)
    return high, middle, value - high - middle


def attend_forward_kernel(scalar_ref, q_ref, k_ref, v_ref, o_ref, log_ref):
    slots, width = q_ref.shape
    half = width // 2
    scale = half ** (-0.5)
    lane = lax.broadcasted_iota(jnp.int32, (slots, width), 1)
    bias = jnp.where(slot_live(scalar_ref, (slots, width), 0), 0.0, masked_score)
    query = q_ref[...].astype(f32) * scale
    key = k_ref[...].astype(f32)
    value = v_ref[...].astype(f32)
    mixed, logs = [], []
    for head in range(2):
        mine = (lane >= half) if head else (lane < half)
        base = 0 if head else half
        query_ext = jnp.where(mine, query, jnp.where(lane == base, 1.0, 0.0)).astype(bf16)
        key_ext = jnp.where(mine, key, jnp.where(lane == base, bias, 0.0)).astype(bf16)
        value_ext = jnp.where(mine, value, 1.0).astype(bf16)
        scores = dot(query_ext, key_ext, NT)
        top = jnp.max(scores, axis=1, keepdims=True)
        weights = jnp.exp(scores - top).astype(bf16)
        total = dot(weights, value_ext)
        sums = pltpu.roll(total, half, 1)
        mixed.append(total / sums)
        logs.append(top + jnp.log(jnp.where(mine, sums, 1.0)))
    first = lane < half
    o_ref[...] = jnp.where(first, mixed[0], mixed[1]).astype(bf16)
    log_ref[...] = jnp.where(first, logs[0], logs[1])


def attend_forward(scalars, projected, feat):
    slots = projected.shape[0]
    width = 2 * feat // HEADS
    pairs = feat // width
    block = lambda offset: pl.BlockSpec((slots, width), lambda i, *_: (0, i + offset))
    return pl.pallas_call(
        attend_forward_kernel,
        out_shape=(
            jax.ShapeDtypeStruct((slots, feat), bf16),
            jax.ShapeDtypeStruct((slots, feat), f32),
        ),
        grid_spec=pltpu.PrefetchScalarGridSpec(
            num_scalar_prefetch=1,
            grid=(pairs,),
            in_specs=[block(0), block(pairs), block(2 * pairs)],
            out_specs=(block(0), block(0)),
        ),
        compiler_params=params(),
        cost_estimate=cost(
            4 * slots * slots * width * 2 * pairs, 12 * slots * feat, HEADS * slots * slots
        ),
        name="attend_forward",
    )(scalars, projected, projected, projected)


def attend_backward_kernel(scalar_ref, q_ref, k_ref, v_ref, o_ref, log_ref, g_ref, dq_ref, dk_ref, dv_ref):
    slots, width = q_ref.shape
    half = width // 2
    scale = half ** (-0.5)
    lane = lax.broadcasted_iota(jnp.int32, (slots, width), 1)
    bias = jnp.where(slot_live(scalar_ref, (slots, width), 0), 0.0, masked_score)
    query = q_ref[...].astype(f32) * scale
    key = k_ref[...].astype(f32)
    value = v_ref[...].astype(f32)
    grad_low = g_ref[...]
    grad = grad_low.astype(f32)
    product = grad * o_ref[...].astype(f32)
    log_all = pltpu.roll(log_ref[...], half, 1)
    query_low = query.astype(bf16)
    key_turned = jnp.transpose(key).astype(bf16)
    parts = []
    for head in range(2):
        mine = (lane >= half) if head else (lane < half)
        base = 0 if head else half
        delta = jnp.sum(jnp.where(mine, product, 0.0), axis=1, keepdims=True)
        logs = lane_parts(log_all)
        deltas = lane_parts(delta)
        spot = [lane == base + k for k in range(4)]
        ones = (lane >= base) & (lane < base + 3)
        query_ext = jnp.where(mine, query, jnp.where(spot[3], 1.0, 0.0))
        grad_ext = jnp.where(mine, grad, 0.0)
        for k in range(3):
            query_ext = jnp.where(spot[k], -logs[k], query_ext)
            grad_ext = jnp.where(spot[k], -deltas[k], grad_ext)
        key_ext = jnp.where(mine, key, jnp.where(ones, 1.0, jnp.where(spot[3], bias, 0.0)))
        value_ext = jnp.where(mine, value, jnp.where(ones, 1.0, 0.0))
        probs = jnp.exp(dot(key_ext.astype(bf16), query_ext.astype(bf16), NT))
        grad_scores = (probs * dot(value_ext.astype(bf16), grad_ext.astype(bf16), NT)).astype(bf16)
        parts.append(
            (
                dot(key_turned, grad_scores),
                dot(grad_scores, query_low),
                dot(probs.astype(bf16), grad_low),
            )
        )
    first = lane < half
    turned = lax.broadcasted_iota(jnp.int32, (width, slots), 0) < half
    dq_ref[...] = (jnp.transpose(jnp.where(turned, parts[0][0], parts[1][0])) * scale).astype(bf16)
    dk_ref[...] = jnp.where(first, parts[0][1], parts[1][1]).astype(bf16)
    dv_ref[...] = jnp.where(first, parts[0][2], parts[1][2]).astype(bf16)


def attend_backward(scalars, projected, attended, logs, grad_attended):
    slots, feat = attended.shape
    width = 2 * feat // HEADS
    pairs = feat // width
    block = lambda offset: pl.BlockSpec((slots, width), lambda i, *_: (0, i + offset))
    part = jax.ShapeDtypeStruct((slots, feat), bf16)
    return pl.pallas_call(
        attend_backward_kernel,
        out_shape=(part, part, part),
        grid_spec=pltpu.PrefetchScalarGridSpec(
            num_scalar_prefetch=1,
            grid=(pairs,),
            in_specs=[block(0), block(pairs), block(2 * pairs), block(0), block(0), block(0)],
            out_specs=(block(0),) * 3,
        ),
        compiler_params=params(),
        cost_estimate=cost(
            10 * slots * slots * width * 2 * pairs, 20 * slots * feat, HEADS * slots * slots
        ),
        name="attend_backward",
    )(scalars, projected, projected, projected, attended, logs, grad_attended)


def normalize(total):
    centered = total - jnp.mean(total, axis=1, keepdims=True)
    scale = lax.rsqrt(jnp.mean(centered * centered, axis=1, keepdims=True) + norm_eps)
    return centered * scale, scale


def normalize_back(grad, normed, scale):
    return (
        grad
        - jnp.mean(grad, axis=1, keepdims=True)
        - normed * jnp.mean(grad * normed, axis=1, keepdims=True)
    ) * scale


def column_sum(value):
    return jnp.sum(value, axis=0, keepdims=True)


def attn_out_kernel(a_ref, w_ref, x_ref, vec_ref, n_ref, s_ref, low_ref):
    total = x_ref[...].astype(f32) + dot(a_ref[...], w_ref[...]) + vec_ref[2:3, :]
    normed, scale = normalize(total)
    n_ref[...] = normed
    s_ref[...] = scale
    low_ref[...] = (normed * vec_ref[3:4, :] + vec_ref[4:5, :]).astype(bf16)


def attn_out(attended, weight, x, vectors):
    slots, feat = x.shape
    return pl.pallas_call(
        attn_out_kernel,
        out_shape=(
            jax.ShapeDtypeStruct((slots, feat), f32),
            jax.ShapeDtypeStruct((slots, 1), f32),
            jax.ShapeDtypeStruct((slots, feat), bf16),
        ),
        compiler_params=params(),
        cost_estimate=cost(2 * slots * feat * feat, 10 * slots * feat + 2 * feat * feat),
        name="attn_out",
    )(attended, weight, x, vectors)


def gelu_parts(hidden):
    size = jnp.abs(hidden) * (0.5**0.5)
    inverse = 1.0 / (1.0 + ERF_T * size)
    poly = ERF_C[4]
    for coefficient in (ERF_C[3], ERF_C[2], ERF_C[1], ERF_C[0]):
        poly = poly * inverse + coefficient
    bell = jnp.exp(-size * size)
    tail = 0.5 * poly * inverse * bell
    return jnp.where(hidden >= 0, 1.0 - tail, tail), bell * 0.3989422804014327


def feed_forward_kernel(
    scalar_ref, n_ref, low_ref, cot_ref, up_ref, down_ref, bias_ref, vec_ref,
    active_ref, slope_ref, out_ref, grad_ref, grad_low_ref, sums_ref, acc_ref,
):
    step = pl.program_id(0)
    hidden = dot(low_ref[...], up_ref[...]) + bias_ref[...]
    phi, density = gelu_parts(hidden)
    active = (hidden * phi).astype(bf16)
    active_ref[...] = active
    slope_ref[...] = phi + hidden * density
    branch = dot(active, down_ref[...], NT)

    @pl.when(step == 0)
    def _():
        acc_ref[...] = branch

    @pl.when(step > 0)
    def _():
        acc_ref[...] += branch

    @pl.when(step == pl.num_programs(0) - 1)
    def _():
        slots, feat = n_ref.shape
        first = n_ref[...] * vec_ref[3:4, :] + vec_ref[4:5, :]
        normed, scale = normalize(first + (acc_ref[...] + vec_ref[5:6, :]))
        live = slot_live(scalar_ref, (slots, feat), 0)
        result = normed * vec_ref[6:7, :] + vec_ref[7:8, :]
        out_ref[...] = jnp.where(live, result, 0.0).astype(bf16)
        grad_result = jnp.where(live, cot_ref[...].astype(f32), 0.0)
        grad = normalize_back(grad_result * vec_ref[6:7, :], normed, scale)
        grad_ref[...] = grad
        grad_low_ref[...] = grad.astype(bf16)
        sums_ref[0:1, :] = column_sum(grad)
        sums_ref[1:2, :] = column_sum(grad_result * normed)
        sums_ref[2:3, :] = column_sum(grad_result)
        sums_ref[3:8, :] = jnp.zeros((5, feat), f32)


def feed_forward(scalars, normed, low, cotangent, up, down, bias, vectors, tile=512):
    slots, feat = normed.shape
    wide = up.shape[1]
    whole = full((slots, feat))
    return pl.pallas_call(
        feed_forward_kernel,
        out_shape=(
            jax.ShapeDtypeStruct((slots, wide), bf16),
            jax.ShapeDtypeStruct((slots, wide), f32),
            jax.ShapeDtypeStruct((slots, feat), bf16),
            jax.ShapeDtypeStruct((slots, feat), f32),
            jax.ShapeDtypeStruct((slots, feat), bf16),
            jax.ShapeDtypeStruct((8, feat), f32),
        ),
        grid_spec=pltpu.PrefetchScalarGridSpec(
            num_scalar_prefetch=1,
            grid=(wide // tile,),
            in_specs=[
                whole, whole, whole,
                pl.BlockSpec((feat, tile), lambda i, *_: (0, i)),
                pl.BlockSpec((feat, tile), lambda i, *_: (0, i)),
                pl.BlockSpec((1, tile), lambda i, *_: (0, i)),
                full(vectors.shape),
            ],
            out_specs=(
                pl.BlockSpec((slots, tile), lambda i, *_: (0, i)),
                pl.BlockSpec((slots, tile), lambda i, *_: (0, i)),
                whole, whole, whole, full((8, feat)),
            ),
            scratch_shapes=[pltpu.VMEM((slots, feat), f32)],
        ),
        compiler_params=params(),
        cost_estimate=cost(
            4 * slots * feat * wide, 6 * slots * wide + 4 * feat * wide, 2 * slots * wide
        ),
        name="feed_forward",
    )(scalars, normed, low, cotangent, up, down, bias, vectors)


def feed_back_kernel(
    low_ref, grad_ref, n_ref, s_ref, slope_ref, up_ref, down_ref, vec_ref,
    hidden_ref, bias_ref, out_ref, out_low_ref, sums_ref, acc_ref,
):
    step = pl.program_id(0)
    grad_hidden = dot(low_ref[...], down_ref[...]) * slope_ref[...]
    bias_ref[...] = column_sum(grad_hidden)
    grad_hidden = grad_hidden.astype(bf16)
    hidden_ref[...] = grad_hidden
    back = dot(grad_hidden, up_ref[...], NT)

    @pl.when(step == 0)
    def _():
        acc_ref[...] = grad_ref[...] + back

    @pl.when(step > 0)
    def _():
        acc_ref[...] += back

    @pl.when(step == pl.num_programs(0) - 1)
    def _():
        grad_first = acc_ref[...]
        normed = n_ref[...]
        grad = normalize_back(grad_first * vec_ref[3:4, :], normed, s_ref[...])
        out_ref[...] = grad
        out_low_ref[...] = grad.astype(bf16)
        sums_ref[0:1, :] = column_sum(grad)
        sums_ref[1:2, :] = column_sum(grad_first * normed)
        sums_ref[2:3, :] = column_sum(grad_first)
        sums_ref[3:8, :] = jnp.zeros((5, grad.shape[1]), f32)


def feed_back(grad_low, grad, normed, scale, slope, up, down, vectors, tile=512):
    slots, feat = normed.shape
    wide = up.shape[1]
    whole = full((slots, feat))
    column = pl.BlockSpec((slots, tile), lambda i: (0, i))
    return pl.pallas_call(
        feed_back_kernel,
        out_shape=(
            jax.ShapeDtypeStruct((slots, wide), bf16),
            jax.ShapeDtypeStruct((1, wide), f32),
            jax.ShapeDtypeStruct((slots, feat), f32),
            jax.ShapeDtypeStruct((slots, feat), bf16),
            jax.ShapeDtypeStruct((8, feat), f32),
        ),
        grid=(wide // tile,),
        in_specs=[
            whole, whole, whole, full((slots, 1)), column,
            pl.BlockSpec((feat, tile), lambda i: (0, i)),
            pl.BlockSpec((feat, tile), lambda i: (0, i)),
            full(vectors.shape),
        ],
        out_specs=(column, pl.BlockSpec((1, tile), lambda i: (0, i)), whole, whole, full((8, feat))),
        scratch_shapes=[pltpu.VMEM((slots, feat), f32)],
        compiler_params=params(),
        cost_estimate=cost(4 * slots * feat * wide, 6 * slots * wide + 4 * feat * wide),
        name="feed_back",
    )(grad_low, grad, normed, scale, slope, up, down, vectors)


def weight_grad_kernel(count, index_ref, *refs):
    pairs = (len(refs) - 4) // 2
    own_ref, other_ref, hold, sem = refs[2 * pairs :]
    index = index_ref[0]
    rows = own_ref.shape[2]
    width = hold.shape[3]
    jobs = []
    column = 0
    for pair in range(pairs):
        cols = refs[2 * pair + 1].shape[1]
        for start in range(0, cols, width):
            jobs.append((pair, start, min(width, cols - start), column + start))
        column += cols

    def drain(slot, size):
        view = hold.at[slot, :, :, pl.ds(0, size)]
        pltpu.make_async_copy(view, view, sem.at[slot]).wait()

    for at, (pair, start, size, column) in enumerate(jobs):
        slot = at % 2
        if at >= 2:
            drain(slot, jobs[at - 2][2])
        left, right = refs[2 * pair], refs[2 * pair + 1]
        product = dot(left[...], right[:, start : start + size], TN)
        for block in range(count):
            hold[slot, block, :, 0:size] = product[block * rows : (block + 1) * rows, :].astype(bf16)
        for offset in range(count):
            target = other_ref if offset % 2 else own_ref
            pltpu.make_async_copy(
                hold.at[slot, index ^ offset, :, pl.ds(0, size)],
                target.at[offset // 2 % 4, offset // 8, :, pl.ds(column, size)],
                sem.at[slot],
            ).start()
    for at in range(max(0, len(jobs) - 2), len(jobs)):
        drain(at % 2, jobs[at][2])


def weight_grad(index, count, *operands):
    feat = operands[0].shape[1]
    rows = feat // count
    cols = sum(right.shape[1] for right in operands[1::2])
    out = jax.ShapeDtypeStruct((4, count // 8, rows, cols), bf16)
    return pl.pallas_call(
        functools.partial(weight_grad_kernel, count),
        out_shape=(out, out),
        grid_spec=pltpu.PrefetchScalarGridSpec(
            num_scalar_prefetch=1,
            grid=(1,),
            in_specs=[full(operand.shape) for operand in operands],
            out_specs=(pl.BlockSpec(memory_space=pl.ANY),) * 2,
            scratch_shapes=[
                pltpu.VMEM((2, count, rows, feat), bf16),
                pltpu.SemaphoreType.DMA((2,)),
            ],
        ),
        compiler_params=params(),
        cost_estimate=cost(
            2 * operands[0].shape[0] * feat * cols,
            2 * feat * cols + sum(2 * operand.size for operand in operands),
        ),
        name="weight_grad",
    )(index, *operands)


def out_back_kernel(grad_ref, w_ref, o_ref):
    o_ref[...] = dot(grad_ref[...], w_ref[...], NT).astype(bf16)


def out_back(grad_low, weight):
    slots, feat = grad_low.shape
    return pl.pallas_call(
        out_back_kernel,
        out_shape=jax.ShapeDtypeStruct((slots, feat), bf16),
        compiler_params=params(),
        cost_estimate=cost(2 * slots * feat * feat, 4 * slots * feat + 2 * feat * feat),
        name="out_back",
    )(grad_low, weight)


def input_back_kernel(dq_ref, dk_ref, dv_ref, w_ref, grad_ref, o_ref):
    feat = dq_ref.shape[1]
    total = grad_ref[...]
    for at, part in enumerate((dq_ref, dk_ref, dv_ref)):
        total = total + dot(part[...], w_ref[:, at * feat : (at + 1) * feat], NT)
    o_ref[...] = total.astype(bf16)


def input_back(parts, weight, grad):
    slots, feat = grad.shape
    return pl.pallas_call(
        input_back_kernel,
        out_shape=jax.ShapeDtypeStruct((slots, feat), bf16),
        compiler_params=params(),
        cost_estimate=cost(6 * slots * feat * feat, 14 * slots * feat + 6 * feat * feat),
        name="input_back",
    )(*parts, weight, grad)


def adam_step(master, first_moment, second_moment, gradient, step_rate, decay_rate):
    first_new = beta_one * first_moment + (1.0 - beta_one) * gradient
    second_new = beta_two * second_moment + (1.0 - beta_two) * gradient * gradient
    ratio = (
        first_new
        / (1.0 - beta_one**STEP)
        / (jnp.sqrt(second_new / (1.0 - beta_two**STEP)) + adam_eps)
    )
    return (master - step_rate * (ratio + decay_rate * master), first_new, second_new)


def on_device(
    tokens,
    cotangent,
    read_lengths,
    row_reads,
    qkv_master,
    out_master,
    up_master,
    down_master,
    vec_master,
    qkv_first,
    out_first,
    up_first,
    down_first,
    vec_first,
    qkv_second,
    out_second,
    up_second,
    down_second,
    vec_second,
):
    groups = lax.axis_size("dp")
    count = groups * lax.axis_size("seq")
    row_count, quarter, feat = tokens.shape
    slots = quarter * groups
    kinds = vec_master.shape[0]
    rows = feat // count
    seq_index = lax.axis_index("seq")
    dp_index = lax.axis_index("dp")
    index = (seq_index * groups + dp_index).astype(jnp.int32).reshape(1)

    first_block = jnp.concatenate(
        [
            qkv_master.astype(bf16),
            out_master.astype(bf16),
            jnp.pad(vec_master.T, ((0, 0), (0, VEC_PAD - kinds))).astype(bf16),
        ],
        axis=1,
    )
    up_block = up_master.astype(bf16)
    down_block = down_master.T.astype(bf16)
    first_pieces = gather_pieces(first_block, count)
    up_pieces = gather_pieces(up_block, count)
    down_pieces = gather_pieces(down_block, count)

    both = jnp.stack([tokens, cotangent], axis=1)
    turned = [lax.dynamic_index_in_dim(both, dp_index ^ m, 0, keepdims=False) for m in range(4)]
    across = swap(jnp.stack([turned[2], turned[3]]), 2, count)
    beside = swap(jnp.stack([turned[1], across[1]]), 1, count)
    mine = jnp.stack([turned[0], beside[0], across[0], beside[1]], axis=1)
    x = mine[0].reshape(slots, feat)
    grad_output = mine[1].reshape(slots, feat)

    read = lax.dynamic_index_in_dim(
        row_reads, seq_index * row_count + dp_index, keepdims=False
    )
    length = lax.dynamic_index_in_dim(read_lengths, read, keepdims=False)
    scalars = jnp.stack([length, dp_index.astype(jnp.int32), jnp.int32(quarter)])

    first_weight = assemble(index, first_pieces)
    qkv_weight = first_weight[:, : 3 * feat]
    out_weight = first_weight[:, 3 * feat : 4 * feat]
    vectors = first_weight[:, 4 * feat : 4 * feat + 16].T.astype(f32)
    proj_bias = jnp.concatenate([vectors[0], jnp.zeros((feat,), f32), vectors[1]])[None]
    wide_bias = vectors[8:kinds].reshape(1, -1)

    projected = project(x, qkv_weight, proj_bias)
    attended, logs = attend_forward(scalars, projected, feat)
    normed, scale, low = attn_out(attended, out_weight, x, vectors)

    up_weight = assemble(index, up_pieces)
    down_weight = assemble(index, down_pieces)
    active, slope, out_row, grad2, grad2_low, sums2 = feed_forward(
        scalars, normed, low, grad_output, up_weight, down_weight, wide_bias, vectors
    )
    down_terms = scatter_sum(*weight_grad(index, count, grad2_low, active), count)
    grad_hidden, bias1, grad1, grad1_low, sums1 = feed_back(
        grad2_low, grad2, normed, scale, slope, up_weight, down_weight, vectors
    )
    up_terms = scatter_sum(*weight_grad(index, count, low, grad_hidden), count)
    grad_attended = out_back(grad1_low, out_weight)
    parts = attend_backward(scalars, projected, attended, logs, grad_attended)
    bias_parts = [jnp.sum(part, axis=0, keepdims=True, dtype=f32) for part in (parts[0], parts[2])]
    grad_vec = jnp.concatenate(
        bias_parts + [sums1[0:3], sums2[0:3], bias1.reshape(-1, feat), jnp.zeros((16 - kinds, feat), f32)]
    ).astype(bf16)
    first_terms = scatter_sum(
        *weight_grad(
            index,
            count,
            x,
            parts[0],
            x,
            parts[1],
            x,
            parts[2],
            attended,
            grad1_low,
            grad_vec,
            jnp.eye(16, VEC_PAD, dtype=bf16),
        ),
        count,
    )
    grad_row = input_back(parts, qkv_weight, grad1)

    def give_back(row):
        row = row.reshape(groups, quarter, feat)
        beside = swap(jnp.stack([row[1], row[3]]), 1, count)
        across = swap(jnp.stack([row[2], beside[1]]), 2, count)
        turned = jnp.stack([row[0], beside[0], across[0], across[1]])
        return jnp.stack(
            [lax.dynamic_index_in_dim(turned, dp_index ^ m, 0, keepdims=False) for m in range(4)]
        )

    output = give_back(out_row)
    input_grad = give_back(grad_row)

    def total(terms):
        result = terms[0][0].astype(f32)
        for term in terms[1:]:
            result = result + term[0].astype(f32)
        return result

    first_sum = total(first_terms)
    gradients = (
        first_sum[:, : 3 * feat],
        first_sum[:, 3 * feat : 4 * feat],
        total(up_terms),
        total(down_terms).T,
        first_sum[:, 4 * feat : 4 * feat + kinds].T,
    )
    masters = (qkv_master, out_master, up_master, down_master, vec_master)
    firsts = (qkv_first, out_first, up_first, down_first, vec_first)
    seconds = (qkv_second, out_second, up_second, down_second, vec_second)
    updates = [
        adam_step(
            masters[i], firsts[i], seconds[i], gradients[i], step_rates[i], step_decays[i]
        )
        for i in range(5)
    ]
    return (output, input_grad) + tuple(updates[i][part] for part in range(3) for i in range(5))


def solution(mesh):
    across_rows = P(("seq", "dp"), None)
    across_columns = P(None, ("seq", "dp"))
    slots = P("seq", "dp", None)
    matrices = (across_rows, across_rows, across_rows, across_columns, across_columns)
    return jax.shard_map(
        on_device,
        mesh=mesh,
        in_specs=(slots, slots, P(), P()) + matrices * 3,
        out_specs=(slots, slots) + matrices * 3,
        check_vma=False,
    )
```

```python
import functools

import jax
import jax.numpy as jnp
from jax import lax
from jax.experimental import pallas as pl
from jax.experimental.pallas import tpu as pltpu
from jax.sharding import PartitionSpec as P

HEADS = 12
STEP = 10
AXES = ("seq", "dp")

norm_eps = 1e-12
beta_one = 0.5
beta_two = 0.5
adam_eps = 1e-08
masked_score = -1e30
step_rates = (0.06, 0.3, 0.05, 0.025, 0.5)
step_decays = (0.01, 0.01, 0.01, 0.01, 0.0)

f32 = jnp.float32
bf16 = jnp.bfloat16
VEC_PAD = 128
WEIGHT = 2000

NT = (((1,), (1,)), ((), ()))
TN = (((0,), (0,)), ((), ()))


def dot(a, b, dims=(((1,), (0,)), ((), ()))):
    return lax.dot_general(a, b, dims, preferred_element_type=f32)


def params(mib=48):
    return pltpu.CompilerParams(vmem_limit_bytes=mib << 20)


def cost(flops, nbytes, trans=0):
    return pl.CostEstimate(
        flops=int(flops), bytes_accessed=int(nbytes), transcendentals=int(trans)
    )


def full(shape):
    return pl.BlockSpec(shape, lambda *_: (0,) * len(shape))


def shape_of(shape, dtype=bf16):
    return jax.ShapeDtypeStruct(shape, dtype)


ANY = pl.BlockSpec(memory_space=pl.ANY)
NEAR = pl.BlockSpec(memory_space=pltpu.VMEM)


def call(kernel, out_shape, operands, in_specs=None, out_specs=None, scalars=(), grid=(1,), scratch=(), mib=16, flops=0, trans=0, aliases=None):
    name = (kernel.func if isinstance(kernel, functools.partial) else kernel).__name__
    outs = out_shape if isinstance(out_shape, tuple) else (out_shape,)
    moved = sum(o.size * o.dtype.itemsize for o in tuple(operands) + outs)
    if in_specs is None:
        in_specs = [full(operand.shape) for operand in operands]
    if out_specs is None:
        out_specs = tuple(full(o.shape) for o in outs)
    result = pl.pallas_call(
        kernel,
        out_shape=outs,
        grid_spec=pltpu.PrefetchScalarGridSpec(
            num_scalar_prefetch=len(scalars),
            grid=grid,
            in_specs=in_specs,
            out_specs=out_specs,
            scratch_shapes=scratch,
        ),
        input_output_aliases=aliases or {},
        compiler_params=params(mib),
        cost_estimate=cost(WEIGHT * flops, WEIGHT * moved, trans),
        name=name.replace("_kernel", ""),
    )(*scalars, *operands)
    return result if isinstance(out_shape, tuple) else result[0]


def swap(value, mask, count):
    return lax.ppermute(value, AXES, [(i, i ^ mask) for i in range(count)])


def after(value, *earlier):
    return lax.optimization_barrier((value, earlier))[0]


def line_masks(count):
    masks, mask = [], count // 2
    while mask >= 8:
        masks.append(mask)
        mask //= 2
    return masks


def line_offset(entry, count):
    return sum(mask for bit, mask in enumerate(line_masks(count)) if entry >> bit & 1)


def longer(line, received):
    return jnp.concatenate([line, received], axis=0)


def gather_plane(line, count):
    return swap(line, 4, count), swap(line, 2, count)


def halves_kernel(x_ref, y_ref, first_ref, second_ref):
    half = first_ref.shape[2]
    first_ref[...] = y_ref[:, :, :half]
    second_ref[...] = x_ref[:, :, half:]


def cross_halves(piece_x, piece_y):
    lines, rows, cols = piece_x.shape
    half = cols // 256 * 128
    return call(
        halves_kernel,
        (shape_of((lines, rows, half)), shape_of((lines, rows, cols - half))),
        (piece_x, piece_y),
    )


def gather_cross(halves, count):
    return [swap(halves[0], 4, count), swap(halves[1], 2, count)]


def beside_core(pieces, count):
    return [swap(piece, 1, count) for piece in pieces]


def place_kernel(plan, *refs):
    index_ref, sources, targets, sem = refs[0], refs[1 : 1 + plan[0]], refs[1 + plan[0] : -1], refs[-1]
    for source, entry, target, at, column in plan[1]:
        piece = sources[source].at[entry] if isinstance(entry, int) else sources[source].at[entry(index_ref[0])]
        spot = at(index_ref[0]) if callable(at) else at
        if column is None:
            goal = targets[target].at[spot]
        else:
            goal = targets[target].at[spot, :, pl.ds(column, sources[source].shape[2])]
        pltpu.make_async_copy(piece, goal, sem).start()
    for target in targets:
        pltpu.make_async_copy(target, target, sem).wait()


def place(index, sources, out_shape, moves, held=NEAR):
    return call(
        functools.partial(place_kernel, (len(sources), moves)),
        out_shape,
        sources,
        in_specs=[held] * len(sources),
        out_specs=(ANY,) * (len(out_shape) if isinstance(out_shape, tuple) else 1),
        scalars=(index,),
        scratch=[pltpu.SemaphoreType.DMA],
        mib=16,
    )


def assemble(index, pieces, others, count):
    lines, rows, cols = pieces[0].shape
    moves = []
    for core, held in enumerate((pieces, others)):
        for which, piece in enumerate(held):
            column = held[3].shape[2] if which == 4 else 0
            for z in range(lines):
                offset = line_offset(z, count) + 2 * min(which, 3) + core
                at = lambda index, offset=offset: index ^ offset
                moves.append((core * len(pieces) + which, z, 0, at, column))
    out = place(index, pieces + others, shape_of((8 * lines, rows, cols)), moves, ANY)
    return out.reshape(8 * lines * rows, cols)


def total_of(*terms):
    total = terms[0].astype(f32)
    for term in terms[1:]:
        total = total + term.astype(f32)
    return total


def cross_kernel(own_ref, received_ref, *out_refs):
    total = total_of(own_ref[0], received_ref[0]).astype(bf16)
    start = 0
    for out_ref in out_refs:
        cols = out_ref.shape[2]
        out_ref[...] = total[:, :, start : start + cols]
        start += cols


def plane_kernel(way, own_y_ref, own_x_ref, received_y_ref, received_x_ref, *refs):
    piece_y = total_of(own_y_ref[0], received_y_ref[0])
    piece_x = total_of(own_x_ref[0], received_x_ref[0])
    y_ref, x_ref = refs[-2:]
    if way == "x":
        piece_y = piece_y + refs[0][...].astype(f32)
    elif way == "y":
        piece_x = piece_x + refs[0][...].astype(f32)
    else:
        half = refs[0].shape[2]
        via_x, via_y = refs[0][...].astype(f32), refs[1][...].astype(f32)
        piece_y = jnp.concatenate([piece_y[:, :, :half] + via_x, piece_y[:, :, half:]], axis=2)
        piece_x = jnp.concatenate([piece_x[:, :, :half], piece_x[:, :, half:] + via_y], axis=2)
    y_ref[...] = piece_y.astype(bf16)
    x_ref[...] = piece_x.astype(bf16)


def line_kernel(own_ref, received_ref, from_y_ref, from_x_ref, *out_refs):
    total = total_of(own_ref[0], received_ref[0], from_y_ref[...], from_x_ref[...]).astype(bf16)
    span = out_refs[0].shape[0]
    for at, out_ref in enumerate(out_refs):
        out_ref[...] = total[at * span : (at + 1) * span]


def fold_kernel(mine_ref, received_ref, *out_refs):
    total = total_of(mine_ref[...], received_ref[...]).astype(bf16)
    span = out_refs[0].shape[0]
    for at, out_ref in enumerate(out_refs):
        out_ref[...] = total[at * span : (at + 1) * span]


class Scatter:
    def __init__(self, own, other, count, way):
        self.own, self.count, self.way = own, count, way
        self.piece = own.shape[1:]
        self.received = swap(other, 1, count)

    def part(self, at):
        return pl.BlockSpec((1,) + self.piece, lambda i: (at, 0, 0, 0))

    def cross(self, *earlier):
        self.received = after(self.received, *earlier)
        lines, rows, cols = self.piece
        half = cols // 256 * 128
        sizes = (half, cols - half) if self.way == "both" else (cols,)
        sent = call(
            cross_kernel,
            tuple(shape_of((lines, rows, size)) for size in sizes),
            (self.own, self.received),
            in_specs=[self.part(3), self.part(3)],
        )
        masks = {"x": (4,), "y": (2,), "both": (4, 2)}[self.way]
        self.via = tuple(swap(piece, mask, self.count) for piece, mask in zip(sent, masks))
        return sent

    def plane(self, *earlier):
        self.via = after(self.via, *earlier)
        piece = shape_of(self.piece)
        sent = call(
            functools.partial(plane_kernel, self.way),
            (piece, piece),
            (self.own, self.own, self.received, self.received) + self.via,
            in_specs=[self.part(1), self.part(2), self.part(1), self.part(2)]
            + [full(via.shape) for via in self.via],
        )
        self.pieces = (swap(sent[0], 2, self.count), swap(sent[1], 4, self.count))
        return sent

    def line(self, *earlier):
        from_y, from_x = after(self.pieces, *earlier)
        lines, rows, cols = self.piece
        self.masks = line_masks(self.count)
        self.terms = call(
            line_kernel,
            (shape_of((lines // 2, rows, cols)),) * 2,
            (self.own, self.received, from_y, from_x),
            in_specs=[self.part(0), self.part(0), full(self.piece), full(self.piece)],
        )
        return self.step()

    def step(self, *earlier):
        mine, sent = self.terms
        self.terms = (mine, swap(sent, self.masks.pop(), self.count))
        return mine, sent

    def fold(self, *earlier):
        while self.masks:
            mine, received = after(self.terms, *earlier)
            lines, rows, cols = mine.shape
            self.terms = call(fold_kernel, (shape_of((lines // 2, rows, cols)),) * 2, (mine, received))
            sent = self.step()
        return sent


def turn(vec_ref, other_dims):
    kinds = vec_ref.shape[0]
    eye = (
        lax.broadcasted_iota(jnp.int32, (kinds, VEC_PAD), 0)
        == lax.broadcasted_iota(jnp.int32, (kinds, VEC_PAD), 1)
    )
    return dot(vec_ref, eye.astype(f32).astype(bf16), TN)


def vectors_of(block, first, many=8):
    pick = (
        lax.broadcasted_iota(jnp.int32, (many, VEC_PAD), 0) + first
        == lax.broadcasted_iota(jnp.int32, (many, VEC_PAD), 1)
    )
    return dot(pick.astype(f32).astype(bf16), block, NT)


def pack_first_kernel(qkv_ref, vec_ref, out_ref):
    cols = qkv_ref.shape[1]
    out_ref[0, :, :cols] = qkv_ref[...].astype(bf16)
    out_ref[0, :, cols:] = turn(vec_ref[...].astype(bf16), VEC_PAD).astype(bf16)


def pack_rest_kernel(up_ref, out_ref, down_ref, second_ref, third_ref):
    cols = up_ref.shape[1]
    second_ref[0, :, :cols] = up_ref[...].astype(bf16)
    second_ref[0, :, cols:] = out_ref[...].astype(bf16)
    third_ref[0] = down_ref[...].astype(bf16)


def project_kernel(x_ref, w_ref, vec_ref, o_ref):
    step = pl.program_id(0)
    bias = vectors_of(vec_ref[...], 0)
    row = jnp.where(step == 0, bias[0:1], jnp.where(step == 2, bias[1:2], 0.0))
    o_ref[...] = (dot(x_ref[...], w_ref[...]) + row).astype(bf16)


def vec_block(feat):
    return pl.BlockSpec((feat, VEC_PAD), lambda *_: (0, 3 * feat // VEC_PAD))


def project(x, weight):
    slots, feat = x.shape
    tile = lambda rows: pl.BlockSpec((rows, feat), lambda i: (0, i))
    return call(
        project_kernel,
        shape_of((slots, 3 * feat)),
        (x, weight, weight),
        in_specs=[full(x.shape), tile(feat), vec_block(feat)],
        out_specs=(tile(slots),),
        grid=(3,),
        mib=20,
        flops=6 * slots * feat * feat,
    )


def live_slots(quarter, index_ref, reads_ref, lengths_ref, slots):
    groups = slots // quarter
    own = index_ref[0] & (groups - 1)
    length = lengths_ref[reads_ref[index_ref[0]]]
    at = lax.broadcasted_iota(jnp.int32, (slots, 1), 0)
    position = at
    for part in range(groups):
        inside = (at >= part * quarter) & (at < (part + 1) * quarter)
        position = jnp.where(inside, at + ((own ^ part) - part) * quarter, position)
    return position < length


def lane_parts(value):
    high = value.astype(bf16).astype(f32)
    middle = (value - high).astype(bf16).astype(f32)
    return high, middle, value - high - middle


def attend_forward_kernel(quarter, index_ref, reads_ref, lengths_ref, q_ref, k_ref, v_ref, *refs):
    o_ref, log_ref = refs[-2:]
    slots, width = q_ref.shape
    half = width // 2
    scale = half ** (-0.5)
    lane = lax.broadcasted_iota(jnp.int32, (slots, width), 1)
    bias = jnp.where(live_slots(quarter, index_ref, reads_ref, lengths_ref, slots), 0.0, masked_score)
    query = q_ref[...].astype(f32) * scale
    key = k_ref[...].astype(f32)
    value = v_ref[...].astype(f32)
    mixed, logs = [], []
    for head in range(2):
        mine = (lane >= half) if head else (lane < half)
        base = 0 if head else half
        query_ext = jnp.where(mine, query, jnp.where(lane == base, 1.0, 0.0)).astype(bf16)
        key_ext = jnp.where(mine, key, jnp.where(lane == base, bias, 0.0)).astype(bf16)
        value_ext = jnp.where(mine, value, 1.0).astype(bf16)
        scores = dot(query_ext, key_ext, NT)
        top = jnp.max(scores, axis=1, keepdims=True)
        weights = jnp.exp(scores - top).astype(bf16)
        total = dot(weights, value_ext)
        sums = pltpu.roll(total, half, 1)
        mixed.append(total / sums)
        logs.append(top + jnp.log(jnp.where(mine, sums, 1.0)))
    first = lane < half
    o_ref[...] = jnp.where(first, mixed[0], mixed[1]).astype(bf16)
    log_ref[...] = jnp.where(first, logs[0], logs[1])


def attend_forward(scalars, projected, feat, quarter, begin, pairs, held=()):
    slots = projected.shape[0]
    width = 2 * feat // HEADS
    every = feat // width
    block = lambda offset: pl.BlockSpec((slots, width), lambda i, *_: (0, i + offset))
    return call(
        functools.partial(attend_forward_kernel, quarter),
        (shape_of((slots, feat)), shape_of((slots, feat), f32)),
        (projected,) * 3 + held,
        in_specs=[block(begin + k * every) for k in range(3)] + [ANY] * len(held),
        out_specs=(block(begin),) * 2,
        scalars=scalars,
        grid=(pairs,),
        flops=8 * slots * slots * width * pairs,
        trans=2 * pairs * slots * slots,
        aliases={6 + k: k for k in range(len(held))},
    )


def attend_backward_kernel(
    quarter, index_ref, reads_ref, lengths_ref, q_ref, k_ref, v_ref, o_ref, log_ref, g_ref, *refs
):
    dq_ref, dk_ref, dv_ref, bq_ref, bv_ref = refs[-5:]
    slots, width = q_ref.shape
    half = width // 2
    scale = half ** (-0.5)
    lane = lax.broadcasted_iota(jnp.int32, (slots, width), 1)
    bias = jnp.where(live_slots(quarter, index_ref, reads_ref, lengths_ref, slots), 0.0, masked_score)
    query = q_ref[...].astype(f32) * scale
    key = k_ref[...].astype(f32)
    value = v_ref[...].astype(f32)
    grad_low = g_ref[...]
    grad = grad_low.astype(f32)
    product = grad * o_ref[...].astype(f32)
    log_all = pltpu.roll(log_ref[...], half, 1)
    query_low = query.astype(bf16)
    key_turned = jnp.transpose(key).astype(bf16)
    parts = []
    for head in range(2):
        mine = (lane >= half) if head else (lane < half)
        base = 0 if head else half
        delta = jnp.sum(jnp.where(mine, product, 0.0), axis=1, keepdims=True)
        logs = lane_parts(log_all)
        deltas = lane_parts(delta)
        spot = [lane == base + k for k in range(4)]
        ones = (lane >= base) & (lane < base + 3)
        query_ext = jnp.where(mine, query, jnp.where(spot[3], 1.0, 0.0))
        grad_ext = jnp.where(mine, grad, 0.0)
        for k in range(3):
            query_ext = jnp.where(spot[k], -logs[k], query_ext)
            grad_ext = jnp.where(spot[k], -deltas[k], grad_ext)
        key_ext = jnp.where(mine, key, jnp.where(ones, 1.0, jnp.where(spot[3], bias, 0.0)))
        value_ext = jnp.where(mine, value, jnp.where(ones, 1.0, 0.0))
        probs = jnp.exp(dot(key_ext.astype(bf16), query_ext.astype(bf16), NT))
        grad_scores = (probs * dot(value_ext.astype(bf16), grad_ext.astype(bf16), NT)).astype(bf16)
        parts.append(
            (
                dot(key_turned, grad_scores),
                dot(grad_scores, query_low),
                dot(probs.astype(bf16), grad_low),
            )
        )
    first = lane < half
    turned = lax.broadcasted_iota(jnp.int32, (width, slots), 0) < half
    grad_query = (jnp.transpose(jnp.where(turned, parts[0][0], parts[1][0])) * scale).astype(bf16)
    grad_value = jnp.where(first, parts[0][2], parts[1][2]).astype(bf16)
    dq_ref[...] = grad_query
    dk_ref[...] = jnp.where(first, parts[0][1], parts[1][1]).astype(bf16)
    dv_ref[...] = grad_value
    bq_ref[...] = column_sum(grad_query.astype(f32))
    bv_ref[...] = column_sum(grad_value.astype(f32))


def attend_backward(scalars, projected, attended, logs, grad_attended, quarter, begin, pairs, held=()):
    slots, feat = attended.shape
    width = 2 * feat // HEADS
    every = feat // width
    block = lambda offset: pl.BlockSpec((slots, width), lambda i, *_: (0, i + offset))
    row = pl.BlockSpec((1, width), lambda i, *_: (0, i + begin))
    return call(
        functools.partial(attend_backward_kernel, quarter),
        (shape_of((slots, feat)),) * 3 + (shape_of((1, feat), f32),) * 2,
        (projected,) * 3 + (attended, logs, grad_attended) + held,
        in_specs=[block(begin + k * every) for k in range(3)] + [block(begin)] * 3 + [ANY] * len(held),
        out_specs=(block(begin),) * 3 + (row,) * 2,
        scalars=scalars,
        grid=(pairs,),
        flops=20 * slots * slots * width * pairs,
        trans=2 * pairs * slots * slots,
        aliases={9 + k: k for k in range(len(held))},
    )


def normalize(total):
    centered = total - jnp.mean(total, axis=1, keepdims=True)
    scale = lax.rsqrt(jnp.mean(centered * centered, axis=1, keepdims=True) + norm_eps)
    return centered * scale, scale


def normalize_back(grad, normed, scale):
    return (
        grad
        - jnp.mean(grad, axis=1, keepdims=True)
        - normed * jnp.mean(grad * normed, axis=1, keepdims=True)
    ) * scale


def column_sum(value):
    return jnp.sum(value, axis=0, keepdims=True)


def attn_out_kernel(a_ref, w_ref, x_ref, vec_ref, n_ref, s_ref, low_ref):
    vec = vectors_of(vec_ref[...], 0)
    normed, scale = normalize(x_ref[...].astype(f32) + dot(a_ref[...], w_ref[...]) + vec[2:3])
    n_ref[...] = normed
    s_ref[...] = scale
    low_ref[...] = (normed * vec[3:4] + vec[4:5]).astype(bf16)


def out_block(feat, second_weight):
    last = second_weight.shape[1] // feat - 1
    return pl.BlockSpec((feat, feat), lambda *_: (0, last))


def attn_out(attended, second_weight, x, first_weight):
    slots, feat = x.shape
    return call(
        attn_out_kernel,
        (shape_of((slots, feat), f32), shape_of((slots, 1), f32), shape_of((slots, feat))),
        (attended, second_weight, x, first_weight),
        in_specs=[full(x.shape), out_block(feat, second_weight), full(x.shape), vec_block(feat)],
        flops=2 * slots * feat * feat,
    )


def feed_up_kernel(low_ref, up_ref, vec_ref, active_ref, slope_ref):
    bias = vectors_of(vec_ref[...], 8 + pl.program_id(0))[0:1]
    hidden = dot(low_ref[...], up_ref[...]) + bias
    phi = 0.5 + 0.5 * lax.erf(hidden * 0.5**0.5)
    density = 0.3989422804014327 * jnp.exp(-0.5 * hidden * hidden)
    active_ref[...] = (hidden * phi).astype(bf16)
    slope_ref[...] = (phi + hidden * density).astype(bf16)


def feed_up(low, second_weight, first_weight):
    slots, feat = low.shape
    wide = second_weight.shape[1] - feat
    column = lambda rows: pl.BlockSpec((rows, feat), lambda i: (0, i))
    return call(
        feed_up_kernel,
        (shape_of((slots, wide)),) * 2,
        (low, second_weight, first_weight),
        in_specs=[full(low.shape), column(feat), vec_block(feat)],
        out_specs=(column(slots),) * 2,
        grid=(wide // feat,),
        mib=20,
        flops=2 * slots * feat * wide,
        trans=2 * slots * wide,
    )


def put_row(value, refs):
    near_ref, beside_ref, across_ref = refs
    quarter = near_ref.shape[1]
    near_ref[0] = value[:quarter]
    beside_ref[0] = value[quarter : 2 * quarter]
    across_ref[0] = value[2 * quarter : 3 * quarter]
    across_ref[1] = value[3 * quarter :]


def row_shapes(quarter, feat):
    return (
        shape_of((1, quarter, feat)),
        shape_of((1, quarter, feat)),
        shape_of((2, quarter, feat)),
    )


def feed_down_kernel(
    quarter, index_ref, reads_ref, lengths_ref, active_ref, down_ref, n_ref, cot_ref, vec_ref,
    grad_ref, grad_low_ref, sums_ref, *row_refs
):
    slots, feat = n_ref.shape
    vec = vectors_of(vec_ref[...], 0)
    first = n_ref[...] * vec[3:4] + vec[4:5]
    normed, scale = normalize(first + dot(active_ref[...], down_ref[...], NT) + vec[5:6])
    live = live_slots(quarter, index_ref, reads_ref, lengths_ref, slots)
    put_row(jnp.where(live, normed * vec[6:7] + vec[7:8], 0.0).astype(bf16), row_refs)
    grad_result = jnp.where(live, cot_ref[...].astype(f32), 0.0)
    grad = normalize_back(grad_result * vec[6:7], normed, scale)
    grad_ref[...] = grad
    grad_low_ref[...] = grad.astype(bf16)
    sums_ref[0:1, :] = column_sum(grad)
    sums_ref[1:2, :] = column_sum(grad_result * normed)
    sums_ref[2:3, :] = column_sum(grad_result)
    sums_ref[3:8, :] = jnp.zeros((5, feat), f32)


def feed_down(scalars, active, down, normed, cotangent, first_weight, quarter):
    slots, feat = normed.shape
    wide = active.shape[1]
    return call(
        functools.partial(feed_down_kernel, quarter),
        (shape_of((slots, feat), f32), shape_of((slots, feat)), shape_of((8, feat), f32))
        + row_shapes(quarter, feat),
        (active, down, normed, cotangent, first_weight),
        in_specs=[
            full(active.shape), full(down.shape), full(normed.shape), full(normed.shape), vec_block(feat),
        ],
        scalars=scalars,
        mib=36,
        flops=2 * slots * feat * wide,
    )


def feed_back_kernel(
    low_ref, grad_ref, n_ref, s_ref, slope_ref, up_ref, down_ref, vec_ref,
    hidden_ref, bias_ref, out_ref, out_low_ref, sums_ref, acc_ref,
):
    step = pl.program_id(0)
    grad_hidden = dot(low_ref[...], down_ref[...]) * slope_ref[...].astype(f32)
    bias_ref[...] = column_sum(grad_hidden)
    grad_hidden = grad_hidden.astype(bf16)
    hidden_ref[...] = grad_hidden
    back = dot(grad_hidden, up_ref[...], NT)

    @pl.when(step == 0)
    def _():
        acc_ref[...] = grad_ref[...] + back

    @pl.when(step > 0)
    def _():
        acc_ref[...] += back

    @pl.when(step == pl.num_programs(0) - 1)
    def _():
        grad_first = acc_ref[...]
        normed = n_ref[...]
        gain = vectors_of(vec_ref[...], 3)[0:1]
        grad = normalize_back(grad_first * gain, normed, s_ref[...])
        out_ref[...] = grad
        out_low_ref[...] = grad.astype(bf16)
        sums_ref[0:1, :] = column_sum(grad)
        sums_ref[1:2, :] = column_sum(grad_first * normed)
        sums_ref[2:3, :] = column_sum(grad_first)
        sums_ref[3:8, :] = jnp.zeros((5, grad.shape[1]), f32)


def feed_back(grad_low, grad, normed, scale, slope, second_weight, down, first_weight):
    slots, feat = normed.shape
    wide = slope.shape[1]
    whole = full((slots, feat))
    column = lambda rows: pl.BlockSpec((rows, feat), lambda i: (0, i))
    return call(
        feed_back_kernel,
        (
            shape_of((slots, wide)),
            shape_of((1, wide), f32),
            shape_of((slots, feat), f32),
            shape_of((slots, feat)),
            shape_of((8, feat), f32),
        ),
        (grad_low, grad, normed, scale, slope, second_weight, down, first_weight),
        in_specs=[
            whole, whole, whole, full((slots, 1)), column(slots), column(feat), column(feat), vec_block(feat),
        ],
        out_specs=(column(slots), column(1), whole, whole, full((8, feat))),
        grid=(wide // feat,),
        scratch=[pltpu.VMEM((slots, feat), f32)],
        mib=32,
        flops=4 * slots * feat * wide,
    )


def weight_grad_kernel(count, lefts, vectors, index_ref, *refs):
    own_ref, other_ref, hold, sem = refs[-4:]
    index = index_ref[0]
    rows = own_ref.shape[2]
    width = hold.shape[3]
    jobs = []
    column = 0
    for at, left in enumerate(lefts):
        right = refs[at]
        for start in range(0, right.shape[1], width):
            jobs.append((left, at, start, min(width, right.shape[1] - start), column + start))
        column += right.shape[1]
    if vectors:
        jobs.append((None, None, 0, VEC_PAD, column))

    def drain(slot, size):
        view = hold.at[slot, :, :, pl.ds(0, size)]
        pltpu.make_async_copy(view, view, sem.at[slot]).wait()

    for job, (left, right, start, size, column) in enumerate(jobs):
        slot = job % 2
        if job >= 2:
            drain(slot, jobs[job - 2][3])
        if left is None:
            query_ref, value_ref, first_ref, second_ref, wide_ref = refs[-9:-4]
            feat = query_ref.shape[1]
            grads = jnp.concatenate(
                [query_ref[...], value_ref[...], first_ref[0:3, :], second_ref[0:3, :]]
                + [wide_ref[:, at : at + feat] for at in range(0, wide_ref.shape[1], feat)],
                axis=0,
            )
            product = turn(grads.astype(bf16), VEC_PAD)
        else:
            product = dot(refs[left][...], refs[right][:, start : start + size], TN)
        for block in range(count):
            hold[slot, block, :, 0:size] = product[block * rows : (block + 1) * rows, :].astype(bf16)
        for offset in range(8):
            target = other_ref if offset % 2 else own_ref
            for entry in range(count // 8):
                pltpu.make_async_copy(
                    hold.at[slot, index ^ (offset + line_offset(entry, count)), :, pl.ds(0, size)],
                    target.at[offset // 2, entry, :, pl.ds(column, size)],
                    sem.at[slot],
                ).start()
    for job in range(max(0, len(jobs) - 2), len(jobs)):
        drain(job % 2, jobs[job][3])


def weight_grad(index, count, pairs, vectors=()):
    rights = [right for left, right in pairs]
    unique = []
    for left, right in pairs:
        if not any(left is held for held in unique):
            unique.append(left)
    places = [
        len(rights) + next(i for i, held in enumerate(unique) if held is left) for left, right in pairs
    ]
    feat = pairs[0][0].shape[1]
    rows = feat // count
    cols = sum(right.shape[1] for right in rights) + (VEC_PAD if vectors else 0)
    out = shape_of((4, count // 8, rows, cols))
    return call(
        functools.partial(weight_grad_kernel, count, tuple(places), bool(vectors)),
        (out, out),
        tuple(rights) + tuple(unique) + tuple(vectors),
        out_specs=(ANY, ANY),
        scalars=(index,),
        scratch=[pltpu.VMEM((2, count, rows, feat), bf16), pltpu.SemaphoreType.DMA((2,))],
        mib=28,
        flops=2 * pairs[0][0].shape[0] * feat * cols,
    )


def out_back_kernel(grad_ref, w_ref, o_ref):
    o_ref[...] = dot(grad_ref[...], w_ref[...], NT).astype(bf16)


def out_back(grad_low, second_weight):
    slots, feat = grad_low.shape
    return call(
        out_back_kernel,
        shape_of((slots, feat)),
        (grad_low, second_weight),
        in_specs=[full(grad_low.shape), out_block(feat, second_weight)],
        flops=2 * slots * feat * feat,
    )


def input_back_kernel(dq_ref, dk_ref, dv_ref, w_ref, grad_ref, *row_refs):
    feat = dq_ref.shape[1]
    total = grad_ref[...]
    for at, part in enumerate((dq_ref, dk_ref, dv_ref)):
        total = total + dot(part[...], w_ref[:, at * feat : (at + 1) * feat], NT)
    put_row(total.astype(bf16), row_refs)


def input_back(parts, weight, grad, quarter):
    slots, feat = grad.shape
    return call(
        input_back_kernel,
        row_shapes(quarter, feat),
        tuple(parts) + (weight, grad),
        in_specs=[full((slots, feat))] * 3
        + [pl.BlockSpec((feat, 3 * feat), lambda i: (0, 0)), full((slots, feat))],
        mib=24,
        flops=6 * slots * feat * feat,
    )


def adam_kernel(kinds, spans, *refs):
    many = len(kinds)
    terms, states, outs = refs[: -6 * many], refs[-6 * many : -3 * many], refs[-3 * many :]
    total = total_of(*[term[0] for term in terms])
    for at, (kind, span) in enumerate(zip(kinds, spans)):
        master, first_moment, second_moment = (states[part * many + at][...] for part in range(3))
        if span is None:
            rows, cols = master.shape
            block = jnp.pad(total[:, -VEC_PAD:], ((0, VEC_PAD - cols), (0, 0)))
            gradient = jnp.transpose(block)[:rows, :cols]
        else:
            gradient = total[:, span[0] : span[1]]
        results = adam_step(
            master, first_moment, second_moment, gradient, step_rates[kind], step_decays[kind]
        )
        for part in range(3):
            outs[part * many + at][...] = results[part]


def adam(terms, kinds, spans, states):
    ordered = [state[part] for part in range(3) for state in states]
    results = call(
        functools.partial(adam_kernel, kinds, spans),
        tuple(shape_of(state.shape, f32) for state in ordered),
        tuple(terms) + tuple(ordered),
    )
    many = len(kinds)
    return [tuple(results[part * many + at] for part in range(3)) for at in range(many)]


def adam_step(master, first_moment, second_moment, gradient, step_rate, decay_rate):
    first_new = beta_one * first_moment + (1.0 - beta_one) * gradient
    second_new = beta_two * second_moment + (1.0 - beta_two) * gradient * gradient
    ratio = (
        first_new
        / (1.0 - beta_one**STEP)
        / (jnp.sqrt(second_new / (1.0 - beta_two**STEP)) + adam_eps)
    )
    return (master - step_rate * (ratio + decay_rate * master), first_new, second_new)


def on_device(
    tokens,
    cotangent,
    read_lengths,
    row_reads,
    qkv_master,
    out_master,
    up_master,
    down_master,
    vec_master,
    qkv_first,
    out_first,
    up_first,
    down_first,
    vec_first,
    qkv_second,
    out_second,
    up_second,
    down_second,
    vec_second,
):
    groups = lax.axis_size("dp")
    count = groups * lax.axis_size("seq")
    row_count, quarter, feat = tokens.shape
    slots = quarter * groups
    wide = up_master.shape[1]
    half_pairs = HEADS // 4
    index = (lax.axis_index("seq") * groups + lax.axis_index("dp")).astype(jnp.int32).reshape(1)
    scalars = (index, row_reads, read_lengths)

    own = lambda m: lambda index: (index & (groups - 1)) ^ m

    def split_rows(rows_held, first_index):
        return place(
            first_index,
            [rows_held],
            row_shapes(quarter, feat),
            [(0, own(0), 0, 0, None), (0, own(1), 1, 0, None), (0, own(2), 2, 0, None), (0, own(3), 2, 1, None)],
        )

    def take_row(near, beside, across, passed):
        moves = [(0, 0, 0, 0, None), (1, 0, 0, 1, None), (2, 0, 0, 2, None), (3, 1, 0, 3, None)]
        out = place(index, [near, beside, across, passed], shape_of((groups, quarter, feat)), moves)
        return out.reshape(slots, feat)

    def give_row(near, beside, across, passed):
        moves = [(0, 0, 0, own(0), None), (1, 0, 0, own(1), None), (2, 0, 0, own(2), None), (3, 1, 0, own(3), None)]
        return place(index, [near, beside, across, passed], shape_of((groups, quarter, feat)), moves)

    first_block = call(
        pack_first_kernel,
        shape_of((1, qkv_master.shape[0], 3 * feat + VEC_PAD)),
        (qkv_master, vec_master),
    )
    masks = line_masks(count)

    def grow(line, steps, *earlier):
        for mask in steps:
            line = longer(line, after(swap(line, mask, count), *earlier))
        return line

    row_parts = split_rows(tokens, after(index, first_block))
    across = swap(row_parts[2], 2, count)
    half1 = grow(first_block, masks[:-1], row_parts)
    second_block, third_block = call(
        pack_rest_kernel,
        (
            shape_of((1, up_master.shape[0], wide + feat)),
            shape_of((1, up_master.shape[0], wide)),
        ),
        (after(up_master, half1), out_master, down_master.T),
    )
    beside = swap(row_parts[1], 1, count)
    line1 = grow(half1, masks[-1:], second_block)
    x1, y1 = gather_plane(line1, count)
    passed = swap(after(across, line1), 1, count)
    x = take_row(row_parts[0], *after((beside, across, passed), line1))
    half2 = grow(after(second_block, line1), masks[:-1], x)
    other1 = beside_core([line1], count)
    x1, y1 = after((x1, y1), half2, other1)
    halves1 = cross_halves(x1, y1)
    cross1 = gather_cross(halves1, count)
    other1 += beside_core([y1, x1], count)
    line2 = grow(half2, masks[-1:], halves1, other1)
    x2, y2 = gather_plane(line2, count)
    cross1 = after(cross1, line2)
    other1 += beside_core(cross1, count)
    first_weight = assemble(index, [line1, y1, x1, *cross1], other1, count)

    projected = project(x, first_weight)
    half3 = grow(after(third_block, line2), masks[:-1], projected)
    x2, y2 = after((x2, y2), half3)
    halves2 = cross_halves(x2, y2)
    cross2 = gather_cross(halves2, count)
    line3 = grow(half3, masks[-1:], halves2)
    x3, y3 = gather_plane(line3, count)
    other2 = beside_core([line2, y2, x2], count)
    held = attend_forward(
        (after(index, line3),) + scalars[1:], projected, feat, quarter, 0, half_pairs
    )
    attended, logs = attend_forward(
        (after(index, other2),) + scalars[1:], projected, feat, quarter, half_pairs, half_pairs, held
    )
    cross2 = after(cross2, attended)
    other2 += beside_core(cross2, count)
    second_weight = assemble(index, [line2, y2, x2, *cross2], other2, count)
    normed, scale, low = attn_out(attended, second_weight, x, first_weight)
    other3 = beside_core([line3], count)
    x3, y3 = after((x3, y3), low, other3)
    halves3 = cross_halves(x3, y3)
    cross3 = gather_cross(halves3, count)
    other3 += beside_core([y3, x3], count)
    cotangent_parts = split_rows(cotangent, after(index, halves3))
    across = swap(cotangent_parts[2], 2, count)
    beside = swap(cotangent_parts[1], 1, count)
    active, slope = feed_up(after(low, cotangent_parts), second_weight, first_weight)
    cross3, other3 = after((cross3, other3), active)
    other3 += beside_core(cross3, count)
    down_weight = assemble(index, [line3, y3, x3, *cross3], other3, count)
    passed = swap(across, 1, count)
    grad_output = take_row(cotangent_parts[0], *after((beside, across, passed), down_weight))

    grad2, grad2_low, sums2, *out_parts = feed_down(
        scalars, active, down_weight, normed, grad_output, first_weight, quarter
    )
    down_parts = weight_grad(index, count, [(grad2_low, active)])
    down_sum = Scatter(*down_parts, count, "both")
    across = swap(out_parts[2], 2, count)
    beside = swap(out_parts[1], 1, count)
    grad_hidden, bias1, grad1, grad1_low, sums1 = feed_back(
        after(grad2_low, down_parts), grad2, normed, scale, slope, second_weight, down_weight, first_weight
    )
    across, beside = after((across, beside), grad1_low)
    passed = swap(across, 1, count)
    done = down_sum.cross(grad1_low)
    up_parts = weight_grad(
        index, count, [(after(low, done), grad_hidden), (attended, grad1_low)]
    )
    up_sum = Scatter(*up_parts, count, "both")
    done = down_sum.plane(up_parts)
    grad_attended = out_back(after(grad1_low, done, passed), second_weight)
    output = give_row(out_parts[0], *after((beside, across, passed), done))
    done = up_sum.cross(grad_attended)
    held = attend_backward(
        (after(index, done),) + scalars[1:],
        projected, attended, logs, grad_attended, quarter, 0, half_pairs,
    )
    done = (down_sum.line(held), up_sum.plane(held))
    *parts, bias_query, bias_value = attend_backward(
        (after(index, done),) + scalars[1:],
        projected, attended, logs, grad_attended, quarter, half_pairs, half_pairs, held,
    )
    done = down_sum.fold(parts)
    first_parts = weight_grad(
        index,
        count,
        [(after(x, done), parts[0]), (x, parts[1]), (x, parts[2])],
        (bias_query, bias_value, sums1, sums2, bias1),
    )
    first_sum = Scatter(*first_parts, count, "both")
    grad_parts = input_back(after(parts, first_parts), first_weight, grad1, quarter)
    done = up_sum.line(grad_parts)
    done = first_sum.cross(done)
    done = up_sum.fold(done)
    (down_new,) = adam(
        after(down_sum.terms, done),
        (3,),
        ((0, wide),),
        [(down_master.T, down_first.T, down_second.T)],
    )
    done = first_sum.plane(down_new)
    up_new, out_new = adam(
        after(up_sum.terms, done),
        (2, 1),
        ((0, wide), (wide, wide + feat)),
        [(up_master, up_first, up_second), (out_master, out_first, out_second)],
    )
    beside = swap(after(grad_parts[1], up_new), 1, count)
    line = first_sum.line(up_new)
    across = swap(after(grad_parts[2], line), 2, count)
    done = first_sum.fold(beside)
    passed = swap(after(across, done), 1, count)
    input_grad = give_row(grad_parts[0], beside, across, passed)
    qkv_new, vec_new = adam(
        after(first_sum.terms, input_grad),
        (0, 4),
        ((0, 3 * feat), None),
        [(qkv_master, qkv_first, qkv_second), (vec_master, vec_first, vec_second)],
    )
    down_new = tuple(value.T for value in down_new)
    updates = (qkv_new, out_new, up_new, down_new, vec_new)
    return (output, input_grad) + tuple(update[part] for part in range(3) for update in updates)


def solution(mesh):
    across_rows = P(("seq", "dp"), None)
    across_columns = P(None, ("seq", "dp"))
    slots = P("seq", "dp", None)
    matrices = (across_rows, across_rows, across_rows, across_columns, across_columns)
    return jax.shard_map(
        on_device,
        mesh=mesh,
        in_specs=(slots, slots, P(), P()) + matrices * 3,
        out_specs=(slots, slots) + matrices * 3,
        check_vma=False,
    )
```

```python
import functools

import jax
import jax.numpy as jnp
from jax import lax
from jax.experimental import pallas as pl
from jax.experimental.pallas import tpu as pltpu
from jax.sharding import PartitionSpec as P

HEADS = 12
STEP = 10
AXES = ("seq", "dp")

norm_eps = 1e-12
beta_one = 0.5
beta_two = 0.5
adam_eps = 1e-08
masked_score = -1e30
step_rates = (0.06, 0.3, 0.05, 0.025, 0.5)
step_decays = (0.01, 0.01, 0.01, 0.01, 0.0)

f32 = jnp.float32
bf16 = jnp.bfloat16
VEC_PAD = 128
WEIGHT = 2000

NT = (((1,), (1,)), ((), ()))
TN = (((0,), (0,)), ((), ()))


def dot(a, b, dims=(((1,), (0,)), ((), ()))):
    return lax.dot_general(a, b, dims, preferred_element_type=f32)


def params(mib=48):
    return pltpu.CompilerParams(vmem_limit_bytes=mib << 20)


def cost(flops, nbytes, trans=0):
    return pl.CostEstimate(
        flops=int(flops), bytes_accessed=int(nbytes), transcendentals=int(trans)
    )


def full(shape):
    return pl.BlockSpec(shape, lambda *_: (0,) * len(shape))


def shape_of(shape, dtype=bf16):
    return jax.ShapeDtypeStruct(shape, dtype)


ANY = pl.BlockSpec(memory_space=pl.ANY)
NEAR = pl.BlockSpec(memory_space=pltpu.VMEM)


def call(kernel, out_shape, operands, in_specs=None, out_specs=None, scalars=(), grid=(1,), scratch=(), mib=16, flops=0, trans=0, aliases=None, light=False):
    name = (kernel.func if isinstance(kernel, functools.partial) else kernel).__name__
    outs = out_shape if isinstance(out_shape, tuple) else (out_shape,)
    moved = sum(o.size * o.dtype.itemsize for o in tuple(operands) + outs)
    if in_specs is None:
        in_specs = [full(operand.shape) for operand in operands]
    if out_specs is None:
        out_specs = tuple(full(o.shape) for o in outs)
    result = pl.pallas_call(
        kernel,
        out_shape=outs,
        grid_spec=pltpu.PrefetchScalarGridSpec(
            num_scalar_prefetch=len(scalars),
            grid=grid,
            in_specs=in_specs,
            out_specs=out_specs,
            scratch_shapes=scratch,
        ),
        input_output_aliases=aliases or {},
        compiler_params=params(mib),
        cost_estimate=cost(0, WEIGHT * moved) if light else cost(WEIGHT * max(flops, 2e7), WEIGHT * moved, trans),
        name=name.replace("_kernel", ""),
    )(*scalars, *operands)
    return result if isinstance(out_shape, tuple) else result[0]


def swap(value, mask, count):
    return lax.ppermute(value, AXES, [(i, i ^ mask) for i in range(count)])


def after(value, *earlier):
    return lax.optimization_barrier((value, earlier))[0]


def line_masks(count):
    masks, mask = [], count // 2
    while mask >= 8:
        masks.append(mask)
        mask //= 2
    return masks


def line_offset(entry, count):
    return sum(mask for bit, mask in enumerate(line_masks(count)) if entry >> bit & 1)


def longer(line, received):
    return jnp.concatenate([line, received], axis=0)


def half_of(cols):
    return cols // 256 * 128


def pass_on_kernel(cols, half, from_x_ref, from_y_ref, *refs):
    to_x_ref, to_y_ref = refs[-2:]
    first = from_y_ref.shape[2] - cols
    to_x_ref[:, :, :half] = from_y_ref[:, :, first : first + half]
    first = from_x_ref.shape[2] - cols
    to_y_ref[:, :, : cols - half] = from_x_ref[:, :, first + half :]
    if len(refs) == 3:
        to_x_ref[:, :, half:] = refs[0][...]
        to_y_ref[:, :, cols - half :] = refs[0][...]


def pass_on(got, cols, half, line, count):
    lines, rows, _ = got[0].shape
    more = () if line is None else (line,)
    width = sum(piece.shape[2] for piece in more)
    sent = call(
        functools.partial(pass_on_kernel, cols, half),
        (shape_of((lines, rows, half + width)), shape_of((lines, rows, cols - half + width))),
        tuple(got) + more,
        light=True,
    )
    return swap(sent[0], 4, count), swap(sent[1], 2, count)


def place_kernel(plan, *refs):
    sources, targets, sem = refs[1 : 1 + plan[0]], refs[1 + plan[0] : -1], refs[-1]
    index = refs[0][0]

    def spot(ref, at, columns):
        at = at(index) if callable(at) else at
        return ref.at[at] if columns is None else ref.at[at, :, pl.ds(*columns)]

    for source, entry, columns, target, at, there in plan[1]:
        pltpu.make_async_copy(
            spot(sources[source], entry, columns), spot(targets[target], at, there), sem
        ).start()
    for target in targets:
        pltpu.make_async_copy(target, target, sem).wait()


def place(index, sources, out_shape, moves, held=NEAR, light=True):
    return call(
        functools.partial(place_kernel, (len(sources), moves)),
        out_shape,
        sources,
        in_specs=[held] * len(sources),
        out_specs=(ANY,) * (len(out_shape) if isinstance(out_shape, tuple) else 1),
        scalars=(index,),
        scratch=[pltpu.SemaphoreType.DMA],
        mib=16,
        light=light,
    )


def assemble(index, line, got, passed, others, half, count):
    lines, rows, cols = line.shape
    moves, sources = [], []
    for core, (line, got, passed) in enumerate(((line, got, passed), others)):
        base = len(sources)
        sources += [line, *got, *passed]
        parts = [
            (0, 0, (0, cols), (0, cols)),
            (1, 4, (got[0].shape[2] - cols, cols), (0, cols)),
            (2, 2, (got[1].shape[2] - cols, cols), (0, cols)),
            (3, 6, (0, half), (0, half)),
            (4, 6, (0, cols - half), (half, cols - half)),
        ]
        for which, offset, columns, there in parts:
            for z in range(lines):
                mask = line_offset(z, count) + offset + core
                at = lambda index, mask=mask: index ^ mask
                moves.append((base + which, z, columns, 0, at, there))
    out = place(index, sources, shape_of((8 * lines, rows, cols)), moves, ANY)
    return out.reshape(8 * lines * rows, cols)


def total_of(*terms):
    total = terms[0].astype(f32)
    for term in terms[1:]:
        total = total + term.astype(f32)
    return total


def cross_kernel(own_ref, received_ref, *out_refs):
    total = total_of(own_ref[0], received_ref[0]).astype(bf16)
    start = 0
    for out_ref in out_refs:
        cols = out_ref.shape[2]
        out_ref[...] = total[:, :, start : start + cols]
        start += cols


def plane_kernel(way, own_y_ref, own_x_ref, received_y_ref, received_x_ref, *refs):
    piece_y = total_of(own_y_ref[0], received_y_ref[0])
    piece_x = total_of(own_x_ref[0], received_x_ref[0])
    y_ref, x_ref = refs[-2:]
    if way == "x":
        piece_y = piece_y + refs[0][...].astype(f32)
    elif way == "y":
        piece_x = piece_x + refs[0][...].astype(f32)
    else:
        half = refs[0].shape[2]
        via_x, via_y = refs[0][...].astype(f32), refs[1][...].astype(f32)
        piece_y = jnp.concatenate([piece_y[:, :, :half] + via_x, piece_y[:, :, half:]], axis=2)
        piece_x = jnp.concatenate([piece_x[:, :, :half], piece_x[:, :, half:] + via_y], axis=2)
    y_ref[...] = piece_y.astype(bf16)
    x_ref[...] = piece_x.astype(bf16)


def line_kernel(own_ref, received_ref, from_y_ref, from_x_ref, *out_refs):
    total = total_of(own_ref[0], received_ref[0], from_y_ref[...], from_x_ref[...]).astype(bf16)
    span = out_refs[0].shape[0]
    for at, out_ref in enumerate(out_refs):
        out_ref[...] = total[at * span : (at + 1) * span]


def fold_kernel(mine_ref, received_ref, *out_refs):
    total = total_of(mine_ref[...], received_ref[...]).astype(bf16)
    span = out_refs[0].shape[0]
    for at, out_ref in enumerate(out_refs):
        out_ref[...] = total[at * span : (at + 1) * span]


class Scatter:
    def __init__(self, own, other, count, way):
        self.own, self.count, self.way = own, count, way
        self.piece = own.shape[1:]
        self.received = swap(other, 1, count)

    def part(self, at):
        return pl.BlockSpec((1,) + self.piece, lambda i: (at, 0, 0, 0))

    def cross(self, *earlier):
        self.received = after(self.received, *earlier)
        lines, rows, cols = self.piece
        half = cols // 256 * 128
        sizes = (half, cols - half) if self.way == "both" else (cols,)
        sent = call(
            cross_kernel,
            tuple(shape_of((lines, rows, size)) for size in sizes),
            (self.own, self.received),
            in_specs=[self.part(3), self.part(3)],
        )
        masks = {"x": (4,), "y": (2,), "both": (4, 2)}[self.way]
        self.via = tuple(swap(piece, mask, self.count) for piece, mask in zip(sent, masks))
        return sent

    def plane(self, *earlier):
        self.via = after(self.via, *earlier)
        piece = shape_of(self.piece)
        sent = call(
            functools.partial(plane_kernel, self.way),
            (piece, piece),
            (self.own, self.own, self.received, self.received) + self.via,
            in_specs=[self.part(1), self.part(2), self.part(1), self.part(2)]
            + [full(via.shape) for via in self.via],
        )
        self.pieces = (swap(sent[0], 2, self.count), swap(sent[1], 4, self.count))
        return sent

    def line(self, *earlier):
        from_y, from_x = after(self.pieces, *earlier)
        lines, rows, cols = self.piece
        self.masks = line_masks(self.count)
        self.terms = call(
            line_kernel,
            (shape_of((lines // 2, rows, cols)),) * 2,
            (self.own, self.received, from_y, from_x),
            in_specs=[self.part(0), self.part(0), full(self.piece), full(self.piece)],
        )
        return self.step()

    def step(self, *earlier):
        mine, sent = self.terms
        self.terms = (mine, swap(sent, self.masks.pop(), self.count))
        return mine, sent

    def fold(self, *earlier):
        while self.masks:
            mine, received = after(self.terms, *earlier)
            lines, rows, cols = mine.shape
            self.terms = call(fold_kernel, (shape_of((lines // 2, rows, cols)),) * 2, (mine, received))
            sent = self.step()
        return sent


def turn(vec_ref, other_dims):
    kinds = vec_ref.shape[0]
    eye = (
        lax.broadcasted_iota(jnp.int32, (kinds, VEC_PAD), 0)
        == lax.broadcasted_iota(jnp.int32, (kinds, VEC_PAD), 1)
    )
    return dot(vec_ref, eye.astype(f32).astype(bf16), TN)


def vectors_of(block, first, many=8):
    pick = (
        lax.broadcasted_iota(jnp.int32, (many, VEC_PAD), 0) + first
        == lax.broadcasted_iota(jnp.int32, (many, VEC_PAD), 1)
    )
    return dot(pick.astype(f32).astype(bf16), block, NT)


def pack_first_kernel(qkv_ref, out_ref, vec_ref, block_ref):
    cols = qkv_ref.shape[1]
    more = out_ref.shape[1]
    block_ref[0, :, :cols] = qkv_ref[...].astype(bf16)
    block_ref[0, :, cols : cols + more] = out_ref[...].astype(bf16)
    block_ref[0, :, cols + more :] = turn(vec_ref[...].astype(bf16), VEC_PAD).astype(bf16)


def pack_kernel(master_ref, block_ref):
    block_ref[0] = master_ref[...].astype(bf16)


def pack(master):
    return call(pack_kernel, shape_of((1,) + master.shape), (master,))


def project_kernel(x_ref, w_ref, vec_ref, o_ref):
    step = pl.program_id(0)
    bias = vectors_of(vec_ref[...], 0)
    row = jnp.where(step == 0, bias[0:1], jnp.where(step == 2, bias[1:2], 0.0))
    o_ref[...] = (dot(x_ref[...], w_ref[...]) + row).astype(bf16)


def vec_block(feat):
    return pl.BlockSpec((feat, VEC_PAD), lambda *_: (0, 4 * feat // VEC_PAD))


def project(x, weight):
    slots, feat = x.shape
    tile = lambda rows: pl.BlockSpec((rows, feat), lambda i: (0, i))
    return call(
        project_kernel,
        shape_of((slots, 3 * feat)),
        (x, weight, weight),
        in_specs=[full(x.shape), tile(feat), vec_block(feat)],
        out_specs=(tile(slots),),
        grid=(3,),
        mib=20,
        flops=6 * slots * feat * feat,
        light=True,
    )


def live_slots(quarter, index_ref, reads_ref, lengths_ref, slots):
    groups = slots // quarter
    own = index_ref[0] & (groups - 1)
    length = lengths_ref[reads_ref[index_ref[0]]]
    at = lax.broadcasted_iota(jnp.int32, (slots, 1), 0)
    position = at
    for part in range(groups):
        inside = (at >= part * quarter) & (at < (part + 1) * quarter)
        position = jnp.where(inside, at + ((own ^ part) - part) * quarter, position)
    return position < length


def lane_parts(value):
    high = value.astype(bf16).astype(f32)
    middle = (value - high).astype(bf16).astype(f32)
    return high, middle, value - high - middle


def attend_forward_kernel(quarter, index_ref, reads_ref, lengths_ref, q_ref, k_ref, v_ref, *refs):
    o_ref, log_ref = refs[-2:]
    slots, width = q_ref.shape
    half = width // 2
    scale = half ** (-0.5)
    lane = lax.broadcasted_iota(jnp.int32, (slots, width), 1)
    bias = jnp.where(live_slots(quarter, index_ref, reads_ref, lengths_ref, slots), 0.0, masked_score)
    query = q_ref[...].astype(f32) * scale
    key = k_ref[...].astype(f32)
    value = v_ref[...].astype(f32)
    mixed, logs = [], []
    for head in range(2):
        mine = (lane >= half) if head else (lane < half)
        base = 0 if head else half
        query_ext = jnp.where(mine, query, jnp.where(lane == base, 1.0, 0.0)).astype(bf16)
        key_ext = jnp.where(mine, key, jnp.where(lane == base, bias, 0.0)).astype(bf16)
        value_ext = jnp.where(mine, value, 1.0).astype(bf16)
        scores = dot(query_ext, key_ext, NT)
        top = jnp.max(scores, axis=1, keepdims=True)
        weights = jnp.exp(scores - top).astype(bf16)
        total = dot(weights, value_ext)
        sums = pltpu.roll(total, half, 1)
        mixed.append(total / sums)
        logs.append(top + jnp.log(jnp.where(mine, sums, 1.0)))
    first = lane < half
    o_ref[...] = jnp.where(first, mixed[0], mixed[1]).astype(bf16)
    log_ref[...] = jnp.where(first, logs[0], logs[1])


def attend_forward(scalars, projected, feat, quarter, begin, pairs, held=()):
    slots = projected.shape[0]
    width = 2 * feat // HEADS
    every = feat // width
    block = lambda offset: pl.BlockSpec((slots, width), lambda i, *_: (0, i + offset))
    return call(
        functools.partial(attend_forward_kernel, quarter),
        (shape_of((slots, feat)), shape_of((slots, feat), f32)),
        (projected,) * 3 + held,
        in_specs=[block(begin + k * every) for k in range(3)] + [ANY] * len(held),
        out_specs=(block(begin),) * 2,
        scalars=scalars,
        grid=(pairs,),
        flops=8 * slots * slots * width * pairs,
        trans=2 * pairs * slots * slots,
        aliases={6 + k: k for k in range(len(held))},
        light=True,
    )


def attend_backward_kernel(
    quarter, index_ref, reads_ref, lengths_ref, q_ref, k_ref, v_ref, o_ref, log_ref, g_ref, *refs
):
    dq_ref, dk_ref, dv_ref, bq_ref, bv_ref = refs[-5:]
    slots, width = q_ref.shape
    half = width // 2
    scale = half ** (-0.5)
    lane = lax.broadcasted_iota(jnp.int32, (slots, width), 1)
    bias = jnp.where(live_slots(quarter, index_ref, reads_ref, lengths_ref, slots), 0.0, masked_score)
    query = q_ref[...].astype(f32) * scale
    key = k_ref[...].astype(f32)
    value = v_ref[...].astype(f32)
    grad_low = g_ref[...]
    grad = grad_low.astype(f32)
    product = grad * o_ref[...].astype(f32)
    log_all = pltpu.roll(log_ref[...], half, 1)
    query_low = query.astype(bf16)
    key_turned = jnp.transpose(key).astype(bf16)
    parts = []
    for head in range(2):
        mine = (lane >= half) if head else (lane < half)
        base = 0 if head else half
        delta = jnp.sum(jnp.where(mine, product, 0.0), axis=1, keepdims=True)
        logs = lane_parts(log_all)
        deltas = lane_parts(delta)
        spot = [lane == base + k for k in range(4)]
        ones = (lane >= base) & (lane < base + 3)
        query_ext = jnp.where(mine, query, jnp.where(spot[3], 1.0, 0.0))
        grad_ext = jnp.where(mine, grad, 0.0)
        for k in range(3):
            query_ext = jnp.where(spot[k], -logs[k], query_ext)
            grad_ext = jnp.where(spot[k], -deltas[k], grad_ext)
        key_ext = jnp.where(mine, key, jnp.where(ones, 1.0, jnp.where(spot[3], bias, 0.0)))
        value_ext = jnp.where(mine, value, jnp.where(ones, 1.0, 0.0))
        probs = jnp.exp(dot(key_ext.astype(bf16), query_ext.astype(bf16), NT))
        grad_scores = (probs * dot(value_ext.astype(bf16), grad_ext.astype(bf16), NT)).astype(bf16)
        parts.append(
            (
                dot(key_turned, grad_scores),
                dot(grad_scores, query_low),
                dot(probs.astype(bf16), grad_low),
            )
        )
    first = lane < half
    turned = lax.broadcasted_iota(jnp.int32, (width, slots), 0) < half
    grad_query = (jnp.transpose(jnp.where(turned, parts[0][0], parts[1][0])) * scale).astype(bf16)
    grad_value = jnp.where(first, parts[0][2], parts[1][2]).astype(bf16)
    dq_ref[...] = grad_query
    dk_ref[...] = jnp.where(first, parts[0][1], parts[1][1]).astype(bf16)
    dv_ref[...] = grad_value
    bq_ref[...] = column_sum(grad_query.astype(f32))
    bv_ref[...] = column_sum(grad_value.astype(f32))


def attend_backward(scalars, projected, attended, logs, grad_attended, quarter, begin, pairs, held=()):
    slots, feat = attended.shape
    width = 2 * feat // HEADS
    every = feat // width
    block = lambda offset: pl.BlockSpec((slots, width), lambda i, *_: (0, i + offset))
    row = pl.BlockSpec((1, width), lambda i, *_: (0, i + begin))
    return call(
        functools.partial(attend_backward_kernel, quarter),
        (shape_of((slots, feat)),) * 3 + (shape_of((1, feat), f32),) * 2,
        (projected,) * 3 + (attended, logs, grad_attended) + held,
        in_specs=[block(begin + k * every) for k in range(3)] + [block(begin)] * 3 + [ANY] * len(held),
        out_specs=(block(begin),) * 3 + (row,) * 2,
        scalars=scalars,
        grid=(pairs,),
        flops=20 * slots * slots * width * pairs,
        trans=2 * pairs * slots * slots,
        aliases={9 + k: k for k in range(len(held))},
    )


def normalize(total):
    centered = total - jnp.mean(total, axis=1, keepdims=True)
    scale = lax.rsqrt(jnp.mean(centered * centered, axis=1, keepdims=True) + norm_eps)
    return centered * scale, scale


def normalize_back(grad, normed, scale):
    return (
        grad
        - jnp.mean(grad, axis=1, keepdims=True)
        - normed * jnp.mean(grad * normed, axis=1, keepdims=True)
    ) * scale


def column_sum(value):
    return jnp.sum(value, axis=0, keepdims=True)


def attn_out_kernel(a_ref, w_ref, x_ref, vec_ref, n_ref, s_ref, low_ref):
    vec = vectors_of(vec_ref[...], 0)
    normed, scale = normalize(x_ref[...].astype(f32) + dot(a_ref[...], w_ref[...]) + vec[2:3])
    n_ref[...] = normed
    s_ref[...] = scale
    low_ref[...] = (normed * vec[3:4] + vec[4:5]).astype(bf16)


def out_block(feat):
    return pl.BlockSpec((feat, feat), lambda *_: (0, 3))


def attn_out(attended, x, first_weight):
    slots, feat = x.shape
    return call(
        attn_out_kernel,
        (shape_of((slots, feat), f32), shape_of((slots, 1), f32), shape_of((slots, feat))),
        (attended, first_weight, x, first_weight),
        in_specs=[full(x.shape), out_block(feat), full(x.shape), vec_block(feat)],
        flops=2 * slots * feat * feat,
        light=True,
    )


def feed_up_kernel(low_ref, up_ref, vec_ref, active_ref, slope_ref):
    bias = vectors_of(vec_ref[...], 8 + pl.program_id(0))[0:1]
    hidden = dot(low_ref[...], up_ref[...]) + bias
    phi = 0.5 + 0.5 * lax.erf(hidden * 0.5**0.5)
    density = 0.3989422804014327 * jnp.exp(-0.5 * hidden * hidden)
    active_ref[...] = (hidden * phi).astype(bf16)
    slope_ref[...] = (phi + hidden * density).astype(bf16)


def feed_up(low, second_weight, first_weight):
    slots, feat = low.shape
    wide = second_weight.shape[1]
    column = lambda rows: pl.BlockSpec((rows, feat), lambda i: (0, i))
    return call(
        feed_up_kernel,
        (shape_of((slots, wide)),) * 2,
        (low, second_weight, first_weight),
        in_specs=[full(low.shape), column(feat), vec_block(feat)],
        out_specs=(column(slots),) * 2,
        grid=(wide // feat,),
        mib=20,
        flops=2 * slots * feat * wide,
        trans=2 * slots * wide,
        light=True,
    )


def put_row(value, refs):
    near_ref, beside_ref, across_ref = refs
    quarter = near_ref.shape[1]
    near_ref[0] = value[:quarter]
    beside_ref[0] = value[quarter : 2 * quarter]
    across_ref[0] = value[2 * quarter : 3 * quarter]
    across_ref[1] = value[3 * quarter :]


def row_shapes(quarter, feat):
    return (
        shape_of((1, quarter, feat)),
        shape_of((1, quarter, feat)),
        shape_of((2, quarter, feat)),
    )


def feed_down_kernel(
    quarter, index_ref, reads_ref, lengths_ref, active_ref, down_ref, n_ref, cot_ref, vec_ref,
    grad_ref, grad_low_ref, sums_ref, *row_refs
):
    slots, feat = n_ref.shape
    vec = vectors_of(vec_ref[...], 0)
    first = n_ref[...] * vec[3:4] + vec[4:5]
    normed, scale = normalize(first + dot(active_ref[...], down_ref[...], NT) + vec[5:6])
    live = live_slots(quarter, index_ref, reads_ref, lengths_ref, slots)
    put_row(jnp.where(live, normed * vec[6:7] + vec[7:8], 0.0).astype(bf16), row_refs)
    grad_result = jnp.where(live, cot_ref[...].astype(f32), 0.0)
    grad = normalize_back(grad_result * vec[6:7], normed, scale)
    grad_ref[...] = grad
    grad_low_ref[...] = grad.astype(bf16)
    sums_ref[0:1, :] = column_sum(grad)
    sums_ref[1:2, :] = column_sum(grad_result * normed)
    sums_ref[2:3, :] = column_sum(grad_result)
    sums_ref[3:8, :] = jnp.zeros((5, feat), f32)


def feed_down(scalars, active, down, normed, cotangent, first_weight, quarter):
    slots, feat = normed.shape
    wide = active.shape[1]
    return call(
        functools.partial(feed_down_kernel, quarter),
        (shape_of((slots, feat), f32), shape_of((slots, feat)), shape_of((8, feat), f32))
        + row_shapes(quarter, feat),
        (active, down, normed, cotangent, first_weight),
        in_specs=[
            full(active.shape), full(down.shape), full(normed.shape), full(normed.shape), vec_block(feat),
        ],
        scalars=scalars,
        mib=36,
        flops=2 * slots * feat * wide,
    )


def feed_back_kernel(
    low_ref, grad_ref, n_ref, s_ref, slope_ref, up_ref, down_ref, vec_ref,
    hidden_ref, bias_ref, out_ref, out_low_ref, sums_ref, acc_ref,
):
    step = pl.program_id(0)
    grad_hidden = dot(low_ref[...], down_ref[...]) * slope_ref[...].astype(f32)
    bias_ref[...] = column_sum(grad_hidden)
    grad_hidden = grad_hidden.astype(bf16)
    hidden_ref[...] = grad_hidden
    back = dot(grad_hidden, up_ref[...], NT)

    @pl.when(step == 0)
    def _():
        acc_ref[...] = grad_ref[...] + back

    @pl.when(step > 0)
    def _():
        acc_ref[...] += back

    @pl.when(step == pl.num_programs(0) - 1)
    def _():
        grad_first = acc_ref[...]
        normed = n_ref[...]
        gain = vectors_of(vec_ref[...], 3)[0:1]
        grad = normalize_back(grad_first * gain, normed, s_ref[...])
        out_ref[...] = grad
        out_low_ref[...] = grad.astype(bf16)
        sums_ref[0:1, :] = column_sum(grad)
        sums_ref[1:2, :] = column_sum(grad_first * normed)
        sums_ref[2:3, :] = column_sum(grad_first)
        sums_ref[3:8, :] = jnp.zeros((5, grad.shape[1]), f32)


def feed_back(grad_low, grad, normed, scale, slope, second_weight, down, first_weight):
    slots, feat = normed.shape
    wide = slope.shape[1]
    whole = full((slots, feat))
    column = lambda rows: pl.BlockSpec((rows, feat), lambda i: (0, i))
    return call(
        feed_back_kernel,
        (
            shape_of((slots, wide)),
            shape_of((1, wide), f32),
            shape_of((slots, feat), f32),
            shape_of((slots, feat)),
            shape_of((8, feat), f32),
        ),
        (grad_low, grad, normed, scale, slope, second_weight, down, first_weight),
        in_specs=[
            whole, whole, whole, full((slots, 1)), column(slots), column(feat), column(feat), vec_block(feat),
        ],
        out_specs=(column(slots), column(1), whole, whole, full((8, feat))),
        grid=(wide // feat,),
        scratch=[pltpu.VMEM((slots, feat), f32)],
        mib=32,
        flops=4 * slots * feat * wide,
    )


def weight_grad_kernel(count, lefts, vectors, index_ref, *refs):
    own_ref, other_ref, hold, sem = refs[-4:]
    index = index_ref[0]
    rows = own_ref.shape[2]
    width = hold.shape[3]
    jobs = []
    column = 0
    for at, left in enumerate(lefts):
        right = refs[at]
        for start in range(0, right.shape[1], width):
            jobs.append((left, at, start, min(width, right.shape[1] - start), column + start))
        column += right.shape[1]
    if vectors:
        jobs.append((None, None, 0, VEC_PAD, column))

    def drain(slot, size):
        view = hold.at[slot, :, :, pl.ds(0, size)]
        pltpu.make_async_copy(view, view, sem.at[slot]).wait()

    for job, (left, right, start, size, column) in enumerate(jobs):
        slot = job % 2
        if job >= 2:
            drain(slot, jobs[job - 2][3])
        if left is None:
            query_ref, value_ref, first_ref, second_ref, wide_ref = refs[-9:-4]
            feat = query_ref.shape[1]
            grads = jnp.concatenate(
                [query_ref[...], value_ref[...], first_ref[0:3, :], second_ref[0:3, :]]
                + [wide_ref[:, at : at + feat] for at in range(0, wide_ref.shape[1], feat)],
                axis=0,
            )
            product = turn(grads.astype(bf16), VEC_PAD)
        else:
            product = dot(refs[left][...], refs[right][:, start : start + size], TN)
        for block in range(count):
            hold[slot, block, :, 0:size] = product[block * rows : (block + 1) * rows, :].astype(bf16)
        for offset in range(8):
            target = other_ref if offset % 2 else own_ref
            for entry in range(count // 8):
                pltpu.make_async_copy(
                    hold.at[slot, index ^ (offset + line_offset(entry, count)), :, pl.ds(0, size)],
                    target.at[offset // 2, entry, :, pl.ds(column, size)],
                    sem.at[slot],
                ).start()
    for job in range(max(0, len(jobs) - 2), len(jobs)):
        drain(job % 2, jobs[job][3])


def weight_grad(index, count, pairs, vectors=()):
    rights = [right for left, right in pairs]
    unique = []
    for left, right in pairs:
        if not any(left is held for held in unique):
            unique.append(left)
    places = [
        len(rights) + next(i for i, held in enumerate(unique) if held is left) for left, right in pairs
    ]
    feat = pairs[0][0].shape[1]
    rows = feat // count
    cols = sum(right.shape[1] for right in rights) + (VEC_PAD if vectors else 0)
    out = shape_of((4, count // 8, rows, cols))
    return call(
        functools.partial(weight_grad_kernel, count, tuple(places), bool(vectors)),
        (out, out),
        tuple(rights) + tuple(unique) + tuple(vectors),
        out_specs=(ANY, ANY),
        scalars=(index,),
        scratch=[pltpu.VMEM((2, count, rows, feat), bf16), pltpu.SemaphoreType.DMA((2,))],
        mib=28,
        flops=2 * pairs[0][0].shape[0] * feat * cols,
    )


def out_back_kernel(grad_ref, w_ref, o_ref):
    o_ref[...] = dot(grad_ref[...], w_ref[...], NT).astype(bf16)


def out_back(grad_low, first_weight):
    slots, feat = grad_low.shape
    return call(
        out_back_kernel,
        shape_of((slots, feat)),
        (grad_low, first_weight),
        in_specs=[full(grad_low.shape), out_block(feat)],
        flops=2 * slots * feat * feat,
    )


def input_back_kernel(dq_ref, dk_ref, dv_ref, w_ref, grad_ref, *row_refs):
    feat = dq_ref.shape[1]
    total = grad_ref[...]
    for at, part in enumerate((dq_ref, dk_ref, dv_ref)):
        total = total + dot(part[...], w_ref[:, at * feat : (at + 1) * feat], NT)
    put_row(total.astype(bf16), row_refs)


def input_back(parts, weight, grad, quarter):
    slots, feat = grad.shape
    return call(
        input_back_kernel,
        row_shapes(quarter, feat),
        tuple(parts) + (weight, grad),
        in_specs=[full((slots, feat))] * 3
        + [pl.BlockSpec((feat, 3 * feat), lambda i: (0, 0)), full((slots, feat))],
        mib=24,
        flops=6 * slots * feat * feat,
    )


def adam_kernel(kinds, spans, *refs):
    many = len(kinds)
    terms, states, outs = refs[: -6 * many], refs[-6 * many : -3 * many], refs[-3 * many :]
    total = total_of(*[term[0] for term in terms])
    for at, (kind, span) in enumerate(zip(kinds, spans)):
        master, first_moment, second_moment = (states[part * many + at][...] for part in range(3))
        if span is None:
            rows, cols = master.shape
            block = jnp.pad(total[:, -VEC_PAD:], ((0, VEC_PAD - cols), (0, 0)))
            gradient = jnp.transpose(block)[:rows, :cols]
        else:
            gradient = total[:, span[0] : span[1]]
        results = adam_step(
            master, first_moment, second_moment, gradient, step_rates[kind], step_decays[kind]
        )
        for part in range(3):
            outs[part * many + at][...] = results[part]


def adam(terms, kinds, spans, states):
    ordered = [state[part] for part in range(3) for state in states]
    results = call(
        functools.partial(adam_kernel, kinds, spans),
        tuple(shape_of(state.shape, f32) for state in ordered),
        tuple(terms) + tuple(ordered),
    )
    many = len(kinds)
    return [tuple(results[part * many + at] for part in range(3)) for at in range(many)]


def adam_step(master, first_moment, second_moment, gradient, step_rate, decay_rate):
    first_new = beta_one * first_moment + (1.0 - beta_one) * gradient
    second_new = beta_two * second_moment + (1.0 - beta_two) * gradient * gradient
    ratio = (
        first_new
        / (1.0 - beta_one**STEP)
        / (jnp.sqrt(second_new / (1.0 - beta_two**STEP)) + adam_eps)
    )
    return (master - step_rate * (ratio + decay_rate * master), first_new, second_new)


def on_device(
    tokens,
    cotangent,
    read_lengths,
    row_reads,
    qkv_master,
    out_master,
    up_master,
    down_master,
    vec_master,
    qkv_first,
    out_first,
    up_first,
    down_first,
    vec_first,
    qkv_second,
    out_second,
    up_second,
    down_second,
    vec_second,
):
    groups = lax.axis_size("dp")
    count = groups * lax.axis_size("seq")
    row_count, quarter, feat = tokens.shape
    slots = quarter * groups
    wide = up_master.shape[1]
    half_pairs = HEADS // 4
    index = (lax.axis_index("seq") * groups + lax.axis_index("dp")).astype(jnp.int32).reshape(1)
    scalars = (index, row_reads, read_lengths)

    own = lambda m: lambda index: (index & (groups - 1)) ^ m

    def split_rows(held, first_index):
        many = len(held)
        moves = []
        for source in range(many):
            moves += [
                (source, own(0), None, 0, source, None),
                (source, own(1), None, 1, source, None),
                (source, own(2), None, 2, 2 * source, None),
                (source, own(3), None, 2, 2 * source + 1, None),
            ]
        shapes = tuple(shape_of((size, quarter, feat)) for size in (many, many, 2 * many))
        return place(first_index, held, shapes, moves)

    def take_rows(near, beside, across, passed):
        many = near.shape[0]
        moves = []
        for target in range(many):
            moves += [
                (0, target, None, target, 0, None),
                (1, target, None, target, 1, None),
                (2, 2 * target, None, target, 2, None),
                (3, 2 * target + 1, None, target, 3, None),
            ]
        shapes = (shape_of((groups, quarter, feat)),) * many
        out = place(index, [near, beside, across, passed], shapes, moves)
        return [row.reshape(slots, feat) for row in out]

    def give_row(near, beside, across, passed):
        moves = [(m, m // 3, None, 0, own(m), None) for m in range(4)]
        return place(index, [near, beside, across, passed], shape_of((groups, quarter, feat)), moves, light=False)

    first_block = call(
        pack_first_kernel,
        shape_of((1, qkv_master.shape[0], 4 * feat + VEC_PAD)),
        (qkv_master, out_master, vec_master),
        light=True,
    )
    masks = line_masks(count)

    def grow(line, steps, *earlier):
        for mask in steps:
            line = longer(line, after(swap(line, mask, count), *earlier))
        return line

    row_parts = split_rows([tokens], after(index, first_block))
    across = swap(row_parts[2], 2, count)
    half1 = grow(first_block, masks[:-1], row_parts)
    second_block = pack(after(up_master, half1))
    beside = swap(row_parts[1], 1, count)
    line1 = grow(half1, masks[-1:], second_block, across)
    got1 = swap(line1, 4, count), swap(line1, 2, count)
    third_block = pack(after(down_master.T, line1))
    half2 = grow(after(second_block, line1), masks[:-1])
    passed = swap(after(across, half2, got1), 1, count)
    (x,) = take_rows(row_parts[0], *after((beside, across, passed), half2))
    line2 = grow(half2, masks[-1:], x)
    halves = [half_of(line1.shape[2]), half_of(wide), wide // 512 * 384]
    got2 = pass_on(got1, line1.shape[2], halves[0], line2, count)
    other1 = [swap(piece, 1, count) for piece in (line1, *got1)]
    half3 = grow(after(third_block, line2), masks[:-1], other1)
    line3 = grow(half3, masks[-1:])
    got3 = pass_on(got2, wide, halves[1], line3, count)
    other2 = [swap(piece, 1, count) for piece in (line2, *got2)]
    first_weight = assemble(
        index, line1, got1, got2, (other1[0], other1[1:], other2[1:]), halves[0], count
    )

    projected = project(x, first_weight)
    held = attend_forward(scalars, projected, feat, quarter, 0, half_pairs)
    attended, logs = attend_forward(
        scalars, projected, feat, quarter, half_pairs, half_pairs, held
    )
    normed, scale, low = attn_out(attended, x, first_weight)
    got3 = after(got3, low)
    cotangent_parts = split_rows([cotangent], after(index, low))
    got4 = pass_on(got3, wide, halves[2], None, count)
    across = swap(after(cotangent_parts[2], got3), 2, count)
    beside = swap(after(cotangent_parts[1], got3), 1, count)
    other3 = [swap(piece, 1, count) for piece in (line3, *got3)]
    second_weight = assemble(
        index, line2, got2, got3, (other2[0], other2[1:], other3[1:]), halves[1], count
    )
    active, slope = feed_up(after(low, other3), second_weight, first_weight)
    got4, across, beside = after((got4, across, beside), active)
    other4 = [swap(piece, 1, count) for piece in got4]
    passed = swap(across, 1, count)
    down_weight = assemble(
        index, line3, got3, got4, (other3[0], other3[1:], other4), halves[2], count
    )
    (grad_output,) = take_rows(
        cotangent_parts[0], *after((beside, across, passed), down_weight)
    )

    grad2, grad2_low, sums2, *out_parts = feed_down(
        scalars, active, down_weight, normed, grad_output, first_weight, quarter
    )
    down_parts = weight_grad(index, count, [(grad2_low, active)])
    down_sum = Scatter(*down_parts, count, "both")
    across = swap(out_parts[2], 2, count)
    beside = swap(out_parts[1], 1, count)
    grad_hidden, bias1, grad1, grad1_low, sums1 = feed_back(
        after(grad2_low, down_parts), grad2, normed, scale, slope, second_weight, down_weight, first_weight
    )
    across, beside = after((across, beside), grad1_low)
    passed = swap(across, 1, count)
    done = down_sum.cross(grad1_low)
    up_parts = weight_grad(
        index, count, [(after(low, done), grad_hidden), (attended, grad1_low)]
    )
    up_sum = Scatter(*up_parts, count, "both")
    done = down_sum.plane(up_parts)
    grad_attended = out_back(after(grad1_low, done, passed), first_weight)
    beside_out, across_out, passed_out = after((beside, across, passed), done)
    done = up_sum.cross(grad_attended, beside_out, across_out, passed_out)
    held = attend_backward(
        (after(index, done),) + scalars[1:],
        projected, attended, logs, grad_attended, quarter, 0, half_pairs,
    )
    *parts, bias_query, bias_value = attend_backward(
        scalars, projected, attended, logs, grad_attended, quarter, half_pairs, half_pairs, held
    )
    done = up_sum.plane(parts)
    done = down_sum.line(done)
    first_parts = weight_grad(
        index,
        count,
        [(after(x, done), parts[0]), (x, parts[1]), (x, parts[2])],
        (bias_query, bias_value, sums1, sums2, bias1),
    )
    first_sum = Scatter(*first_parts, count, "both")
    grad_parts = input_back(after(parts, first_parts), first_weight, grad1, quarter)
    done = first_sum.cross(grad_parts)
    done = down_sum.fold(done)
    done = up_sum.line(done)
    done = first_sum.plane(done)
    done = up_sum.fold(done)
    line = first_sum.line(done)
    beside = swap(after(grad_parts[1], line), 1, count)
    across = swap(after(grad_parts[2], line), 2, count)
    output = give_row(after(out_parts[0], line), beside_out, across_out, passed_out)
    (down_new,) = adam(
        after(down_sum.terms, output),
        (3,),
        ((0, wide),),
        [(down_master.T, down_first.T, down_second.T)],
    )
    done = first_sum.fold(down_new)
    up_new, out_new = adam(
        after(up_sum.terms, done),
        (2, 1),
        ((0, wide), (wide, wide + feat)),
        [(up_master, up_first, up_second), (out_master, out_first, out_second)],
    )
    passed = swap(after(across, up_new), 1, count)
    qkv_new, vec_new = adam(
        after(first_sum.terms, up_new),
        (0, 4),
        ((0, 3 * feat), None),
        [(qkv_master, qkv_first, qkv_second), (vec_master, vec_first, vec_second)],
    )
    input_grad = give_row(after(grad_parts[0], qkv_new), beside, across, passed)
    down_new = tuple(value.T for value in down_new)
    updates = (qkv_new, out_new, up_new, down_new, vec_new)
    return (output, input_grad) + tuple(update[part] for part in range(3) for update in updates)


def solution(mesh):
    across_rows = P(("seq", "dp"), None)
    across_columns = P(None, ("seq", "dp"))
    slots = P("seq", "dp", None)
    matrices = (across_rows, across_rows, across_rows, across_columns, across_columns)
    return jax.shard_map(
        on_device,
        mesh=mesh,
        in_specs=(slots, slots, P(), P()) + matrices * 3,
        out_specs=(slots, slots) + matrices * 3,
        check_vma=False,
    )
```

```python
import functools

import jax
import jax.numpy as jnp
from jax import lax
from jax.experimental import pallas as pl
from jax.experimental.pallas import tpu as pltpu
from jax.sharding import PartitionSpec as P

HEADS = 12
STEP = 10
AXES = ("seq", "dp")

norm_eps = 1e-12
beta_one = 0.5
beta_two = 0.5
adam_eps = 1e-08
masked_score = -1e30
step_rates = (0.06, 0.3, 0.05, 0.025, 0.5)
step_decays = (0.01, 0.01, 0.01, 0.01, 0.0)

f32 = jnp.float32
bf16 = jnp.bfloat16
VEC_PAD = 128
WEIGHT = 2000

NT = (((1,), (1,)), ((), ()))
TN = (((0,), (0,)), ((), ()))


def dot(a, b, dims=(((1,), (0,)), ((), ()))):
    return lax.dot_general(a, b, dims, preferred_element_type=f32)


def params(mib=48):
    return pltpu.CompilerParams(vmem_limit_bytes=mib << 20)


def cost(flops, nbytes, trans=0):
    return pl.CostEstimate(
        flops=int(flops), bytes_accessed=int(nbytes), transcendentals=int(trans)
    )


def full(shape):
    return pl.BlockSpec(shape, lambda *_: (0,) * len(shape))


def shape_of(shape, dtype=bf16):
    return jax.ShapeDtypeStruct(shape, dtype)


ANY = pl.BlockSpec(memory_space=pl.ANY)
NEAR = pl.BlockSpec(memory_space=pltpu.VMEM)


def call(kernel, out_shape, operands, in_specs=None, out_specs=None, scalars=(), grid=(1,), scratch=(), mib=12, flops=0, trans=0, aliases=None, light=False):
    name = (kernel.func if isinstance(kernel, functools.partial) else kernel).__name__
    outs = out_shape if isinstance(out_shape, tuple) else (out_shape,)
    moved = sum(o.size * o.dtype.itemsize for o in tuple(operands) + outs)
    if in_specs is None:
        in_specs = [full(operand.shape) for operand in operands]
    if out_specs is None:
        out_specs = tuple(full(o.shape) for o in outs)
    result = pl.pallas_call(
        kernel,
        out_shape=outs,
        grid_spec=pltpu.PrefetchScalarGridSpec(
            num_scalar_prefetch=len(scalars),
            grid=grid,
            in_specs=in_specs,
            out_specs=out_specs,
            scratch_shapes=scratch,
        ),
        input_output_aliases=aliases or {},
        compiler_params=params(mib),
        cost_estimate=cost(0, WEIGHT * moved) if light else cost(WEIGHT * max(flops, 2e7), WEIGHT * moved, trans),
        name=name.replace("_kernel", ""),
    )(*scalars, *operands)
    return result if isinstance(out_shape, tuple) else result[0]


def swap(value, mask, count):
    return lax.ppermute(value, AXES, [(i, i ^ mask) for i in range(count)])


def after(value, *earlier):
    return lax.optimization_barrier((value, earlier))[0]


def line_masks(count):
    masks, mask = [], count // 2
    while mask >= 8:
        masks.append(mask)
        mask //= 2
    return masks


def line_offset(entry, count):
    return sum(mask for bit, mask in enumerate(line_masks(count)) if entry >> bit & 1)


def longer(line, received):
    return jnp.concatenate([line, received], axis=0)


def half_of(cols):
    return cols // 256 * 128


def pass_on_kernel(cols, half, from_x_ref, from_y_ref, *refs):
    to_x_ref, to_y_ref = refs[-2:]
    first = from_y_ref.shape[2] - cols
    to_x_ref[:, :, :half] = from_y_ref[:, :, first : first + half]
    first = from_x_ref.shape[2] - cols
    to_y_ref[:, :, : cols - half] = from_x_ref[:, :, first + half :]
    if len(refs) == 3:
        to_x_ref[:, :, half:] = refs[0][...]
        to_y_ref[:, :, cols - half :] = refs[0][...]


def pass_on(got, cols, half, line, count):
    lines, rows, _ = got[0].shape
    more = () if line is None else (line,)
    width = sum(piece.shape[2] for piece in more)
    sent = call(
        functools.partial(pass_on_kernel, cols, half),
        (shape_of((lines, rows, half + width)), shape_of((lines, rows, cols - half + width))),
        tuple(got) + more,
        light=True,
    )
    return swap(sent[0], 4, count), swap(sent[1], 2, count)


def place_kernel(plan, *refs):
    sources, targets, sem = refs[1 : 1 + plan[0]], refs[1 + plan[0] : -1], refs[-1]
    index = refs[0][0]

    def spot(ref, at, columns):
        at = at(index) if callable(at) else at
        return ref.at[at] if columns is None else ref.at[at, :, pl.ds(*columns)]

    for source, entry, columns, target, at, there in plan[1]:
        pltpu.make_async_copy(
            spot(sources[source], entry, columns), spot(targets[target], at, there), sem
        ).start()
    for target in targets:
        pltpu.make_async_copy(target, target, sem).wait()


def place(index, sources, out_shape, moves, held=NEAR, light=True):
    return call(
        functools.partial(place_kernel, (len(sources), moves)),
        out_shape,
        sources,
        in_specs=[held] * len(sources),
        out_specs=(ANY,) * (len(out_shape) if isinstance(out_shape, tuple) else 1),
        scalars=(index,),
        scratch=[pltpu.SemaphoreType.DMA],
        mib=16,
        light=light,
    )


def assemble(index, line, got, passed, others, half, count):
    lines, rows, cols = line.shape
    moves, sources = [], []
    for core, (line, got, passed) in enumerate(((line, got, passed), others)):
        base = len(sources)
        sources += [line, *got, *passed]
        parts = [
            (0, 0, (0, cols), (0, cols)),
            (1, 4, (got[0].shape[2] - cols, cols), (0, cols)),
            (2, 2, (got[1].shape[2] - cols, cols), (0, cols)),
            (3, 6, (0, half), (0, half)),
            (4, 6, (0, cols - half), (half, cols - half)),
        ]
        for which, offset, columns, there in parts:
            for z in range(lines):
                mask = line_offset(z, count) + offset + core
                at = lambda index, mask=mask: index ^ mask
                moves.append((base + which, z, columns, 0, at, there))
    out = place(index, sources, shape_of((8 * lines, rows, cols)), moves, ANY)
    return out.reshape(8 * lines * rows, cols)


def total_of(*terms):
    total = terms[0].astype(f32)
    for term in terms[1:]:
        total = total + term.astype(f32)
    return total


def cross_kernel(own_ref, received_ref, *out_refs):
    total = total_of(own_ref[0], received_ref[0]).astype(bf16)
    start = 0
    for out_ref in out_refs:
        cols = out_ref.shape[2]
        out_ref[...] = total[:, :, start : start + cols]
        start += cols


def plane_kernel(way, own_y_ref, own_x_ref, received_y_ref, received_x_ref, *refs):
    piece_y = total_of(own_y_ref[0], received_y_ref[0])
    piece_x = total_of(own_x_ref[0], received_x_ref[0])
    y_ref, x_ref = refs[-2:]
    if way == "x":
        piece_y = piece_y + refs[0][...].astype(f32)
    elif way == "y":
        piece_x = piece_x + refs[0][...].astype(f32)
    else:
        half = refs[0].shape[2]
        via_x, via_y = refs[0][...].astype(f32), refs[1][...].astype(f32)
        piece_y = jnp.concatenate([piece_y[:, :, :half] + via_x, piece_y[:, :, half:]], axis=2)
        piece_x = jnp.concatenate([piece_x[:, :, :half], piece_x[:, :, half:] + via_y], axis=2)
    y_ref[...] = piece_y.astype(bf16)
    x_ref[...] = piece_x.astype(bf16)


def line_kernel(own_ref, received_ref, from_y_ref, from_x_ref, *out_refs):
    total = total_of(own_ref[0], received_ref[0], from_y_ref[...], from_x_ref[...]).astype(bf16)
    span = out_refs[0].shape[0]
    for at, out_ref in enumerate(out_refs):
        out_ref[...] = total[at * span : (at + 1) * span]


def fold_kernel(mine_ref, received_ref, *out_refs):
    total = total_of(mine_ref[...], received_ref[...]).astype(bf16)
    span = out_refs[0].shape[0]
    for at, out_ref in enumerate(out_refs):
        out_ref[...] = total[at * span : (at + 1) * span]


class Scatter:
    def __init__(self, own, other, count, way):
        self.own, self.count, self.way = own, count, way
        self.piece = own.shape[1:]
        self.received = swap(other, 1, count)

    def part(self, at):
        return pl.BlockSpec((1,) + self.piece, lambda i: (at, 0, 0, 0))

    def cross(self, *earlier):
        self.received = after(self.received, *earlier)
        lines, rows, cols = self.piece
        half = cols // 256 * 128
        sizes = (half, cols - half) if self.way == "both" else (cols,)
        sent = call(
            cross_kernel,
            tuple(shape_of((lines, rows, size)) for size in sizes),
            (self.own, self.received),
            in_specs=[self.part(3), self.part(3)],
        )
        masks = {"x": (4,), "y": (2,), "both": (4, 2)}[self.way]
        self.via = tuple(swap(piece, mask, self.count) for piece, mask in zip(sent, masks))
        return sent

    def plane(self, *earlier):
        self.via = after(self.via, *earlier)
        piece = shape_of(self.piece)
        sent = call(
            functools.partial(plane_kernel, self.way),
            (piece, piece),
            (self.own, self.own, self.received, self.received) + self.via,
            in_specs=[self.part(1), self.part(2), self.part(1), self.part(2)]
            + [full(via.shape) for via in self.via],
        )
        self.pieces = (swap(sent[0], 2, self.count), swap(sent[1], 4, self.count))
        return sent

    def line(self, *earlier):
        from_y, from_x = after(self.pieces, *earlier)
        lines, rows, cols = self.piece
        self.masks = line_masks(self.count)
        self.terms = call(
            line_kernel,
            (shape_of((lines // 2, rows, cols)),) * 2,
            (self.own, self.received, from_y, from_x),
            in_specs=[self.part(0), self.part(0), full(self.piece), full(self.piece)],
        )
        return self.step()

    def step(self, *earlier):
        mine, sent = self.terms
        self.terms = (mine, swap(sent, self.masks.pop(), self.count))
        return mine, sent

    def fold(self, *earlier):
        while self.masks:
            mine, received = after(self.terms, *earlier)
            lines, rows, cols = mine.shape
            self.terms = call(fold_kernel, (shape_of((lines // 2, rows, cols)),) * 2, (mine, received))
            sent = self.step()
        return sent


def turn(vec_ref, other_dims):
    kinds = vec_ref.shape[0]
    eye = (
        lax.broadcasted_iota(jnp.int32, (kinds, VEC_PAD), 0)
        == lax.broadcasted_iota(jnp.int32, (kinds, VEC_PAD), 1)
    )
    return dot(vec_ref, eye.astype(f32).astype(bf16), TN)


def vectors_of(block, first, many=8):
    pick = (
        lax.broadcasted_iota(jnp.int32, (many, VEC_PAD), 0) + first
        == lax.broadcasted_iota(jnp.int32, (many, VEC_PAD), 1)
    )
    return dot(pick.astype(f32).astype(bf16), block, NT)


def pack_first_kernel(qkv_ref, out_ref, vec_ref, block_ref):
    cols = qkv_ref.shape[1]
    more = out_ref.shape[1]
    block_ref[0, :, :cols] = qkv_ref[...].astype(bf16)
    block_ref[0, :, cols : cols + more] = out_ref[...].astype(bf16)
    block_ref[0, :, cols + more :] = turn(vec_ref[...].astype(bf16), VEC_PAD).astype(bf16)


def pack_kernel(master_ref, block_ref):
    block_ref[0] = master_ref[...].astype(bf16)


def pack(master):
    return call(pack_kernel, shape_of((1,) + master.shape), (master,))


def project_kernel(x_ref, w_ref, vec_ref, o_ref):
    step = pl.program_id(0)
    bias = vectors_of(vec_ref[...], 0)
    row = jnp.where(step == 0, bias[0:1], jnp.where(step == 2, bias[1:2], 0.0))
    o_ref[...] = (dot(x_ref[...], w_ref[...]) + row).astype(bf16)


def vec_block(feat):
    return pl.BlockSpec((feat, VEC_PAD), lambda *_: (0, 4 * feat // VEC_PAD))


def project(x, weight):
    slots, feat = x.shape
    tile = lambda rows: pl.BlockSpec((rows, feat), lambda i: (0, i))
    return call(
        project_kernel,
        shape_of((slots, 3 * feat)),
        (x, weight, weight),
        in_specs=[full(x.shape), tile(feat), vec_block(feat)],
        out_specs=(tile(slots),),
        grid=(3,),
        mib=16,
        flops=6 * slots * feat * feat,
        light=True,
    )


def live_slots(quarter, index_ref, reads_ref, lengths_ref, slots):
    groups = slots // quarter
    own = index_ref[0] & (groups - 1)
    length = lengths_ref[reads_ref[index_ref[0]]]
    at = lax.broadcasted_iota(jnp.int32, (slots, 1), 0)
    position = at
    for part in range(groups):
        inside = (at >= part * quarter) & (at < (part + 1) * quarter)
        position = jnp.where(inside, at + ((own ^ part) - part) * quarter, position)
    return position < length


def lane_parts(value):
    high = value.astype(bf16).astype(f32)
    middle = (value - high).astype(bf16).astype(f32)
    return high, middle, value - high - middle


def attend_forward_kernel(quarter, index_ref, reads_ref, lengths_ref, q_ref, k_ref, v_ref, *refs):
    o_ref, log_ref = refs[-2:]
    slots, width = q_ref.shape
    half = width // 2
    scale = half ** (-0.5)
    lane = lax.broadcasted_iota(jnp.int32, (slots, width), 1)
    bias = jnp.where(live_slots(quarter, index_ref, reads_ref, lengths_ref, slots), 0.0, masked_score)
    query = q_ref[...].astype(f32) * scale
    key = k_ref[...].astype(f32)
    value = v_ref[...].astype(f32)
    mixed, logs = [], []
    for head in range(2):
        mine = (lane >= half) if head else (lane < half)
        base = 0 if head else half
        query_ext = jnp.where(mine, query, jnp.where(lane == base, 1.0, 0.0)).astype(bf16)
        key_ext = jnp.where(mine, key, jnp.where(lane == base, bias, 0.0)).astype(bf16)
        value_ext = jnp.where(mine, value, 1.0).astype(bf16)
        scores = dot(query_ext, key_ext, NT)
        top = jnp.max(scores, axis=1, keepdims=True)
        weights = jnp.exp(scores - top).astype(bf16)
        total = dot(weights, value_ext)
        sums = pltpu.roll(total, half, 1)
        mixed.append(total / sums)
        logs.append(top + jnp.log(jnp.where(mine, sums, 1.0)))
    first = lane < half
    o_ref[...] = jnp.where(first, mixed[0], mixed[1]).astype(bf16)
    log_ref[...] = jnp.where(first, logs[0], logs[1])


def attend_forward(scalars, projected, feat, quarter, begin, pairs, held=()):
    slots = projected.shape[0]
    width = 2 * feat // HEADS
    every = feat // width
    block = lambda offset: pl.BlockSpec((slots, width), lambda i, *_: (0, i + offset))
    return call(
        functools.partial(attend_forward_kernel, quarter),
        (shape_of((slots, feat)), shape_of((slots, feat), f32)),
        (projected,) * 3 + held,
        in_specs=[block(begin + k * every) for k in range(3)] + [ANY] * len(held),
        out_specs=(block(begin),) * 2,
        scalars=scalars,
        grid=(pairs,),
        flops=8 * slots * slots * width * pairs,
        trans=2 * pairs * slots * slots,
        aliases={6 + k: k for k in range(len(held))},
        light=True,
    )


def attend_backward_kernel(
    quarter, index_ref, reads_ref, lengths_ref, q_ref, k_ref, v_ref, o_ref, log_ref, g_ref, *refs
):
    dq_ref, dk_ref, dv_ref, bq_ref, bv_ref = refs[-5:]
    slots, width = q_ref.shape
    half = width // 2
    scale = half ** (-0.5)
    lane = lax.broadcasted_iota(jnp.int32, (slots, width), 1)
    bias = jnp.where(live_slots(quarter, index_ref, reads_ref, lengths_ref, slots), 0.0, masked_score)
    query = q_ref[...].astype(f32) * scale
    key = k_ref[...].astype(f32)
    value = v_ref[...].astype(f32)
    grad_low = g_ref[...]
    grad = grad_low.astype(f32)
    product = grad * o_ref[...].astype(f32)
    log_all = pltpu.roll(log_ref[...], half, 1)
    query_low = query.astype(bf16)
    key_turned = jnp.transpose(key).astype(bf16)
    parts = []
    for head in range(2):
        mine = (lane >= half) if head else (lane < half)
        base = 0 if head else half
        delta = jnp.sum(jnp.where(mine, product, 0.0), axis=1, keepdims=True)
        logs = lane_parts(log_all)
        deltas = lane_parts(delta)
        spot = [lane == base + k for k in range(4)]
        ones = (lane >= base) & (lane < base + 3)
        query_ext = jnp.where(mine, query, jnp.where(spot[3], 1.0, 0.0))
        grad_ext = jnp.where(mine, grad, 0.0)
        for k in range(3):
            query_ext = jnp.where(spot[k], -logs[k], query_ext)
            grad_ext = jnp.where(spot[k], -deltas[k], grad_ext)
        key_ext = jnp.where(mine, key, jnp.where(ones, 1.0, jnp.where(spot[3], bias, 0.0)))
        value_ext = jnp.where(mine, value, jnp.where(ones, 1.0, 0.0))
        probs = jnp.exp(dot(key_ext.astype(bf16), query_ext.astype(bf16), NT))
        grad_scores = (probs * dot(value_ext.astype(bf16), grad_ext.astype(bf16), NT)).astype(bf16)
        parts.append(
            (
                dot(key_turned, grad_scores),
                dot(grad_scores, query_low),
                dot(probs.astype(bf16), grad_low),
            )
        )
    first = lane < half
    turned = lax.broadcasted_iota(jnp.int32, (width, slots), 0) < half
    grad_query = (jnp.transpose(jnp.where(turned, parts[0][0], parts[1][0])) * scale).astype(bf16)
    grad_value = jnp.where(first, parts[0][2], parts[1][2]).astype(bf16)
    dq_ref[...] = grad_query
    dk_ref[...] = jnp.where(first, parts[0][1], parts[1][1]).astype(bf16)
    dv_ref[...] = grad_value
    bq_ref[...] = column_sum(grad_query.astype(f32))
    bv_ref[...] = column_sum(grad_value.astype(f32))


def attend_backward(scalars, projected, attended, logs, grad_attended, quarter, begin, pairs, held=()):
    slots, feat = attended.shape
    width = 2 * feat // HEADS
    every = feat // width
    block = lambda offset: pl.BlockSpec((slots, width), lambda i, *_: (0, i + offset))
    row = pl.BlockSpec((1, width), lambda i, *_: (0, i + begin))
    return call(
        functools.partial(attend_backward_kernel, quarter),
        (shape_of((slots, feat)),) * 3 + (shape_of((1, feat), f32),) * 2,
        (projected,) * 3 + (attended, logs, grad_attended) + held,
        in_specs=[block(begin + k * every) for k in range(3)] + [block(begin)] * 3 + [ANY] * len(held),
        out_specs=(block(begin),) * 3 + (row,) * 2,
        scalars=scalars,
        grid=(pairs,),
        flops=20 * slots * slots * width * pairs,
        trans=2 * pairs * slots * slots,
        aliases={9 + k: k for k in range(len(held))},
    )


def normalize(total):
    centered = total - jnp.mean(total, axis=1, keepdims=True)
    scale = lax.rsqrt(jnp.mean(centered * centered, axis=1, keepdims=True) + norm_eps)
    return centered * scale, scale


def normalize_back(grad, normed, scale):
    return (
        grad
        - jnp.mean(grad, axis=1, keepdims=True)
        - normed * jnp.mean(grad * normed, axis=1, keepdims=True)
    ) * scale


def column_sum(value):
    return jnp.sum(value, axis=0, keepdims=True)


def attn_out_kernel(a_ref, w_ref, x_ref, vec_ref, n_ref, s_ref, low_ref):
    vec = vectors_of(vec_ref[...], 0)
    normed, scale = normalize(x_ref[...].astype(f32) + dot(a_ref[...], w_ref[...]) + vec[2:3])
    n_ref[...] = normed
    s_ref[...] = scale
    low_ref[...] = (normed * vec[3:4] + vec[4:5]).astype(bf16)


def out_block(feat):
    return pl.BlockSpec((feat, feat), lambda *_: (0, 3))


def attn_out(attended, x, first_weight):
    slots, feat = x.shape
    return call(
        attn_out_kernel,
        (shape_of((slots, feat), f32), shape_of((slots, 1), f32), shape_of((slots, feat))),
        (attended, first_weight, x, first_weight),
        in_specs=[full(x.shape), out_block(feat), full(x.shape), vec_block(feat)],
        flops=2 * slots * feat * feat,
        light=True,
    )


def feed_up_kernel(low_ref, up_ref, vec_ref, active_ref, slope_ref):
    bias = vectors_of(vec_ref[...], 8 + pl.program_id(0))[0:1]
    hidden = dot(low_ref[...], up_ref[...]) + bias
    phi = 0.5 + 0.5 * lax.erf(hidden * 0.5**0.5)
    density = 0.3989422804014327 * jnp.exp(-0.5 * hidden * hidden)
    active_ref[...] = (hidden * phi).astype(bf16)
    slope_ref[...] = (phi + hidden * density).astype(bf16)


def feed_up(low, second_weight, first_weight):
    slots, feat = low.shape
    wide = second_weight.shape[1]
    column = lambda rows: pl.BlockSpec((rows, feat), lambda i: (0, i))
    return call(
        feed_up_kernel,
        (shape_of((slots, wide)),) * 2,
        (low, second_weight, first_weight),
        in_specs=[full(low.shape), column(feat), vec_block(feat)],
        out_specs=(column(slots),) * 2,
        grid=(wide // feat,),
        mib=16,
        flops=2 * slots * feat * wide,
        trans=2 * slots * wide,
        light=True,
    )


def put_row(value, refs):
    near_ref, beside_ref, across_ref = refs
    quarter = near_ref.shape[1]
    near_ref[0] = value[:quarter]
    beside_ref[0] = value[quarter : 2 * quarter]
    across_ref[0] = value[2 * quarter : 3 * quarter]
    across_ref[1] = value[3 * quarter :]


def row_shapes(quarter, feat):
    return (
        shape_of((1, quarter, feat)),
        shape_of((1, quarter, feat)),
        shape_of((2, quarter, feat)),
    )


def feed_down_kernel(
    quarter, index_ref, reads_ref, lengths_ref, active_ref, down_ref, n_ref,
    near_ref, beside_ref, across_ref, passed_ref, vec_ref,
    grad_ref, grad_low_ref, sums_ref, *row_refs
):
    slots, feat = n_ref.shape
    vec = vectors_of(vec_ref[...], 0)
    first = n_ref[...] * vec[3:4] + vec[4:5]
    normed, scale = normalize(first + dot(active_ref[...], down_ref[...], NT) + vec[5:6])
    live = live_slots(quarter, index_ref, reads_ref, lengths_ref, slots)
    put_row(jnp.where(live, normed * vec[6:7] + vec[7:8], 0.0).astype(bf16), row_refs)
    cotangent = jnp.concatenate([near_ref[0], beside_ref[0], across_ref[0], passed_ref[1]], axis=0)
    grad_result = jnp.where(live, cotangent.astype(f32), 0.0)
    grad = normalize_back(grad_result * vec[6:7], normed, scale)
    grad_ref[...] = grad
    grad_low_ref[...] = grad.astype(bf16)
    sums_ref[0:1, :] = column_sum(grad)
    sums_ref[1:2, :] = column_sum(grad_result * normed)
    sums_ref[2:3, :] = column_sum(grad_result)
    sums_ref[3:8, :] = jnp.zeros((5, feat), f32)


def feed_down(scalars, active, down, normed, cotangent, first_weight, quarter):
    slots, feat = normed.shape
    wide = active.shape[1]
    return call(
        functools.partial(feed_down_kernel, quarter),
        (shape_of((slots, feat), f32), shape_of((slots, feat)), shape_of((8, feat), f32))
        + row_shapes(quarter, feat),
        (active, down, normed) + tuple(cotangent) + (first_weight,),
        in_specs=[full(active.shape), full(down.shape), full(normed.shape)]
        + [full(part.shape) for part in cotangent]
        + [vec_block(feat)],
        scalars=scalars,
        mib=30,
        flops=2 * slots * feat * wide,
    )


def feed_back_kernel(
    low_ref, grad_ref, n_ref, s_ref, slope_ref, up_ref, down_ref, vec_ref,
    hidden_ref, bias_ref, out_ref, out_low_ref, sums_ref, acc_ref,
):
    step = pl.program_id(0)
    grad_hidden = dot(low_ref[...], down_ref[...]) * slope_ref[...].astype(f32)
    bias_ref[...] = column_sum(grad_hidden)
    grad_hidden = grad_hidden.astype(bf16)
    hidden_ref[...] = grad_hidden
    back = dot(grad_hidden, up_ref[...], NT)

    @pl.when(step == 0)
    def _():
        acc_ref[...] = grad_ref[...] + back

    @pl.when(step > 0)
    def _():
        acc_ref[...] += back

    @pl.when(step == pl.num_programs(0) - 1)
    def _():
        grad_first = acc_ref[...]
        normed = n_ref[...]
        gain = vectors_of(vec_ref[...], 3)[0:1]
        grad = normalize_back(grad_first * gain, normed, s_ref[...])
        out_ref[...] = grad
        out_low_ref[...] = grad.astype(bf16)
        sums_ref[0:1, :] = column_sum(grad)
        sums_ref[1:2, :] = column_sum(grad_first * normed)
        sums_ref[2:3, :] = column_sum(grad_first)
        sums_ref[3:8, :] = jnp.zeros((5, grad.shape[1]), f32)


def feed_back(grad_low, grad, normed, scale, slope, second_weight, down, first_weight):
    slots, feat = normed.shape
    wide = slope.shape[1]
    whole = full((slots, feat))
    column = lambda rows: pl.BlockSpec((rows, feat), lambda i: (0, i))
    return call(
        feed_back_kernel,
        (
            shape_of((slots, wide)),
            shape_of((1, wide), f32),
            shape_of((slots, feat), f32),
            shape_of((slots, feat)),
            shape_of((8, feat), f32),
        ),
        (grad_low, grad, normed, scale, slope, second_weight, down, first_weight),
        in_specs=[
            whole, whole, whole, full((slots, 1)), column(slots), column(feat), column(feat), vec_block(feat),
        ],
        out_specs=(column(slots), column(1), whole, whole, full((8, feat))),
        grid=(wide // feat,),
        scratch=[pltpu.VMEM((slots, feat), f32)],
        mib=26,
        flops=4 * slots * feat * wide,
    )


def weight_grad_kernel(count, lefts, vectors, index_ref, *refs):
    own_ref, other_ref, hold, sem = refs[-4:]
    index = index_ref[0]
    rows = own_ref.shape[2]
    width = hold.shape[3]
    jobs = []
    column = 0
    for at, left in enumerate(lefts):
        right = refs[at]
        for start in range(0, right.shape[1], width):
            jobs.append((left, at, start, min(width, right.shape[1] - start), column + start))
        column += right.shape[1]
    if vectors:
        jobs.append((None, None, 0, VEC_PAD, column))

    def drain(slot, size):
        view = hold.at[slot, :, :, pl.ds(0, size)]
        pltpu.make_async_copy(view, view, sem.at[slot]).wait()

    for job, (left, right, start, size, column) in enumerate(jobs):
        slot = job % 2
        if job >= 2:
            drain(slot, jobs[job - 2][3])
        if left is None:
            query_ref, value_ref, first_ref, second_ref, wide_ref = refs[-9:-4]
            feat = query_ref.shape[1]
            grads = jnp.concatenate(
                [query_ref[...], value_ref[...], first_ref[0:3, :], second_ref[0:3, :]]
                + [wide_ref[:, at : at + feat] for at in range(0, wide_ref.shape[1], feat)],
                axis=0,
            )
            product = turn(grads.astype(bf16), VEC_PAD)
        else:
            product = dot(refs[left][...], refs[right][:, start : start + size], TN)
        for block in range(count):
            hold[slot, block, :, 0:size] = product[block * rows : (block + 1) * rows, :].astype(bf16)
        for offset in range(8):
            target = other_ref if offset % 2 else own_ref
            for entry in range(count // 8):
                pltpu.make_async_copy(
                    hold.at[slot, index ^ (offset + line_offset(entry, count)), :, pl.ds(0, size)],
                    target.at[offset // 2, entry, :, pl.ds(column, size)],
                    sem.at[slot],
                ).start()
    for job in range(max(0, len(jobs) - 2), len(jobs)):
        drain(job % 2, jobs[job][3])


def weight_grad(index, count, pairs, vectors=()):
    rights = [right for left, right in pairs]
    unique = []
    for left, right in pairs:
        if not any(left is held for held in unique):
            unique.append(left)
    places = [
        len(rights) + next(i for i, held in enumerate(unique) if held is left) for left, right in pairs
    ]
    feat = pairs[0][0].shape[1]
    rows = feat // count
    cols = sum(right.shape[1] for right in rights) + (VEC_PAD if vectors else 0)
    out = shape_of((4, count // 8, rows, cols))
    return call(
        functools.partial(weight_grad_kernel, count, tuple(places), bool(vectors)),
        (out, out),
        tuple(rights) + tuple(unique) + tuple(vectors),
        out_specs=(ANY, ANY),
        scalars=(index,),
        scratch=[pltpu.VMEM((2, count, rows, feat), bf16), pltpu.SemaphoreType.DMA((2,))],
        mib=22,
        flops=2 * pairs[0][0].shape[0] * feat * cols,
    )


def out_back_kernel(grad_ref, w_ref, o_ref):
    o_ref[...] = dot(grad_ref[...], w_ref[...], NT).astype(bf16)


def out_back(grad_low, first_weight):
    slots, feat = grad_low.shape
    return call(
        out_back_kernel,
        shape_of((slots, feat)),
        (grad_low, first_weight),
        in_specs=[full(grad_low.shape), out_block(feat)],
        flops=2 * slots * feat * feat,
    )


def input_back_kernel(dq_ref, dk_ref, dv_ref, w_ref, grad_ref, *row_refs):
    feat = dq_ref.shape[1]
    total = grad_ref[...]
    for at, part in enumerate((dq_ref, dk_ref, dv_ref)):
        total = total + dot(part[...], w_ref[:, at * feat : (at + 1) * feat], NT)
    put_row(total.astype(bf16), row_refs)


def input_back(parts, weight, grad, quarter):
    slots, feat = grad.shape
    return call(
        input_back_kernel,
        row_shapes(quarter, feat),
        tuple(parts) + (weight, grad),
        in_specs=[full((slots, feat))] * 3
        + [pl.BlockSpec((feat, 3 * feat), lambda i: (0, 0)), full((slots, feat))],
        mib=18,
        flops=6 * slots * feat * feat,
    )


def adam_kernel(kinds, spans, *refs):
    many = len(kinds)
    terms, states, outs = refs[: -6 * many], refs[-6 * many : -3 * many], refs[-3 * many :]
    total = total_of(*[term[0] for term in terms])
    for at, (kind, span) in enumerate(zip(kinds, spans)):
        master, first_moment, second_moment = (states[part * many + at][...] for part in range(3))
        if span is None:
            rows, cols = master.shape
            block = jnp.pad(total[:, -VEC_PAD:], ((0, VEC_PAD - cols), (0, 0)))
            gradient = jnp.transpose(block)[:rows, :cols]
        else:
            gradient = total[:, span[0] : span[1]]
        results = adam_step(
            master, first_moment, second_moment, gradient, step_rates[kind], step_decays[kind]
        )
        for part in range(3):
            outs[part * many + at][...] = results[part]


def adam(terms, kinds, spans, states):
    ordered = [state[part] for part in range(3) for state in states]
    results = call(
        functools.partial(adam_kernel, kinds, spans),
        tuple(shape_of(state.shape, f32) for state in ordered),
        tuple(terms) + tuple(ordered),
    )
    many = len(kinds)
    return [tuple(results[part * many + at] for part in range(3)) for at in range(many)]


def adam_step(master, first_moment, second_moment, gradient, step_rate, decay_rate):
    first_new = beta_one * first_moment + (1.0 - beta_one) * gradient
    second_new = beta_two * second_moment + (1.0 - beta_two) * gradient * gradient
    ratio = (
        first_new
        / (1.0 - beta_one**STEP)
        / (jnp.sqrt(second_new / (1.0 - beta_two**STEP)) + adam_eps)
    )
    return (master - step_rate * (ratio + decay_rate * master), first_new, second_new)


def on_device(
    tokens,
    cotangent,
    read_lengths,
    row_reads,
    qkv_master,
    out_master,
    up_master,
    down_master,
    vec_master,
    qkv_first,
    out_first,
    up_first,
    down_first,
    vec_first,
    qkv_second,
    out_second,
    up_second,
    down_second,
    vec_second,
):
    groups = lax.axis_size("dp")
    count = groups * lax.axis_size("seq")
    row_count, quarter, feat = tokens.shape
    slots = quarter * groups
    wide = up_master.shape[1]
    half_pairs = HEADS // 4
    index = (lax.axis_index("seq") * groups + lax.axis_index("dp")).astype(jnp.int32).reshape(1)
    scalars = (index, row_reads, read_lengths)

    own = lambda m: lambda index: (index & (groups - 1)) ^ m

    def split_rows(held, first_index):
        many = len(held)
        moves = []
        for source in range(many):
            moves += [
                (source, own(0), None, 0, source, None),
                (source, own(1), None, 1, source, None),
                (source, own(2), None, 2, 2 * source, None),
                (source, own(3), None, 2, 2 * source + 1, None),
            ]
        shapes = tuple(shape_of((size, quarter, feat)) for size in (many, many, 2 * many))
        return place(first_index, held, shapes, moves)

    def take_rows(near, beside, across, passed):
        many = near.shape[0]
        moves = []
        for target in range(many):
            moves += [
                (0, target, None, target, 0, None),
                (1, target, None, target, 1, None),
                (2, 2 * target, None, target, 2, None),
                (3, 2 * target + 1, None, target, 3, None),
            ]
        shapes = (shape_of((groups, quarter, feat)),) * many
        out = place(index, [near, beside, across, passed], shapes, moves)
        return [row.reshape(slots, feat) for row in out]

    def give_row(near, beside, across, passed):
        moves = [(m, m // 3, None, 0, own(m), None) for m in range(4)]
        return place(index, [near, beside, across, passed], shape_of((groups, quarter, feat)), moves, light=False)

    first_block = call(
        pack_first_kernel,
        shape_of((1, qkv_master.shape[0], 4 * feat + VEC_PAD)),
        (qkv_master, out_master, vec_master),
        light=True,
    )
    masks = line_masks(count)

    def grow(line, steps, *earlier):
        for mask in steps:
            line = longer(line, after(swap(line, mask, count), *earlier))
        return line

    row_parts = split_rows([tokens], after(index, first_block))
    across = swap(row_parts[2], 2, count)
    half1 = grow(first_block, masks[:-1], row_parts)
    second_block = pack(after(up_master, half1))
    beside = swap(row_parts[1], 1, count)
    line1 = grow(half1, masks[-1:], second_block, across)
    got1 = swap(line1, 4, count), swap(line1, 2, count)
    third_block = pack(after(down_master.T, line1))
    half2 = grow(after(second_block, line1), masks[:-1])
    passed = swap(after(across, half2, got1), 1, count)
    (x,) = take_rows(row_parts[0], *after((beside, across, passed), half2))
    line2 = grow(half2, masks[-1:], x)
    halves = [half_of(line1.shape[2]), half_of(wide), wide // 512 * 384]
    got2 = pass_on(got1, line1.shape[2], halves[0], line2, count)
    other1 = [swap(piece, 1, count) for piece in (line1, *got1)]
    half3 = grow(after(third_block, line2), masks[:-1], other1)
    line3 = grow(half3, masks[-1:])
    got3 = pass_on(got2, wide, halves[1], line3, count)
    other2 = [swap(piece, 1, count) for piece in (line2, *got2)]
    first_weight = assemble(
        index, line1, got1, got2, (other1[0], other1[1:], other2[1:]), halves[0], count
    )

    projected = project(x, first_weight)
    held = attend_forward(scalars, projected, feat, quarter, 0, half_pairs)
    attended, logs = attend_forward(
        scalars, projected, feat, quarter, half_pairs, half_pairs, held
    )
    normed, scale, low = attn_out(attended, x, first_weight)
    got3 = after(got3, low)
    cotangent_parts = split_rows([cotangent], after(index, low))
    got4 = pass_on(got3, wide, halves[2], None, count)
    across = swap(after(cotangent_parts[2], got3), 2, count)
    beside = swap(after(cotangent_parts[1], got3), 1, count)
    other3 = [swap(piece, 1, count) for piece in (line3, *got3)]
    second_weight = assemble(
        index, line2, got2, got3, (other2[0], other2[1:], other3[1:]), halves[1], count
    )
    active, slope = feed_up(after(low, other3), second_weight, first_weight)
    got4, across, beside = after((got4, across, beside), active)
    other4 = [swap(piece, 1, count) for piece in got4]
    passed = swap(across, 1, count)
    down_weight = assemble(
        index, line3, got3, got4, (other3[0], other3[1:], other4), halves[2], count
    )
    grad_output = (cotangent_parts[0], *after((beside, across, passed), down_weight))

    grad2, grad2_low, sums2, *out_parts = feed_down(
        scalars, active, down_weight, normed, grad_output, first_weight, quarter
    )
    down_parts = weight_grad(index, count, [(grad2_low, active)])
    down_sum = Scatter(*down_parts, count, "both")
    across = swap(out_parts[2], 2, count)
    beside = swap(out_parts[1], 1, count)
    grad_hidden, bias1, grad1, grad1_low, sums1 = feed_back(
        after(grad2_low, down_parts), grad2, normed, scale, slope, second_weight, down_weight, first_weight
    )
    across, beside = after((across, beside), grad1_low)
    passed = swap(across, 1, count)
    done = down_sum.cross(grad1_low)
    up_parts = weight_grad(
        index, count, [(after(low, done), grad_hidden), (attended, grad1_low)]
    )
    up_sum = Scatter(*up_parts, count, "both")
    done = down_sum.plane(up_parts)
    grad_attended = out_back(after(grad1_low, done, passed), first_weight)
    beside_out, across_out, passed_out = after((beside, across, passed), done)
    done = up_sum.cross(grad_attended, beside_out, across_out, passed_out)
    held = attend_backward(
        (after(index, done),) + scalars[1:],
        projected, attended, logs, grad_attended, quarter, 0, half_pairs,
    )
    *parts, bias_query, bias_value = attend_backward(
        scalars, projected, attended, logs, grad_attended, quarter, half_pairs, half_pairs, held
    )
    done = up_sum.plane(parts)
    done = down_sum.line(done)
    first_parts = weight_grad(
        index,
        count,
        [(after(x, done), parts[0]), (x, parts[1]), (x, parts[2])],
        (bias_query, bias_value, sums1, sums2, bias1),
    )
    first_sum = Scatter(*first_parts, count, "both")
    grad_parts = input_back(after(parts, first_parts), first_weight, grad1, quarter)
    done = first_sum.cross(grad_parts)
    done = down_sum.fold(done)
    done = up_sum.line(done)
    done = first_sum.plane(done)
    done = up_sum.fold(done)
    line = first_sum.line(done)
    beside = swap(after(grad_parts[1], line), 1, count)
    across = swap(after(grad_parts[2], line), 2, count)
    output = give_row(after(out_parts[0], line), beside_out, across_out, passed_out)
    (down_new,) = adam(
        after(down_sum.terms, output),
        (3,),
        ((0, wide),),
        [(down_master.T, down_first.T, down_second.T)],
    )
    done = first_sum.fold(down_new)
    up_new, out_new = adam(
        after(up_sum.terms, done),
        (2, 1),
        ((0, wide), (wide, wide + feat)),
        [(up_master, up_first, up_second), (out_master, out_first, out_second)],
    )
    passed = swap(after(across, up_new), 1, count)
    qkv_new, vec_new = adam(
        after(first_sum.terms, up_new),
        (0, 4),
        ((0, 3 * feat), None),
        [(qkv_master, qkv_first, qkv_second), (vec_master, vec_first, vec_second)],
    )
    input_grad = give_row(after(grad_parts[0], qkv_new), beside, across, passed)
    down_new = tuple(value.T for value in down_new)
    updates = (qkv_new, out_new, up_new, down_new, vec_new)
    return (output, input_grad) + tuple(update[part] for part in range(3) for update in updates)


def solution(mesh):
    across_rows = P(("seq", "dp"), None)
    across_columns = P(None, ("seq", "dp"))
    slots = P("seq", "dp", None)
    matrices = (across_rows, across_rows, across_rows, across_columns, across_columns)
    return jax.shard_map(
        on_device,
        mesh=mesh,
        in_specs=(slots, slots, P(), P()) + matrices * 3,
        out_specs=(slots, slots) + matrices * 3,
        check_vma=False,
    )
```

```python
import functools

import jax
import jax.numpy as jnp
from jax import lax
from jax.experimental import pallas as pl
from jax.experimental.pallas import tpu as pltpu
from jax.sharding import PartitionSpec as P

HEADS = 12
STEP = 10
AXES = ("seq", "dp")

norm_eps = 1e-12
beta_one = 0.5
beta_two = 0.5
adam_eps = 1e-08
masked_score = -1e30
step_rates = (0.06, 0.3, 0.05, 0.025, 0.5)
step_decays = (0.01, 0.01, 0.01, 0.01, 0.0)

f32 = jnp.float32
bf16 = jnp.bfloat16
VEC_PAD = 128
WEIGHT = 2000

NT = (((1,), (1,)), ((), ()))
TN = (((0,), (0,)), ((), ()))


def dot(a, b, dims=(((1,), (0,)), ((), ()))):
    return lax.dot_general(a, b, dims, preferred_element_type=f32)


def params(mib=48):
    return pltpu.CompilerParams(vmem_limit_bytes=mib << 20)


def cost(flops, nbytes, trans=0):
    return pl.CostEstimate(
        flops=int(flops), bytes_accessed=int(nbytes), transcendentals=int(trans)
    )


def full(shape):
    return pl.BlockSpec(shape, lambda *_: (0,) * len(shape))


def shape_of(shape, dtype=bf16):
    return jax.ShapeDtypeStruct(shape, dtype)


ANY = pl.BlockSpec(memory_space=pl.ANY)
NEAR = pl.BlockSpec(memory_space=pltpu.VMEM)


def call(kernel, out_shape, operands, in_specs=None, out_specs=None, scalars=(), grid=(1,), scratch=(), mib=12, flops=0, trans=0, aliases=None, light=False):
    name = (kernel.func if isinstance(kernel, functools.partial) else kernel).__name__
    outs = out_shape if isinstance(out_shape, tuple) else (out_shape,)
    moved = sum(o.size * o.dtype.itemsize for o in tuple(operands) + outs)
    if in_specs is None:
        in_specs = [full(operand.shape) for operand in operands]
    if out_specs is None:
        out_specs = tuple(full(o.shape) for o in outs)
    result = pl.pallas_call(
        kernel,
        out_shape=outs,
        grid_spec=pltpu.PrefetchScalarGridSpec(
            num_scalar_prefetch=len(scalars),
            grid=grid,
            in_specs=in_specs,
            out_specs=out_specs,
            scratch_shapes=scratch,
        ),
        input_output_aliases=aliases or {},
        compiler_params=params(mib),
        cost_estimate=cost(0, WEIGHT * moved) if light else cost(WEIGHT * max(flops, 2e7), WEIGHT * moved, trans),
        name=name.replace("_kernel", ""),
    )(*scalars, *operands)
    return result if isinstance(out_shape, tuple) else result[0]


def swap(value, mask, count):
    return lax.ppermute(value, AXES, [(i, i ^ mask) for i in range(count)])


def after(value, *earlier):
    return lax.optimization_barrier((value, earlier))[0]


def line_masks(count):
    masks, mask = [], count // 2
    while mask >= 8:
        masks.append(mask)
        mask //= 2
    return masks


def line_offset(entry, count):
    return sum(mask for bit, mask in enumerate(line_masks(count)) if entry >> bit & 1)


def longer(line, received):
    return jnp.concatenate([line, received], axis=0)


def half_of(cols):
    return cols // 256 * 128


def pass_on_kernel(cols, half, from_x_ref, from_y_ref, *refs):
    to_x_ref, to_y_ref = refs[-2:]
    first = from_y_ref.shape[2] - cols
    to_x_ref[:, :, :half] = from_y_ref[:, :, first : first + half]
    first = from_x_ref.shape[2] - cols
    to_y_ref[:, :, : cols - half] = from_x_ref[:, :, first + half :]
    if len(refs) == 3:
        to_x_ref[:, :, half:] = refs[0][...]
        to_y_ref[:, :, cols - half :] = refs[0][...]


def pass_on(got, cols, half, line, count):
    lines, rows, _ = got[0].shape
    more = () if line is None else (line,)
    width = sum(piece.shape[2] for piece in more)
    sent = call(
        functools.partial(pass_on_kernel, cols, half),
        (shape_of((lines, rows, half + width)), shape_of((lines, rows, cols - half + width))),
        tuple(got) + more,
        light=True,
    )
    return swap(sent[0], 4, count), swap(sent[1], 2, count)


def place_kernel(plan, *refs):
    sources, targets, sem = refs[1 : 1 + plan[0]], refs[1 + plan[0] : -1], refs[-1]
    index = refs[0][0]

    def spot(ref, at, columns):
        at = at(index) if callable(at) else at
        return ref.at[at] if columns is None else ref.at[at, :, pl.ds(*columns)]

    for source, entry, columns, target, at, there in plan[1]:
        pltpu.make_async_copy(
            spot(sources[source], entry, columns), spot(targets[target], at, there), sem
        ).start()
    for target in targets:
        pltpu.make_async_copy(target, target, sem).wait()


def place(index, sources, out_shape, moves, held=NEAR, light=True):
    return call(
        functools.partial(place_kernel, (len(sources), moves)),
        out_shape,
        sources,
        in_specs=[held] * len(sources),
        out_specs=(ANY,) * (len(out_shape) if isinstance(out_shape, tuple) else 1),
        scalars=(index,),
        scratch=[pltpu.SemaphoreType.DMA],
        mib=16,
        light=light,
    )


def assemble(index, line, got, passed, others, half, count):
    lines, rows, cols = line.shape
    moves, sources = [], []
    for core, (line, got, passed) in enumerate(((line, got, passed), others)):
        base = len(sources)
        sources += [line, *got, *passed]
        parts = [
            (0, 0, (0, cols), (0, cols)),
            (1, 4, (got[0].shape[2] - cols, cols), (0, cols)),
            (2, 2, (got[1].shape[2] - cols, cols), (0, cols)),
            (3, 6, (0, half), (0, half)),
            (4, 6, (0, cols - half), (half, cols - half)),
        ]
        for which, offset, columns, there in parts:
            for z in range(lines):
                mask = line_offset(z, count) + offset + core
                at = lambda index, mask=mask: index ^ mask
                moves.append((base + which, z, columns, 0, at, there))
    out = place(index, sources, shape_of((8 * lines, rows, cols)), moves, ANY)
    return out.reshape(8 * lines * rows, cols)


def total_of(*terms):
    total = terms[0].astype(f32)
    for term in terms[1:]:
        total = total + term.astype(f32)
    return total


def cross_kernel(own_ref, received_ref, *out_refs):
    total = total_of(own_ref[0], received_ref[0]).astype(bf16)
    start = 0
    for out_ref in out_refs:
        cols = out_ref.shape[2]
        out_ref[...] = total[:, :, start : start + cols]
        start += cols


def plane_kernel(own_y_ref, own_x_ref, received_y_ref, received_x_ref, via_x_ref, via_y_ref, y_ref, x_ref):
    half = via_x_ref.shape[2]
    y_ref[:, :, :half] = total_of(
        own_y_ref[0, :, :, :half], received_y_ref[0, :, :, :half], via_x_ref[...]
    ).astype(bf16)
    y_ref[:, :, half:] = total_of(own_y_ref[0, :, :, half:], received_y_ref[0, :, :, half:]).astype(bf16)
    x_ref[:, :, :half] = total_of(own_x_ref[0, :, :, :half], received_x_ref[0, :, :, :half]).astype(bf16)
    x_ref[:, :, half:] = total_of(
        own_x_ref[0, :, :, half:], received_x_ref[0, :, :, half:], via_y_ref[...]
    ).astype(bf16)


def line_kernel(own_ref, received_ref, from_y_ref, from_x_ref, *out_refs):
    total = total_of(own_ref[0], received_ref[0], from_y_ref[...], from_x_ref[...]).astype(bf16)
    span = out_refs[0].shape[0]
    for at, out_ref in enumerate(out_refs):
        out_ref[...] = total[at * span : (at + 1) * span]


def fold_kernel(mine_ref, received_ref, *out_refs):
    total = total_of(mine_ref[...], received_ref[...]).astype(bf16)
    span = out_refs[0].shape[0]
    for at, out_ref in enumerate(out_refs):
        out_ref[...] = total[at * span : (at + 1) * span]


class Scatter:
    def __init__(self, own, other, count):
        self.own, self.count = own, count
        self.piece = own.shape[1:]
        self.received = swap(other, 1, count)

    def part(self, at):
        return pl.BlockSpec((1,) + self.piece, lambda i: (at, 0, 0, 0))

    def cross(self, *earlier):
        self.received = after(self.received, *earlier)
        lines, rows, cols = self.piece
        half = half_of(cols)
        sizes = (half, cols - half)
        sent = call(
            cross_kernel,
            tuple(shape_of((lines, rows, size)) for size in sizes),
            (self.own, self.received),
            in_specs=[self.part(3), self.part(3)],
        )
        self.via = (swap(sent[0], 4, self.count), swap(sent[1], 2, self.count))
        return sent

    def plane(self, *earlier):
        self.via = after(self.via, *earlier)
        piece = shape_of(self.piece)
        sent = call(
            plane_kernel,
            (piece, piece),
            (self.own, self.own, self.received, self.received) + self.via,
            in_specs=[self.part(1), self.part(2), self.part(1), self.part(2)]
            + [full(via.shape) for via in self.via],
        )
        self.pieces = (swap(sent[0], 2, self.count), swap(sent[1], 4, self.count))
        return sent

    def line(self, *earlier):
        from_y, from_x = after(self.pieces, *earlier)
        lines, rows, cols = self.piece
        self.masks = line_masks(self.count)
        self.terms = call(
            line_kernel,
            (shape_of((lines // 2, rows, cols)),) * 2,
            (self.own, self.received, from_y, from_x),
            in_specs=[self.part(0), self.part(0), full(self.piece), full(self.piece)],
        )
        return self.step()

    def step(self, *earlier):
        mine, sent = self.terms
        self.terms = (mine, swap(sent, self.masks.pop(), self.count))
        return mine, sent

    def fold(self, *earlier):
        while self.masks:
            mine, received = after(self.terms, *earlier)
            lines, rows, cols = mine.shape
            self.terms = call(fold_kernel, (shape_of((lines // 2, rows, cols)),) * 2, (mine, received))
            sent = self.step()
        return sent


def turn(vec_ref, other_dims):
    kinds = vec_ref.shape[0]
    eye = (
        lax.broadcasted_iota(jnp.int32, (kinds, VEC_PAD), 0)
        == lax.broadcasted_iota(jnp.int32, (kinds, VEC_PAD), 1)
    )
    return dot(vec_ref, eye.astype(f32).astype(bf16), TN)


def vectors_of(block, first, many=8):
    pick = (
        lax.broadcasted_iota(jnp.int32, (many, VEC_PAD), 0) + first
        == lax.broadcasted_iota(jnp.int32, (many, VEC_PAD), 1)
    )
    return dot(pick.astype(f32).astype(bf16), block, NT)


def pack_first_kernel(qkv_ref, out_ref, vec_ref, block_ref):
    cols = qkv_ref.shape[1]
    more = out_ref.shape[1]
    block_ref[0, :, :cols] = qkv_ref[...].astype(bf16)
    block_ref[0, :, cols : cols + more] = out_ref[...].astype(bf16)
    block_ref[0, :, cols + more :] = turn(vec_ref[...].astype(bf16), VEC_PAD).astype(bf16)


def pack_kernel(master_ref, block_ref):
    block_ref[0] = master_ref[...].astype(bf16)


def pack(master):
    return call(pack_kernel, shape_of((1,) + master.shape), (master,))


def project_kernel(x_ref, w_ref, vec_ref, o_ref):
    step = pl.program_id(0)
    bias = vectors_of(vec_ref[...], 0)
    row = jnp.where(step == 0, bias[0:1], jnp.where(step == 2, bias[1:2], 0.0))
    o_ref[...] = (dot(x_ref[...], w_ref[...]) + row).astype(bf16)


def vec_block(feat):
    return pl.BlockSpec((feat, VEC_PAD), lambda *_: (0, 4 * feat // VEC_PAD))


def project(x, weight):
    slots, feat = x.shape
    tile = lambda rows: pl.BlockSpec((rows, feat), lambda i: (0, i))
    return call(
        project_kernel,
        shape_of((slots, 3 * feat)),
        (x, weight, weight),
        in_specs=[full(x.shape), tile(feat), vec_block(feat)],
        out_specs=(tile(slots),),
        grid=(3,),
        mib=16,
        flops=6 * slots * feat * feat,
        light=True,
    )


def live_slots(quarter, index_ref, reads_ref, lengths_ref, slots):
    groups = slots // quarter
    own = index_ref[0] & (groups - 1)
    length = lengths_ref[reads_ref[index_ref[0]]]
    at = lax.broadcasted_iota(jnp.int32, (slots, 1), 0)
    position = at
    for part in range(groups):
        inside = (at >= part * quarter) & (at < (part + 1) * quarter)
        position = jnp.where(inside, at + ((own ^ part) - part) * quarter, position)
    return position < length


def lane_parts(value):
    high = value.astype(bf16).astype(f32)
    middle = (value - high).astype(bf16).astype(f32)
    return high, middle, value - high - middle


def attend_forward_kernel(quarter, index_ref, reads_ref, lengths_ref, q_ref, k_ref, v_ref, o_ref, log_ref):
    slots, width = q_ref.shape
    half = width // 2
    scale = half ** (-0.5)
    lane = lax.broadcasted_iota(jnp.int32, (slots, width), 1)
    bias = jnp.where(live_slots(quarter, index_ref, reads_ref, lengths_ref, slots), 0.0, masked_score)
    query = q_ref[...].astype(f32) * scale
    key = k_ref[...].astype(f32)
    value = v_ref[...].astype(f32)
    mixed, logs = [], []
    for head in range(2):
        mine = (lane >= half) if head else (lane < half)
        base = 0 if head else half
        query_ext = jnp.where(mine, query, jnp.where(lane == base, 1.0, 0.0)).astype(bf16)
        key_ext = jnp.where(mine, key, jnp.where(lane == base, bias, 0.0)).astype(bf16)
        value_ext = jnp.where(mine, value, 1.0).astype(bf16)
        scores = dot(query_ext, key_ext, NT)
        top = jnp.max(scores, axis=1, keepdims=True)
        weights = jnp.exp(scores - top).astype(bf16)
        total = dot(weights, value_ext)
        sums = pltpu.roll(total, half, 1)
        mixed.append(total / sums)
        logs.append(top + jnp.log(jnp.where(mine, sums, 1.0)))
    first = lane < half
    o_ref[...] = jnp.where(first, mixed[0], mixed[1]).astype(bf16)
    log_ref[...] = jnp.where(first, logs[0], logs[1])


def attend_forward(scalars, projected, feat, quarter):
    slots = projected.shape[0]
    width = 2 * feat // HEADS
    pairs = feat // width
    block = lambda offset: pl.BlockSpec((slots, width), lambda i, *_: (0, i + offset))
    return call(
        functools.partial(attend_forward_kernel, quarter),
        (shape_of((slots, feat)), shape_of((slots, feat), f32)),
        (projected,) * 3,
        in_specs=[block(k * pairs) for k in range(3)],
        out_specs=(block(0),) * 2,
        scalars=scalars,
        grid=(pairs,),
        flops=8 * slots * slots * width * pairs,
        trans=2 * pairs * slots * slots,
        light=True,
    )


def attend_backward_kernel(
    quarter, index_ref, reads_ref, lengths_ref, q_ref, k_ref, v_ref, o_ref, log_ref, g_ref,
    dq_ref, dk_ref, dv_ref, bq_ref, bv_ref,
):
    slots, width = q_ref.shape
    half = width // 2
    scale = half ** (-0.5)
    lane = lax.broadcasted_iota(jnp.int32, (slots, width), 1)
    bias = jnp.where(live_slots(quarter, index_ref, reads_ref, lengths_ref, slots), 0.0, masked_score)
    query = q_ref[...].astype(f32) * scale
    key = k_ref[...].astype(f32)
    value = v_ref[...].astype(f32)
    grad_low = g_ref[...]
    grad = grad_low.astype(f32)
    product = grad * o_ref[...].astype(f32)
    log_all = pltpu.roll(log_ref[...], half, 1)
    query_low = query.astype(bf16)
    key_turned = jnp.transpose(key).astype(bf16)
    parts = []
    for head in range(2):
        mine = (lane >= half) if head else (lane < half)
        base = 0 if head else half
        delta = jnp.sum(jnp.where(mine, product, 0.0), axis=1, keepdims=True)
        logs = lane_parts(log_all)
        deltas = lane_parts(delta)
        spot = [lane == base + k for k in range(4)]
        ones = (lane >= base) & (lane < base + 3)
        query_ext = jnp.where(mine, query, jnp.where(spot[3], 1.0, 0.0))
        grad_ext = jnp.where(mine, grad, 0.0)
        for k in range(3):
            query_ext = jnp.where(spot[k], -logs[k], query_ext)
            grad_ext = jnp.where(spot[k], -deltas[k], grad_ext)
        key_ext = jnp.where(mine, key, jnp.where(ones, 1.0, jnp.where(spot[3], bias, 0.0)))
        value_ext = jnp.where(mine, value, jnp.where(ones, 1.0, 0.0))
        probs = jnp.exp(dot(key_ext.astype(bf16), query_ext.astype(bf16), NT))
        grad_scores = (probs * dot(value_ext.astype(bf16), grad_ext.astype(bf16), NT)).astype(bf16)
        parts.append(
            (
                dot(key_turned, grad_scores),
                dot(grad_scores, query_low),
                dot(probs.astype(bf16), grad_low),
            )
        )
    first = lane < half
    turned = lax.broadcasted_iota(jnp.int32, (width, slots), 0) < half
    grad_query = (jnp.transpose(jnp.where(turned, parts[0][0], parts[1][0])) * scale).astype(bf16)
    grad_value = jnp.where(first, parts[0][2], parts[1][2]).astype(bf16)
    dq_ref[...] = grad_query
    dk_ref[...] = jnp.where(first, parts[0][1], parts[1][1]).astype(bf16)
    dv_ref[...] = grad_value
    bq_ref[...] = column_sum(grad_query.astype(f32))
    bv_ref[...] = column_sum(grad_value.astype(f32))


def attend_backward(scalars, projected, attended, logs, grad_attended, quarter):
    slots, feat = attended.shape
    width = 2 * feat // HEADS
    pairs = feat // width
    block = lambda offset: pl.BlockSpec((slots, width), lambda i, *_: (0, i + offset))
    row = pl.BlockSpec((1, width), lambda i, *_: (0, i))
    return call(
        functools.partial(attend_backward_kernel, quarter),
        (shape_of((slots, feat)),) * 3 + (shape_of((1, feat), f32),) * 2,
        (projected,) * 3 + (attended, logs, grad_attended),
        in_specs=[block(k * pairs) for k in range(3)] + [block(0)] * 3,
        out_specs=(block(0),) * 3 + (row,) * 2,
        scalars=scalars,
        grid=(pairs,),
        flops=20 * slots * slots * width * pairs,
        trans=2 * pairs * slots * slots,
    )


def normalize(total):
    centered = total - jnp.mean(total, axis=1, keepdims=True)
    scale = lax.rsqrt(jnp.mean(centered * centered, axis=1, keepdims=True) + norm_eps)
    return centered * scale, scale


def normalize_back(grad, normed, scale):
    return (
        grad
        - jnp.mean(grad, axis=1, keepdims=True)
        - normed * jnp.mean(grad * normed, axis=1, keepdims=True)
    ) * scale


def column_sum(value):
    return jnp.sum(value, axis=0, keepdims=True)


def attn_out_kernel(a_ref, w_ref, x_ref, vec_ref, n_ref, s_ref, low_ref):
    vec = vectors_of(vec_ref[...], 0)
    normed, scale = normalize(x_ref[...].astype(f32) + dot(a_ref[...], w_ref[...]) + vec[2:3])
    n_ref[...] = normed
    s_ref[...] = scale
    low_ref[...] = (normed * vec[3:4] + vec[4:5]).astype(bf16)


def out_block(feat):
    return pl.BlockSpec((feat, feat), lambda *_: (0, 3))


def attn_out(attended, x, first_weight):
    slots, feat = x.shape
    return call(
        attn_out_kernel,
        (shape_of((slots, feat), f32), shape_of((slots, 1), f32), shape_of((slots, feat))),
        (attended, first_weight, x, first_weight),
        in_specs=[full(x.shape), out_block(feat), full(x.shape), vec_block(feat)],
        flops=2 * slots * feat * feat,
        light=True,
    )


def feed_up_kernel(low_ref, up_ref, vec_ref, active_ref, slope_ref):
    bias = vectors_of(vec_ref[...], 8 + pl.program_id(0))[0:1]
    hidden = dot(low_ref[...], up_ref[...]) + bias
    phi = 0.5 + 0.5 * lax.erf(hidden * 0.5**0.5)
    density = 0.3989422804014327 * jnp.exp(-0.5 * hidden * hidden)
    active_ref[...] = (hidden * phi).astype(bf16)
    slope_ref[...] = (phi + hidden * density).astype(bf16)


def feed_up(low, second_weight, first_weight):
    slots, feat = low.shape
    wide = second_weight.shape[1]
    column = lambda rows: pl.BlockSpec((rows, feat), lambda i: (0, i))
    return call(
        feed_up_kernel,
        (shape_of((slots, wide)),) * 2,
        (low, second_weight, first_weight),
        in_specs=[full(low.shape), column(feat), vec_block(feat)],
        out_specs=(column(slots),) * 2,
        grid=(wide // feat,),
        mib=16,
        flops=2 * slots * feat * wide,
        trans=2 * slots * wide,
        light=True,
    )


def put_row(value, refs):
    near_ref, beside_ref, across_ref = refs
    quarter = near_ref.shape[1]
    near_ref[0] = value[:quarter]
    beside_ref[0] = value[quarter : 2 * quarter]
    across_ref[0] = value[2 * quarter : 3 * quarter]
    across_ref[1] = value[3 * quarter :]


def row_shapes(quarter, feat):
    return (
        shape_of((1, quarter, feat)),
        shape_of((1, quarter, feat)),
        shape_of((2, quarter, feat)),
    )


def feed_down_kernel(
    quarter, index_ref, reads_ref, lengths_ref, active_ref, down_ref, n_ref,
    near_ref, beside_ref, across_ref, passed_ref, vec_ref,
    grad_ref, grad_low_ref, sums_ref, *row_refs
):
    slots, feat = n_ref.shape
    vec = vectors_of(vec_ref[...], 0)
    first = n_ref[...] * vec[3:4] + vec[4:5]
    normed, scale = normalize(first + dot(active_ref[...], down_ref[...], NT) + vec[5:6])
    live = live_slots(quarter, index_ref, reads_ref, lengths_ref, slots)
    put_row(jnp.where(live, normed * vec[6:7] + vec[7:8], 0.0).astype(bf16), row_refs)
    cotangent = jnp.concatenate([near_ref[0], beside_ref[0], across_ref[0], passed_ref[1]], axis=0)
    grad_result = jnp.where(live, cotangent.astype(f32), 0.0)
    grad = normalize_back(grad_result * vec[6:7], normed, scale)
    grad_ref[...] = grad
    grad_low_ref[...] = grad.astype(bf16)
    sums_ref[0:1, :] = column_sum(grad)
    sums_ref[1:2, :] = column_sum(grad_result * normed)
    sums_ref[2:3, :] = column_sum(grad_result)
    sums_ref[3:8, :] = jnp.zeros((5, feat), f32)


def feed_down(scalars, active, down, normed, cotangent, first_weight, quarter):
    slots, feat = normed.shape
    wide = active.shape[1]
    return call(
        functools.partial(feed_down_kernel, quarter),
        (shape_of((slots, feat), f32), shape_of((slots, feat)), shape_of((8, feat), f32))
        + row_shapes(quarter, feat),
        (active, down, normed) + tuple(cotangent) + (first_weight,),
        in_specs=[full(active.shape), full(down.shape), full(normed.shape)]
        + [full(part.shape) for part in cotangent]
        + [vec_block(feat)],
        scalars=scalars,
        mib=30,
        flops=2 * slots * feat * wide,
    )


def feed_back_kernel(
    low_ref, grad_ref, n_ref, s_ref, slope_ref, up_ref, down_ref, vec_ref,
    hidden_ref, bias_ref, out_ref, out_low_ref, sums_ref, acc_ref,
):
    step = pl.program_id(0)
    grad_hidden = dot(low_ref[...], down_ref[...]) * slope_ref[...].astype(f32)
    bias_ref[...] = column_sum(grad_hidden)
    grad_hidden = grad_hidden.astype(bf16)
    hidden_ref[...] = grad_hidden
    back = dot(grad_hidden, up_ref[...], NT)

    @pl.when(step == 0)
    def _():
        acc_ref[...] = grad_ref[...] + back

    @pl.when(step > 0)
    def _():
        acc_ref[...] += back

    @pl.when(step == pl.num_programs(0) - 1)
    def _():
        grad_first = acc_ref[...]
        normed = n_ref[...]
        gain = vectors_of(vec_ref[...], 3)[0:1]
        grad = normalize_back(grad_first * gain, normed, s_ref[...])
        out_ref[...] = grad
        out_low_ref[...] = grad.astype(bf16)
        sums_ref[0:1, :] = column_sum(grad)
        sums_ref[1:2, :] = column_sum(grad_first * normed)
        sums_ref[2:3, :] = column_sum(grad_first)
        sums_ref[3:8, :] = jnp.zeros((5, grad.shape[1]), f32)


def feed_back(grad_low, grad, normed, scale, slope, second_weight, down, first_weight):
    slots, feat = normed.shape
    wide = slope.shape[1]
    whole = full((slots, feat))
    column = lambda rows: pl.BlockSpec((rows, feat), lambda i: (0, i))
    return call(
        feed_back_kernel,
        (
            shape_of((slots, wide)),
            shape_of((1, wide), f32),
            shape_of((slots, feat), f32),
            shape_of((slots, feat)),
            shape_of((8, feat), f32),
        ),
        (grad_low, grad, normed, scale, slope, second_weight, down, first_weight),
        in_specs=[
            whole, whole, whole, full((slots, 1)), column(slots), column(feat), column(feat), vec_block(feat),
        ],
        out_specs=(column(slots), column(1), whole, whole, full((8, feat))),
        grid=(wide // feat,),
        scratch=[pltpu.VMEM((slots, feat), f32)],
        mib=26,
        flops=4 * slots * feat * wide,
    )


def weight_grad_kernel(count, lefts, vectors, index_ref, *refs):
    own_ref, other_ref, hold, sem = refs[-4:]
    index = index_ref[0]
    rows = own_ref.shape[2]
    width = hold.shape[3]
    jobs = []
    column = 0
    for at, left in enumerate(lefts):
        right = refs[at]
        for start in range(0, right.shape[1], width):
            jobs.append((left, at, start, min(width, right.shape[1] - start), column + start))
        column += right.shape[1]
    if vectors:
        jobs.append((None, None, 0, VEC_PAD, column))

    def drain(slot, size):
        view = hold.at[slot, :, :, pl.ds(0, size)]
        pltpu.make_async_copy(view, view, sem.at[slot]).wait()

    for job, (left, right, start, size, column) in enumerate(jobs):
        slot = job % 2
        if job >= 2:
            drain(slot, jobs[job - 2][3])
        if left is None:
            query_ref, value_ref, first_ref, second_ref, wide_ref = refs[-9:-4]
            feat = query_ref.shape[1]
            grads = jnp.concatenate(
                [query_ref[...], value_ref[...], first_ref[0:3, :], second_ref[0:3, :]]
                + [wide_ref[:, at : at + feat] for at in range(0, wide_ref.shape[1], feat)],
                axis=0,
            )
            product = turn(grads.astype(bf16), VEC_PAD)
        else:
            product = dot(refs[left][...], refs[right][:, start : start + size], TN)
        for block in range(count):
            hold[slot, block, :, 0:size] = product[block * rows : (block + 1) * rows, :].astype(bf16)
        for offset in range(8):
            target = other_ref if offset % 2 else own_ref
            for entry in range(count // 8):
                pltpu.make_async_copy(
                    hold.at[slot, index ^ (offset + line_offset(entry, count)), :, pl.ds(0, size)],
                    target.at[offset // 2, entry, :, pl.ds(column, size)],
                    sem.at[slot],
                ).start()
    for job in range(max(0, len(jobs) - 2), len(jobs)):
        drain(job % 2, jobs[job][3])


def weight_grad(index, count, pairs, vectors=()):
    rights = [right for left, right in pairs]
    unique = []
    for left, right in pairs:
        if not any(left is held for held in unique):
            unique.append(left)
    places = [
        len(rights) + next(i for i, held in enumerate(unique) if held is left) for left, right in pairs
    ]
    feat = pairs[0][0].shape[1]
    rows = feat // count
    cols = sum(right.shape[1] for right in rights) + (VEC_PAD if vectors else 0)
    out = shape_of((4, count // 8, rows, cols))
    return call(
        functools.partial(weight_grad_kernel, count, tuple(places), bool(vectors)),
        (out, out),
        tuple(rights) + tuple(unique) + tuple(vectors),
        out_specs=(ANY, ANY),
        scalars=(index,),
        scratch=[pltpu.VMEM((2, count, rows, feat), bf16), pltpu.SemaphoreType.DMA((2,))],
        mib=22,
        flops=2 * pairs[0][0].shape[0] * feat * cols,
    )


def out_back_kernel(grad_ref, w_ref, o_ref):
    o_ref[...] = dot(grad_ref[...], w_ref[...], NT).astype(bf16)


def out_back(grad_low, first_weight):
    slots, feat = grad_low.shape
    return call(
        out_back_kernel,
        shape_of((slots, feat)),
        (grad_low, first_weight),
        in_specs=[full(grad_low.shape), out_block(feat)],
        flops=2 * slots * feat * feat,
    )


def input_back_kernel(dq_ref, dk_ref, dv_ref, w_ref, grad_ref, *row_refs):
    feat = dq_ref.shape[1]
    total = grad_ref[...]
    for at, part in enumerate((dq_ref, dk_ref, dv_ref)):
        total = total + dot(part[...], w_ref[:, at * feat : (at + 1) * feat], NT)
    put_row(total.astype(bf16), row_refs)


def input_back(parts, weight, grad, quarter):
    slots, feat = grad.shape
    return call(
        input_back_kernel,
        row_shapes(quarter, feat),
        tuple(parts) + (weight, grad),
        in_specs=[full((slots, feat))] * 3
        + [pl.BlockSpec((feat, 3 * feat), lambda i: (0, 0)), full((slots, feat))],
        mib=18,
        flops=6 * slots * feat * feat,
    )


def adam_kernel(kinds, spans, *refs):
    many = len(kinds)
    terms, states, outs = refs[: -6 * many], refs[-6 * many : -3 * many], refs[-3 * many :]
    total = total_of(*[term[0] for term in terms])
    for at, (kind, span) in enumerate(zip(kinds, spans)):
        master, first_moment, second_moment = (states[part * many + at][...] for part in range(3))
        if span is None:
            rows, cols = master.shape
            block = jnp.pad(total[:, -VEC_PAD:], ((0, VEC_PAD - cols), (0, 0)))
            gradient = jnp.transpose(block)[:rows, :cols]
        else:
            gradient = total[:, span[0] : span[1]]
        results = adam_step(
            master, first_moment, second_moment, gradient, step_rates[kind], step_decays[kind]
        )
        for part in range(3):
            outs[part * many + at][...] = results[part]


def adam(terms, kinds, spans, states):
    ordered = [state[part] for part in range(3) for state in states]
    results = call(
        functools.partial(adam_kernel, kinds, spans),
        tuple(shape_of(state.shape, f32) for state in ordered),
        tuple(terms) + tuple(ordered),
    )
    many = len(kinds)
    return [tuple(results[part * many + at] for part in range(3)) for at in range(many)]


def adam_step(master, first_moment, second_moment, gradient, step_rate, decay_rate):
    first_new = beta_one * first_moment + (1.0 - beta_one) * gradient
    second_new = beta_two * second_moment + (1.0 - beta_two) * gradient * gradient
    ratio = (
        first_new
        / (1.0 - beta_one**STEP)
        / (jnp.sqrt(second_new / (1.0 - beta_two**STEP)) + adam_eps)
    )
    return (master - step_rate * (ratio + decay_rate * master), first_new, second_new)


def on_device(
    tokens,
    cotangent,
    read_lengths,
    row_reads,
    qkv_master,
    out_master,
    up_master,
    down_master,
    vec_master,
    qkv_first,
    out_first,
    up_first,
    down_first,
    vec_first,
    qkv_second,
    out_second,
    up_second,
    down_second,
    vec_second,
):
    groups = lax.axis_size("dp")
    count = groups * lax.axis_size("seq")
    row_count, quarter, feat = tokens.shape
    slots = quarter * groups
    wide = up_master.shape[1]
    index = (lax.axis_index("seq") * groups + lax.axis_index("dp")).astype(jnp.int32).reshape(1)
    scalars = (index, row_reads, read_lengths)

    own = lambda m: lambda index: (index & (groups - 1)) ^ m

    def split_rows(held, first_index):
        many = len(held)
        moves = []
        for source in range(many):
            moves += [
                (source, own(0), None, 0, source, None),
                (source, own(1), None, 1, source, None),
                (source, own(2), None, 2, 2 * source, None),
                (source, own(3), None, 2, 2 * source + 1, None),
            ]
        shapes = tuple(shape_of((size, quarter, feat)) for size in (many, many, 2 * many))
        return place(first_index, held, shapes, moves)

    def take_rows(near, beside, across, passed):
        many = near.shape[0]
        moves = []
        for target in range(many):
            moves += [
                (0, target, None, target, 0, None),
                (1, target, None, target, 1, None),
                (2, 2 * target, None, target, 2, None),
                (3, 2 * target + 1, None, target, 3, None),
            ]
        shapes = (shape_of((groups, quarter, feat)),) * many
        out = place(index, [near, beside, across, passed], shapes, moves)
        return [row.reshape(slots, feat) for row in out]

    def give_row(near, beside, across, passed):
        moves = [(m, m // 3, None, 0, own(m), None) for m in range(4)]
        return place(index, [near, beside, across, passed], shape_of((groups, quarter, feat)), moves, light=False)

    first_block = call(
        pack_first_kernel,
        shape_of((1, qkv_master.shape[0], 4 * feat + VEC_PAD)),
        (qkv_master, out_master, vec_master),
        light=True,
    )
    masks = line_masks(count)

    def grow(line, steps, *earlier):
        for mask in steps:
            line = longer(line, after(swap(line, mask, count), *earlier))
        return line

    row_parts = split_rows([tokens], after(index, first_block))
    across = swap(row_parts[2], 2, count)
    half1 = grow(first_block, masks[:-1], row_parts)
    second_block = pack(after(up_master, half1))
    beside = swap(row_parts[1], 1, count)
    line1 = grow(half1, masks[-1:], second_block, across)
    got1 = swap(line1, 4, count), swap(line1, 2, count)
    third_block = pack(after(down_master.T, line1))
    half2 = grow(after(second_block, line1), masks[:-1])
    passed = swap(after(across, half2, got1), 1, count)
    (x,) = take_rows(row_parts[0], *after((beside, across, passed), half2))
    line2 = grow(half2, masks[-1:], x)
    halves = [half_of(line1.shape[2]), half_of(wide), wide // 512 * 384]
    got2 = pass_on(got1, line1.shape[2], halves[0], line2, count)
    other1 = [swap(piece, 1, count) for piece in (line1, *got1)]
    half3 = grow(after(third_block, line2), masks[:-1], other1)
    line3 = grow(half3, masks[-1:])
    got3 = pass_on(got2, wide, halves[1], line3, count)
    other2 = [swap(piece, 1, count) for piece in (line2, *got2)]
    first_weight = assemble(
        index, line1, got1, got2, (other1[0], other1[1:], other2[1:]), halves[0], count
    )

    projected = project(x, first_weight)
    attended, logs = attend_forward(scalars, projected, feat, quarter)
    normed, scale, low = attn_out(attended, x, first_weight)
    got3 = after(got3, low)
    cotangent_parts = split_rows([cotangent], after(index, low))
    got4 = pass_on(got3, wide, halves[2], None, count)
    across = swap(after(cotangent_parts[2], got3), 2, count)
    beside = swap(after(cotangent_parts[1], got3), 1, count)
    other3 = [swap(piece, 1, count) for piece in (line3, *got3)]
    second_weight = assemble(
        index, line2, got2, got3, (other2[0], other2[1:], other3[1:]), halves[1], count
    )
    active, slope = feed_up(after(low, other3), second_weight, first_weight)
    got4, across, beside = after((got4, across, beside), active)
    other4 = [swap(piece, 1, count) for piece in got4]
    passed = swap(across, 1, count)
    down_weight = assemble(
        index, line3, got3, got4, (other3[0], other3[1:], other4), halves[2], count
    )
    grad_output = (cotangent_parts[0], *after((beside, across, passed), down_weight))

    grad2, grad2_low, sums2, *out_parts = feed_down(
        scalars, active, down_weight, normed, grad_output, first_weight, quarter
    )
    down_parts = weight_grad(index, count, [(grad2_low, active)])
    down_sum = Scatter(*down_parts, count)
    across = swap(out_parts[2], 2, count)
    beside = swap(out_parts[1], 1, count)
    grad_hidden, bias1, grad1, grad1_low, sums1 = feed_back(
        after(grad2_low, down_parts), grad2, normed, scale, slope, second_weight, down_weight, first_weight
    )
    across, beside = after((across, beside), grad1_low)
    passed = swap(across, 1, count)
    done = down_sum.cross(grad1_low)
    up_parts = weight_grad(
        index, count, [(after(low, done), grad_hidden), (attended, grad1_low)]
    )
    up_sum = Scatter(*up_parts, count)
    done = down_sum.plane(up_parts)
    grad_attended = out_back(after(grad1_low, done, passed), first_weight)
    beside_out, across_out, passed_out = after((beside, across, passed), done)
    done = up_sum.cross(grad_attended, beside_out, across_out, passed_out)
    *parts, bias_query, bias_value = attend_backward(
        (after(index, done),) + scalars[1:], projected, attended, logs, grad_attended, quarter
    )
    done = down_sum.line(parts)
    done = up_sum.plane(done)
    first_parts = weight_grad(
        index,
        count,
        [(after(x, done), parts[0]), (x, parts[1]), (x, parts[2])],
        (bias_query, bias_value, sums1, sums2, bias1),
    )
    first_sum = Scatter(*first_parts, count)
    done = down_sum.fold(first_parts)
    done = first_sum.cross(done)
    grad_parts = input_back(after(parts, done), first_weight, grad1, quarter)
    done = up_sum.line(grad_parts)
    done = first_sum.plane(done)
    done = up_sum.fold(done)
    line = first_sum.line(done)
    beside = swap(after(grad_parts[1], line), 1, count)
    across = swap(after(grad_parts[2], line), 2, count)
    output = give_row(after(out_parts[0], line), beside_out, across_out, passed_out)
    (down_new,) = adam(
        after(down_sum.terms, output),
        (3,),
        ((0, wide),),
        [(down_master.T, down_first.T, down_second.T)],
    )
    done = first_sum.fold(down_new)
    up_new, out_new = adam(
        after(up_sum.terms, done),
        (2, 1),
        ((0, wide), (wide, wide + feat)),
        [(up_master, up_first, up_second), (out_master, out_first, out_second)],
    )
    passed = swap(after(across, up_new), 1, count)
    qkv_new, vec_new = adam(
        after(first_sum.terms, up_new),
        (0, 4),
        ((0, 3 * feat), None),
        [(qkv_master, qkv_first, qkv_second), (vec_master, vec_first, vec_second)],
    )
    input_grad = give_row(after(grad_parts[0], qkv_new), beside, across, passed)
    down_new = tuple(value.T for value in down_new)
    updates = (qkv_new, out_new, up_new, down_new, vec_new)
    return (output, input_grad) + tuple(update[part] for part in range(3) for update in updates)


def solution(mesh):
    across_rows = P(("seq", "dp"), None)
    across_columns = P(None, ("seq", "dp"))
    slots = P("seq", "dp", None)
    matrices = (across_rows, across_rows, across_rows, across_columns, across_columns)
    return jax.shard_map(
        on_device,
        mesh=mesh,
        in_specs=(slots, slots, P(), P()) + matrices * 3,
        out_specs=(slots, slots) + matrices * 3,
        check_vma=False,
    )
```
